32 devices in a mesh: dp: 8 (over y, x, core), seq: 4 (over z).
Axes of the slice: x: 2, y: 2, z: 4, core: 2. Of those that a mesh axis runs over, the one named last changes fastest.
Arguments:
- tokens: bfloat16 [16, 1024, 1536], P('dp', 'seq'), may hold values from -6 to 6
- cotangent: bfloat16 [16, 1024, 1536], P('dp', 'seq'), may hold values from -6 to 6
- in_proj: float32 [1536, 6448], P(('dp', 'seq')), may hold values from -0.15625 to 0.15625
- in_proj_mom: float32 [1536, 6448], P(('dp', 'seq')), may hold values from -6 to 6
- in_proj_var: float32 [1536, 6448], P(('dp', 'seq')), may hold values from 0.5 to 50
- out_proj: float32 [3072, 1536], P(('dp', 'seq')), may hold values from -0.109375 to 0.109375
- out_proj_mom: float32 [3072, 1536], P(('dp', 'seq')), may hold values from -6 to 6
- out_proj_var: float32 [3072, 1536], P(('dp', 'seq')), may hold values from 0.5 to 50
- conv_params: float32 [5, 3328], P(None, ('dp', 'seq')), may hold values from -0.6 to 0.6
- conv_mom: float32 [5, 3328], P(None, ('dp', 'seq')), may hold values from -6 to 6
- conv_var: float32 [5, 3328], P(None, ('dp', 'seq')), may hold values from 0.5 to 50
- norm_gain: float32 [1536], P(('dp', 'seq')), may hold values from 0.5 to 1.5
- norm_mom: float32 [1536], P(('dp', 'seq')), may hold values from -6 to 6
- norm_var: float32 [1536], P(('dp', 'seq')), may hold values from 0.5 to 50
- gate_gain: float32 [3072], P(('dp', 'seq')), may hold values from 0.5 to 1.5
- gate_mom: float32 [3072], P(('dp', 'seq')), may hold values from -6 to 6
- gate_var: float32 [3072], P(('dp', 'seq')), may hold values from 0.5 to 50
- head_params: float32 [3, 48], replicated, may hold values from -5 to 1.5, as said below
- head_mom: float32 [3, 48], replicated, may hold values from -6 to 6
- head_var: float32 [3, 48], replicated, may hold values from 0.5 to 50
Outputs:
- block_out: bfloat16 [16, 1024, 1536], P('dp', 'seq')
- tokens_grad: float32 [16, 1024, 1536], P('dp', 'seq')
- in_proj_grad: float32 [1536, 6448], P(('dp', 'seq'))
- out_proj_grad: float32 [3072, 1536], P(('dp', 'seq'))
- conv_grad: float32 [5, 3328], P(None, ('dp', 'seq'))
- norm_grad: float32 [1536], P(('dp', 'seq'))
- gate_grad: float32 [3072], P(('dp', 'seq'))
- head_grad: float32 [3, 48], replicated
- in_proj_new: float32 [1536, 6448], P(('dp', 'seq'))
- in_proj_mom_new: float32 [1536, 6448], P(('dp', 'seq'))
- in_proj_var_new: float32 [1536, 6448], P(('dp', 'seq'))
- out_proj_new: float32 [3072, 1536], P(('dp', 'seq'))
- out_proj_mom_new: float32 [3072, 1536], P(('dp', 'seq'))
- out_proj_var_new: float32 [3072, 1536], P(('dp', 'seq'))
- conv_new: float32 [5, 3328], P(None, ('dp', 'seq'))
- conv_mom_new: float32 [5, 3328], P(None, ('dp', 'seq'))
- conv_var_new: float32 [5, 3328], P(None, ('dp', 'seq'))
- norm_new: float32 [1536], P(('dp', 'seq'))
- norm_mom_new: float32 [1536], P(('dp', 'seq'))
- norm_var_new: float32 [1536], P(('dp', 'seq'))
- gate_new: float32 [3072], P(('dp', 'seq'))
- gate_mom_new: float32 [3072], P(('dp', 'seq'))
- gate_var_new: float32 [3072], P(('dp', 'seq'))
- head_new: float32 [3, 48], replicated
- head_mom_new: float32 [3, 48], replicated
- head_var_new: float32 [3, 48], replicated
The draws below stay inside these ranges and needn't reach their ends.
Inputs may be any that keep to these rules, and one draw needn't show every extreme that they name: `head_params`: row 0 holds the logarithms of decay rates, row 1 skip weights, row 2 step biases.
All inputs are finite; a program needn't handle non-finite values.
Results may differ from the reference program's by a relative error of at most 0.0044.
The reference program's roundings to bfloat16 on the way count: a program that leaves them out, or rounds other values in their place, can miss the bound.
Values may be sent and summed in bfloat16 or wider, within the bound.
A program may use at most 256 MiB of HBM per device.

```python
import math
import jax
import jax.numpy as jnp
from jax import lax

D = 1536
DI = 3072
HEADS = 48
HEAD_DIM = 64
STATE = 128
KERNEL = 4
SPAN = 256
STEP = 3
PROJ = 6448
CONV = 3328
SEQS = 16
LEN = 1024


def draw_head_params(key, part):
    subkeys = jax.random.split(key, 3)
    log_rates = jax.random.uniform(subkeys[0], (HEADS,), jnp.float32, -3.5, 1.1)
    skip_weights = jax.random.uniform(subkeys[1], (HEADS,), jnp.float32, 0.5, 1.5)
    biases = jax.random.uniform(subkeys[2], (HEADS,), jnp.float32, -5.0, -3.0)
    return jnp.stack([log_rates, skip_weights, biases])


def steps_of(own_key, extent, cuts, smallest, largest):
    factor_of = 1.0
    for axis_at, blocks in cuts:
        steps = jax.random.uniform(jax.random.fold_in(jax.random.fold_in(own_key, 6), axis_at), (blocks,), jnp.float32, smallest / len(cuts), largest / len(cuts))
        factor_of = factor_of * jnp.repeat(jnp.exp(steps), extent[axis_at] // blocks).reshape((-1,) + (1,) * (len(extent) - 1 - axis_at))
    return factor_of


def bell_draw(key, extent, scale, bound, shards=(), dtype=jnp.bfloat16):
    entries = scale * jax.random.normal(key, extent, jnp.float32)
    if shards:
        entries = entries * steps_of(key, extent, shards, -0.22, 0.18)
    return jnp.clip(entries, -bound, bound).astype(dtype)


def setup_inputs(seed: int = 0) -> dict:
    key_list = jax.random.split(jax.random.key(seed), 21)
    tokens = bell_draw(key_list[0], (SEQS, LEN, D), 1.0, 6.0, ((0, 8), (1, 4)))
    cotangent = bell_draw(key_list[1], (SEQS, LEN, D), 1.0, 6.0, ((0, 8), (1, 4)))
    in_proj = bell_draw(key_list[2], (D, PROJ), D ** -0.5, 0.15625, ((0, 32),), jnp.float32)
    in_proj_mom = bell_draw(key_list[3], (D, PROJ), 1.0, 6.0, ((0, 32),), jnp.float32)
    in_proj_var = jnp.clip(jnp.exp(math.log(50.0) - 4.6051702 * jax.random.uniform(key_list[4], (D, PROJ), jnp.float32) ** steps_of(key_list[4], (D, PROJ), ((0, 32),), -0.2, 0.2)), 0.5, 50.0)
    out_proj = bell_draw(key_list[5], (DI, D), DI ** -0.5, 0.109375, ((0, 32),), jnp.float32)
    out_proj_mom = bell_draw(key_list[6], (DI, D), 1.0, 6.0, ((0, 32),), jnp.float32)
    out_proj_var = jnp.clip(jnp.exp(math.log(50.0) - 4.6051702 * jax.random.uniform(key_list[7], (DI, D), jnp.float32) ** steps_of(key_list[7], (DI, D), ((0, 32),), -0.2, 0.2)), 0.5, 50.0)
    conv_params = jnp.clip(jax.random.uniform(key_list[8], (KERNEL + 1, CONV), jnp.float32, -0.6, 0.6) * steps_of(key_list[8], (KERNEL + 1, CONV), ((1, 32),), -0.4, 0.0), -0.6, 0.6)
    conv_mom = bell_draw(key_list[9], (KERNEL + 1, CONV), 1.0, 6.0, ((1, 32),), jnp.float32)
    conv_var = jnp.clip(jnp.exp(math.log(50.0) - 4.6051702 * jax.random.uniform(key_list[10], (KERNEL + 1, CONV), jnp.float32) ** steps_of(key_list[10], (KERNEL + 1, CONV), ((1, 32),), -0.2, 0.2)), 0.5, 50.0)
    norm_gain = jnp.clip(1.0 + 0.1 * jax.random.normal(key_list[11], (D,), jnp.float32), 0.5, 1.5)
    norm_mom = bell_draw(key_list[12], (D,), 1.0, 6.0, ((0, 32),), jnp.float32)
    norm_var = jnp.clip(jnp.exp(math.log(50.0) - 4.6051702 * jax.random.uniform(key_list[13], (D,), jnp.float32) ** steps_of(key_list[13], (D,), ((0, 32),), -0.2, 0.2)), 0.5, 50.0)
    gate_gain = jnp.clip(1.0 + 0.1 * jax.random.normal(key_list[14], (DI,), jnp.float32), 0.5, 1.5)
    gate_mom = bell_draw(key_list[15], (DI,), 1.0, 6.0, ((0, 32),), jnp.float32)
    gate_var = jnp.clip(jnp.exp(math.log(50.0) - 4.6051702 * jax.random.uniform(key_list[16], (DI,), jnp.float32) ** steps_of(key_list[16], (DI,), ((0, 32),), -0.2, 0.2)), 0.5, 50.0)
    head_params = draw_head_params(jax.random.fold_in(key_list[20], 71), 0)
    head_mom = bell_draw(key_list[18], (3, HEADS), 1.0, 6.0, (), jnp.float32)
    head_var = jnp.clip(jnp.exp(jax.random.uniform(key_list[19], (3, HEADS), jnp.float32, math.log(0.5), math.log(50.0))), 0.5, 50.0)
    return {"tokens": tokens, "cotangent": cotangent, "in_proj": in_proj, "in_proj_mom": in_proj_mom, "in_proj_var": in_proj_var, "out_proj": out_proj, "out_proj_mom": out_proj_mom, "out_proj_var": out_proj_var, "conv_params": conv_params, "conv_mom": conv_mom, "conv_var": conv_var, "norm_gain": norm_gain, "norm_mom": norm_mom, "norm_var": norm_var, "gate_gain": gate_gain, "gate_mom": gate_mom, "gate_var": gate_var, "head_params": head_params, "head_mom": head_mom, "head_var": head_var}


@jax.custom_vjp
def low(v):
    return lax.optimization_barrier(v.astype(jnp.bfloat16)).astype(jnp.float32)

@jax.custom_vjp
def low_back(v):
    return v

def low_keep(v):
    return (low(v), None)

def low_pass(kept, grad):
    return (grad,)

def back_keep(v):
    return (v, None)

def back_low(kept, grad):
    return (low(grad),)
low.defvjp(low_keep, low_pass)
low_back.defvjp(back_keep, back_low)
highest = lax.Precision.HIGHEST
norm_eps = 1e-05
beta_one = 0.9
beta_two = 0.95
learn_rate = 0.01
decay_rate = 0.1
adam_eps = 1e-08

def rms_scale(values, gain):
    return values * lax.rsqrt(lax.optimization_barrier(jnp.mean(values * values, axis=-1, keepdims=True)) + norm_eps) * gain

def span_step(state, pieces):
    head_x, b_proj, c_proj, step_size, decay_sum = pieces
    length = decay_sum.shape[1]
    scores = jnp.einsum('gtn,gsn->gts', c_proj, b_proj, precision=highest)
    row_ids = lax.broadcasted_iota(jnp.int32, (length, length), 0)
    col_ids = lax.broadcasted_iota(jnp.int32, (length, length), 1)
    causal = (col_ids <= row_ids)[None, :, :, None]
    gap_sums = decay_sum[:, :, None, :] - decay_sum[:, None, :, :]
    decay_mat = jnp.exp(jnp.where(causal, gap_sums, -1e+30))
    weights = scores[:, :, :, None] * decay_mat * step_size[:, None, :, :]
    inner_out = jnp.einsum('gtsh,gshp->gthp', weights, head_x, precision=highest)
    carried = jnp.exp(decay_sum)[..., None] * jnp.einsum('gtn,ghpn->gthp', c_proj, state, precision=highest)
    last_sum = decay_sum[:, -1, :]
    tail_weight = jnp.exp(last_sum[:, None, :] - decay_sum) * step_size
    local_state = jnp.einsum('gsh,gshp,gsn->ghpn', tail_weight, head_x, b_proj, precision=highest)
    new_state = jnp.exp(last_sum)[:, :, None, None] * state + local_state
    return (new_state, inner_out + carried)

def forward(tokens_in, in_weight, out_weight, conv_weight, norm_weight, gate_weight, head_weight):
    seq_count = tokens_in.shape[0]
    normed_in = rms_scale(tokens_in, norm_weight)
    projected = low_back(jnp.einsum('gtd,dp->gtp', low(normed_in), low(in_weight), precision=highest))
    gate_z = projected[:, :, :DI]
    conv_in = projected[:, :, DI:DI + CONV]
    step_raw = projected[:, :, DI + CONV:]
    padded = jnp.pad(conv_in, ((0, 0), (KERNEL - 1, 0), (0, 0)))
    conv_out = conv_weight[KERNEL]
    for tap_index in range(KERNEL):
        conv_out = conv_out + conv_weight[tap_index] * padded[:, tap_index:tap_index + LEN, :]
    activated = jax.nn.silu(conv_out)
    head_x = activated[:, :, :DI].reshape(seq_count, LEN, HEADS, HEAD_DIM)
    b_proj = activated[:, :, DI:DI + STATE]
    c_proj = activated[:, :, DI + STATE:]
    step_size = jax.nn.softplus(step_raw + head_weight[2])
    rate = step_size * -jnp.exp(head_weight[0])
    blocks = LEN // SPAN

    def to_blocks(values):
        return jnp.moveaxis(values.reshape((seq_count, blocks, SPAN) + values.shape[2:]), 1, 0)
    decay_sum = jnp.cumsum(to_blocks(rate), axis=2)
    start = jnp.zeros((seq_count, HEADS, HEAD_DIM, STATE), jnp.float32)
    ending, outputs = lax.scan(jax.checkpoint(span_step), start, (to_blocks(head_x), to_blocks(b_proj), to_blocks(c_proj), to_blocks(step_size), decay_sum))
    mixed_y = jnp.moveaxis(outputs, 0, 1).reshape(seq_count, LEN, HEADS, HEAD_DIM) + head_weight[1][:, None] * head_x
    gated = mixed_y.reshape(seq_count, LEN, DI) * jax.nn.silu(gate_z)
    out_normed = rms_scale(gated, gate_weight)
    branch = low_back(jnp.einsum('gti,id->gtd', low(out_normed), low(out_weight), precision=highest))
    return tokens_in + branch

def adamw(weight, moment_one, moment_two, gradient, decay_on):
    one_new = beta_one * moment_one + (1.0 - beta_one) * gradient
    two_new = beta_two * moment_two + (1.0 - beta_two) * gradient * gradient
    mean_hat = one_new / (1.0 - beta_one ** STEP)
    var_hat = two_new / (1.0 - beta_two ** STEP)
    weight_new = weight - learn_rate * (mean_hat / (jnp.sqrt(var_hat) + adam_eps) + decay_on * weight)
    return (weight_new, one_new, two_new)

def reference(tokens, cotangent, in_proj, in_proj_mom, in_proj_var, out_proj, out_proj_mom, out_proj_var, conv_params, conv_mom, conv_var, norm_gain, norm_mom, norm_var, gate_gain, gate_mom, gate_var, head_params, head_mom, head_var):
    group_size = math.gcd(SEQS, max(1, 4096 // LEN))
    groups = SEQS // group_size
    inputs = tokens.astype(jnp.float32).reshape(groups, group_size, LEN, D)
    cot_in = cotangent.astype(jnp.float32).reshape(groups, group_size, LEN, D)

    def group_step(totals, pair_in):
        tokens_in, cot_group = pair_in
        result, pullback = jax.vjp(forward, tokens_in, in_proj, out_proj, conv_params, norm_gain, gate_gain, head_params)
        gradients = pullback(cot_group)
        summed = (totals[0] + gradients[1], totals[1] + gradients[2], totals[2] + gradients[3], totals[3] + gradients[4], totals[4] + gradients[5], totals[5] + gradients[6])
        return (summed, (result.astype(jnp.bfloat16), gradients[0]))
    start = (jnp.zeros_like(in_proj), jnp.zeros_like(out_proj), jnp.zeros_like(conv_params), jnp.zeros_like(norm_gain), jnp.zeros_like(gate_gain), jnp.zeros_like(head_params))
    totals, (outputs, input_grads) = lax.scan(group_step, start, (inputs, cot_in))
    block_out = outputs.reshape(SEQS, LEN, D)
    tokens_grad = input_grads.reshape(SEQS, LEN, D)
    in_grad, out_grad, conv_grad, norm_grad, gate_grad, head_grad = totals
    in_new, in_mom_new, in_var_new = adamw(in_proj, in_proj_mom, in_proj_var, in_grad, decay_rate)
    out_new, out_mom_new, out_var_new = adamw(out_proj, out_proj_mom, out_proj_var, out_grad, decay_rate)
    conv_new, conv_mom_new, conv_var_new = adamw(conv_params, conv_mom, conv_var, conv_grad, decay_rate)
    norm_new, norm_mom_new, norm_var_new = adamw(norm_gain, norm_mom, norm_var, norm_grad, 0.0)
    gate_new, gate_mom_new, gate_var_new = adamw(gate_gain, gate_mom, gate_var, gate_grad, 0.0)
    head_new, head_mom_new, head_var_new = adamw(head_params, head_mom, head_var, head_grad, 0.0)
    return (block_out, tokens_grad, in_grad, out_grad, conv_grad, norm_grad, gate_grad, head_grad, in_new, in_mom_new, in_var_new, out_new, out_mom_new, out_var_new, conv_new, conv_mom_new, conv_var_new, norm_new, norm_mom_new, norm_var_new, gate_new, gate_mom_new, gate_var_new, head_new, head_mom_new, head_var_new)
```

```python
import functools

import jax
import jax.numpy as jnp
from jax import lax
from jax.experimental import pallas as pl
from jax.experimental.pallas import tpu as pltpu
from jax.sharding import PartitionSpec as P

MESH = pl.DeviceIdType.MESH

DI = 3072
HEADS = 48
HEAD_DIM = 64
STATE = 128
KERNEL = 4
STEP = 3
CONV = 3328


highest = lax.Precision.HIGHEST
norm_eps = 1e-05
beta_one = 0.9
beta_two = 0.95
learn_rate = 0.01
decay_rate = 0.1
adam_eps = 1e-08


def from_behind(array, axis, by):
    size = lax.axis_size(axis)
    pairs = [(i, i + by) for i in range(size) if 0 <= i + by < size]
    return lax.ppermute(array, axis, pairs)


def entering(part, axis, combine, identity):
    place = lax.axis_index(axis)
    gathered = jax.tree.map(lambda a: lax.all_gather(a, axis), part)
    state = jax.tree.map(lambda a, e: jnp.zeros_like(a) + jnp.asarray(e, a.dtype), part, identity)

    def one(lap, state):
        return combine(
            state, jax.tree.map(lambda a: lax.dynamic_index_in_dim(a, lap, 0, False), gathered)
        )

    return lax.fori_loop(0, place, one, state)


def prefix(array, axis, combine, identity):
    size, here = (lax.axis_size(axis), lax.axis_index(axis))
    everything = jax.tree.map(
        lambda part, kind: lax.all_gather(part.astype(kind), axis),
        array,
        jax.tree.map(lambda a: jnp.bfloat16 if a.dtype == jnp.float32 else a.dtype, array),
    )
    start = jax.tree.map(
        lambda part, zero: jnp.broadcast_to(jnp.asarray(zero, part.dtype), part.shape),
        array,
        identity,
    )

    def lap(k, before):
        at = size - 1 - k
        reached = at > here
        new = combine(
            before, jax.tree.map(lambda part, own: part[at].astype(own.dtype), everything, array)
        )
        return jax.tree.map(lambda a, b: jnp.where(reached, a, b), new, before)

    return lax.fori_loop(0, size, lap, start)


def rms_scale(values, gain):
    return values * lax.rsqrt(jnp.mean(values * values, axis=-1, keepdims=True) + norm_eps) * gain


def adamw(weight, moment_one, moment_two, gradient, decay_on):
    one_new = beta_one * moment_one + (1.0 - beta_one) * gradient
    two_new = beta_two * moment_two + (1.0 - beta_two) * gradient * gradient
    mean_hat = one_new / (1.0 - beta_one**STEP)
    var_hat = two_new / (1.0 - beta_two**STEP)
    weight_new = weight - learn_rate * (
        mean_hat / (jnp.sqrt(var_hat) + adam_eps) + decay_on * weight
    )
    return (weight_new, one_new, two_new)


def fold_pair(earlier, later):
    decay_early, state_early = earlier
    decay_later, state_later = later
    return (decay_early * decay_later, decay_later[:, :, None, None] * state_early + state_later)


def intra_item(pieces):
    head_x, b_proj, c_proj, step_size, decay_sum = pieces
    length = decay_sum.shape[0]
    scores = jnp.dot(c_proj, b_proj.T, precision=highest)
    row_ids = lax.broadcasted_iota(jnp.int32, (length, length), 0)
    col_ids = lax.broadcasted_iota(jnp.int32, (length, length), 1)
    causal = (col_ids <= row_ids)[None, :, :]
    sums_by_head = decay_sum.T
    gap_sums = sums_by_head[:, :, None] - sums_by_head[:, None, :]
    decay_mat = jnp.exp(jnp.where(causal, gap_sums, -1e30))
    weights = scores[None, :, :] * decay_mat * step_size.T[:, None, :]
    return jnp.einsum("hts,shp->thp", weights, head_x, precision=highest)


def front(conv_in, previous, conv_weight, step_raw, head_weight):
    seq_count = conv_in.shape[0]
    length = conv_in.shape[1]
    padded = jnp.concatenate([previous, conv_in], axis=1)
    conv_out = conv_weight[KERNEL]
    for tap_index in range(KERNEL):
        conv_out = conv_out + conv_weight[tap_index] * padded[:, tap_index : tap_index + length, :]
    activated = jax.nn.silu(conv_out)
    head_x = activated[:, :, :DI].reshape(seq_count, length, HEADS, HEAD_DIM)
    b_proj = activated[:, :, DI : DI + STATE]
    c_proj = activated[:, :, DI + STATE :]
    step_size = jax.nn.softplus(step_raw + head_weight[2])
    decay_sum = jnp.cumsum(step_size * -jnp.exp(head_weight[0]), axis=1)
    last_sum = decay_sum[:, -1, :]
    tail_weight = jnp.exp(last_sum[:, None, :] - decay_sum) * step_size
    local_state = jnp.einsum("gsh,gshp,gsn->ghpn", tail_weight, head_x, b_proj, precision=highest)
    return (local_state, jnp.exp(last_sum), head_x, b_proj, c_proj, step_size, decay_sum)


def back(head_x, b_proj, c_proj, step_size, decay_sum, head_weight, gate_z, gate_weight, state_in):
    seq_count = gate_z.shape[0]
    length = gate_z.shape[1]
    inner_out = lax.map(jax.checkpoint(intra_item), (head_x, b_proj, c_proj, step_size, decay_sum))
    carried = jnp.exp(decay_sum)[..., None] * jnp.einsum(
        "gtn,ghpn->gthp", c_proj, state_in, precision=highest
    )
    mixed_y = inner_out + carried + head_weight[1][:, None] * head_x
    gated = mixed_y.reshape(seq_count, length, DI) * jax.nn.silu(gate_z)
    return rms_scale(gated, gate_weight)


TM, TN = 1536, 256
HT = TN // 2

def rs_call(lhs, rhs, lhs_of, rhs_of, n, skew, collective_id):
    SK = skew
    NS = SK + 1
    def kernel(lhs_ref, rhs_ref, out_ref, own0, own1, own2, own3, s0, s1, s2, s3, r0, r1, r2, r3,
               ss0, ss1, ss2, ss3, rr0, rr1, rr2, rr3):
        dp = lax.axis_index("dp"); z = lax.axis_index("seq")
        c = lax.rem(dp, 2); x = lax.rem(dp // 2, 2); y = dp // 4
        core_peer = {"dp": dp + 1 - 2 * c}
        x_peer = {"dp": dp + 2 - 4 * x}
        y_peer = {"dp": dp + 4 - 8 * y}
        def zp(k): return {"seq": lax.rem(z + k, 4)}
        bar = pltpu.get_barrier_semaphore()
        for d in (core_peer, x_peer, y_peer, zp(1), zp(2), zp(3)):
            pl.semaphore_signal(bar, inc=1, device_id=d, device_id_type=MESH)
        pl.semaphore_wait(bar, 6)

        def c0(i, sl): return pltpu.make_async_remote_copy(src_ref=s0.at[sl], dst_ref=r0.at[i], send_sem=ss0.at[sl], recv_sem=rr0.at[i], device_id=core_peer, device_id_type=MESH)
        def c1(i, sl, h): return pltpu.make_async_remote_copy(src_ref=s1.at[sl, h], dst_ref=r1.at[i, h], send_sem=ss1.at[sl, h], recv_sem=rr1.at[i, h], device_id=(x_peer, y_peer)[h], device_id_type=MESH)
        def c2(i, sl, h): return pltpu.make_async_remote_copy(src_ref=s2.at[sl, h], dst_ref=r2.at[i, h], send_sem=ss2.at[sl, h], recv_sem=rr2.at[i, h], device_id=(y_peer, x_peer)[h], device_id_type=MESH)
        def c3(i, sl, k): return pltpu.make_async_remote_copy(src_ref=s3.at[sl, k - 1], dst_ref=r3.at[i, k - 1], send_sem=ss3.at[sl, k - 1], recv_sem=rr3.at[i, k - 1], device_id=zp(k), device_id_type=MESH)
        bf = jnp.bfloat16; f32 = jnp.float32

        def step(it, _):
            @pl.when(it < n)
            def _():
                i = it; sl = lax.rem(i, NS)
                @pl.when(i >= NS)
                def _(): c0(i, sl).wait_send()
                li, ri = lhs_of(i), rhs_of(i)
                part = jnp.dot(lhs_ref[li, 1 - c], rhs_ref[ri], preferred_element_type=f32).astype(bf).reshape(2, 2, 192, TN)
                for h in range(2):
                    s0[sl, h] = part[..., h * HT:(h + 1) * HT]
                c0(i, sl).start()
                part = jnp.dot(lhs_ref[li, c], rhs_ref[ri], preferred_element_type=f32).reshape(2, 2, 192, TN)
                for h in range(2):
                    own0[sl, h] = part[..., h * HT:(h + 1) * HT]
            @pl.when((it >= SK) & (it < n + SK))
            def _():
                i = it - SK; sl = lax.rem(i, NS)
                @pl.when(i >= NS)
                def _():
                    for h in range(2): c1(i, sl, h).wait_send()
                c0(i, sl).wait_recv()
                s1[sl, 0] = (own0[sl, 0, 1 - x] + r0[i, 0, 1 - x].astype(f32)).astype(bf)
                c1(i, sl, 0).start()
                for a in range(2):
                    s1[sl, 1, a] = (own0[sl, 1, a, 1 - y] + r0[i, 1, a, 1 - y].astype(f32)).astype(bf)
                c1(i, sl, 1).start()
                own1[sl, 0] = own0[sl, 0, x] + r0[i, 0, x].astype(f32)
                for a in range(2):
                    own1[sl, 1, a] = own0[sl, 1, a, y] + r0[i, 1, a, y].astype(f32)
            @pl.when((it >= 2 * SK) & (it < n + 2 * SK))
            def _():
                i = it - 2 * SK; sl = lax.rem(i, NS)
                @pl.when(i >= NS)
                def _():
                    for h in range(2): c2(i, sl, h).wait_send()
                for h, g in ((0, y), (1, x)):
                    c1(i, sl, h).wait_recv()
                    s2[sl, h] = (own1[sl, h, 1 - g] + r1[i, h, 1 - g].astype(f32)).astype(bf)
                    c2(i, sl, h).start()
                    own2[sl, h] = own1[sl, h, g] + r1[i, h, g].astype(f32)
            @pl.when((it >= 3 * SK) & (it < n + 3 * SK))
            def _():
                i = it - 3 * SK; sl = lax.rem(i, NS)
                @pl.when(i >= NS)
                def _():
                    for k in range(1, 4): c3(i, sl, k).wait_send()
                for h in range(2): c2(i, sl, h).wait_recv()
                for k in (2, 1, 3):
                    zz = lax.rem(z + k, 4) * 48
                    for h in range(2):
                        rows = pl.ds(pl.multiple_of(zz, 16), 48)
                        s3[sl, k - 1, h] = (own2[sl, h, rows] + r2[i, h, rows].astype(f32)).astype(bf)
                    c3(i, sl, k).start()
                rows = pl.ds(pl.multiple_of(z * 48, 16), 48)
                for h in range(2):
                    own3[sl, h] = own2[sl, h, rows] + r2[i, h, rows].astype(f32)
            @pl.when(it >= 4 * SK)
            def _():
                i = it - 4 * SK; sl = lax.rem(i, NS)
                for k in range(1, 4): c3(i, sl, k).wait_recv()
                acc = own3[sl]
                for k in range(3): acc = acc + r3[i, k].astype(f32)
                out_ref[i] = acc
            return 0
        lax.fori_loop(0, n + 4 * SK, step, 0)
        for j in range(NS):
            i = n - NS + j; sl = i % NS
            c0(i, sl).wait_send()
            for h in range(2): c1(i, sl, h).wait_send(); c2(i, sl, h).wait_send()
            for k in range(1, 4): c3(i, sl, k).wait_send()
    bf = jnp.bfloat16; f32 = jnp.float32
    V = pltpu.VMEM; D = pltpu.SemaphoreType.DMA
    return pl.pallas_call(
        kernel, out_shape=jax.ShapeDtypeStruct((n, 2, 48, HT), f32),
        in_specs=[pl.BlockSpec(memory_space=pltpu.VMEM)] * 2, out_specs=pl.BlockSpec(memory_space=pltpu.VMEM),
        scratch_shapes=[V((NS, 2, 2, 2, 192, HT), f32), V((NS, 2, 2, 192, HT), f32), V((NS, 2, 192, HT), f32), V((NS, 2, 48, HT), f32),
            V((NS, 2, 2, 2, 192, HT), bf), V((NS, 2, 2, 192, HT), bf), V((NS, 2, 192, HT), bf), V((NS, 3, 2, 48, HT), bf),
            V((n, 2, 2, 2, 192, HT), bf), V((n, 2, 2, 192, HT), bf), V((n, 2, 192, HT), bf), V((n, 3, 2, 48, HT), bf),
            D((NS,)), D((NS, 2)), D((NS, 2)), D((NS, 3)), D((n,)), D((n, 2)), D((n, 2)), D((n, 3))],
        compiler_params=pltpu.CompilerParams(collective_id=collective_id, has_side_effects=True, vmem_limit_bytes=63 << 20),
        name="rs",
    )(lhs, rhs)


def by_owner(rows):
    per = rows.shape[0] // 32
    subs = per // 48
    rows = rows.reshape(2, 2, 2, 4, subs, 48, rows.shape[1])
    return rows.transpose(4, 2, 1, 0, 3, 5, 6).reshape(subs, 2, 768, rows.shape[-1])


def in_columns(columns):
    tokens, width = columns.shape
    return columns.reshape(tokens, width // TN, TN).transpose(1, 0, 2)


def reduce_out(out_lowered, cotangent):
    sums = rs_call(
        by_owner(out_lowered.T), in_columns(cotangent), lambda i: lax.rem(i, 2), lambda i: i // 2, 12, 2, 1
    )
    sums = sums.reshape(6, 2, 2, 48, HT).transpose(1, 3, 0, 2, 4)
    return sums.reshape(96, 6 * TN)


def reduce_in(lowered, d_projected):
    width = d_projected.shape[1]
    tasks = -(-width // TN)
    padded = jnp.pad(d_projected, ((0, 0), (0, tasks * TN - width)))
    sums = rs_call(by_owner(lowered.T), in_columns(padded), lambda i: 0, lambda i: i, tasks, 2, 2)
    return sums.transpose(2, 0, 1, 3).reshape(48, tasks * TN)[:, :width]


def body(
    own_reduce,
    tokens,
    cotangent,
    in_proj,
    in_proj_mom,
    in_proj_var,
    out_proj,
    out_proj_mom,
    out_proj_var,
    conv_params,
    conv_mom,
    conv_var,
    norm_gain,
    norm_mom,
    norm_var,
    gate_gain,
    gate_mom,
    gate_var,
    head_params,
    head_mom,
    head_var,
):
    in_full, out_full = (
        lax.all_gather(in_proj.astype(jnp.bfloat16), ("dp", "seq"), axis=0, tiled=True),
        lax.all_gather(out_proj.astype(jnp.bfloat16), ("dp", "seq"), axis=0, tiled=True),
    )
    taps = conv_params.shape[1]
    small = lax.all_gather(
        jnp.concatenate([conv_params.reshape(-1), norm_gain, gate_gain]), ("dp", "seq"), axis=0
    )
    conv_full = small[:, : 5 * taps].reshape(-1, 5, taps).transpose(1, 0, 2).reshape(5, -1)
    norm_full = small[:, 5 * taps : 5 * taps + norm_gain.shape[0]].reshape(-1)
    gate_full = small[:, 5 * taps + norm_gain.shape[0] :].reshape(-1)
    length = tokens.shape[1]
    rim_start = length - (KERNEL - 1)
    inputs = tokens.astype(jnp.float32)
    normed_in, norm_pull = jax.vjp(rms_scale, inputs, norm_full)
    lowered = normed_in.astype(jnp.bfloat16)
    projected = jnp.einsum("gtd,dp->gtp", lowered, in_full, preferred_element_type=jnp.float32)
    gate_z = projected[:, :, :DI]
    conv_in = projected[:, :, DI : DI + CONV]
    step_raw = projected[:, :, DI + CONV :]
    previous = from_behind(conv_in[:, rim_start:, :], "seq", 1)
    front_out, front_pull = jax.vjp(front, conv_in, previous, conv_full, step_raw, head_params)
    local_state, decays, head_x, b_proj, c_proj, step_size, decay_sum = front_out
    unit_decay = jnp.ones_like(decays)
    zero_state = jnp.zeros_like(local_state)
    reached, state_in = entering((decays, local_state), "seq", fold_pair, (unit_decay, zero_state))
    out_normed, back_pull = jax.vjp(
        back, head_x, b_proj, c_proj, step_size, decay_sum, head_params, gate_z, gate_full, state_in
    )
    out_lowered = out_normed.astype(jnp.bfloat16)
    branch = jnp.einsum("gti,id->gtd", out_lowered, out_full, preferred_element_type=jnp.float32)
    block_out = (inputs + branch).astype(jnp.bfloat16)
    flat = tokens.shape[0] * length
    if own_reduce:
        out_grad = reduce_out(out_lowered.reshape(flat, -1), cotangent.reshape(flat, -1))
    else:
        out_grad_local = jnp.einsum(
            "gti,gtd->id", out_lowered, cotangent, preferred_element_type=jnp.float32
        )
        out_grad = lax.psum_scatter(
            out_grad_local, ("dp", "seq"), scatter_dimension=0, tiled=True
        )
    d_normed = jnp.einsum("gtd,id->gti", cotangent, out_full, preferred_element_type=jnp.float32)
    (
        d_head_x,
        d_b_proj,
        d_c_proj,
        d_step,
        d_decay_sum,
        d_head_back,
        d_gate_z,
        d_gate_gain,
        d_state_in,
    ) = back_pull(d_normed)
    later_decay, d_state_out = prefix(
        (decays, d_state_in), "seq", fold_pair, (unit_decay, zero_state)
    )
    d_decays = jnp.sum(d_state_out * state_in, axis=(2, 3))
    d_conv_in, d_previous, d_conv, d_step_raw, d_head_front = front_pull(
        (d_state_out, d_decays, d_head_x, d_b_proj, d_c_proj, d_step, d_decay_sum)
    )
    returned = from_behind(d_previous.astype(jnp.bfloat16), "seq", -1).astype(d_previous.dtype)
    d_conv_in = jnp.concatenate(
        [d_conv_in[:, :rim_start, :], d_conv_in[:, rim_start:, :] + returned], axis=1
    )
    d_projected = jnp.concatenate([d_gate_z, d_conv_in, d_step_raw], axis=-1).astype(jnp.bfloat16)
    if own_reduce:
        in_grad = reduce_in(lowered.reshape(flat, -1), d_projected.reshape(flat, -1))
    else:
        in_grad_local = jnp.einsum(
            "gtd,gtp->dp", lowered, d_projected, preferred_element_type=jnp.float32
        )
        in_grad = lax.psum_scatter(in_grad_local, ("dp", "seq"), scatter_dimension=0, tiled=True)
    d_normed_in = jnp.einsum(
        "gtp,dp->gtd", d_projected, in_full, preferred_element_type=jnp.float32
    )
    d_inputs, norm_grad_local = norm_pull(d_normed_in)
    tokens_grad = cotangent.astype(jnp.float32) + d_inputs
    head_grad = lax.psum(d_head_back + d_head_front, ("dp", "seq"))
    conv_grad, norm_grad, gate_grad = (
        lax.psum_scatter(d_conv, ("dp", "seq"), scatter_dimension=1, tiled=True),
        lax.psum_scatter(norm_grad_local, ("dp", "seq"), scatter_dimension=0, tiled=True),
        lax.psum_scatter(d_gate_gain, ("dp", "seq"), scatter_dimension=0, tiled=True),
    )
    in_new, in_mom_new, in_var_new = adamw(in_proj, in_proj_mom, in_proj_var, in_grad, decay_rate)
    out_new, out_mom_new, out_var_new = adamw(
        out_proj, out_proj_mom, out_proj_var, out_grad, decay_rate
    )
    conv_new, conv_mom_new, conv_var_new = adamw(
        conv_params, conv_mom, conv_var, conv_grad, decay_rate
    )
    norm_new, norm_mom_new, norm_var_new = adamw(norm_gain, norm_mom, norm_var, norm_grad, 0.0)
    gate_new, gate_mom_new, gate_var_new = adamw(gate_gain, gate_mom, gate_var, gate_grad, 0.0)
    head_new, head_mom_new, head_var_new = adamw(head_params, head_mom, head_var, head_grad, 0.0)
    return (
        block_out,
        tokens_grad,
        in_grad,
        out_grad,
        conv_grad,
        norm_grad,
        gate_grad,
        head_grad,
        in_new,
        in_mom_new,
        in_var_new,
        out_new,
        out_mom_new,
        out_var_new,
        conv_new,
        conv_mom_new,
        conv_var_new,
        norm_new,
        norm_mom_new,
        norm_var_new,
        gate_new,
        gate_mom_new,
        gate_var_new,
        head_new,
        head_mom_new,
        head_var_new,
    )


def solution(mesh):
    in_specs = (
        P("dp", "seq", None),
        P("dp", "seq", None),
        P(("dp", "seq"), None),
        P(("dp", "seq"), None),
        P(("dp", "seq"), None),
        P(("dp", "seq"), None),
        P(("dp", "seq"), None),
        P(("dp", "seq"), None),
        P(None, ("dp", "seq")),
        P(None, ("dp", "seq")),
        P(None, ("dp", "seq")),
        P(("dp", "seq")),
        P(("dp", "seq")),
        P(("dp", "seq")),
        P(("dp", "seq")),
        P(("dp", "seq")),
        P(("dp", "seq")),
        P(),
        P(),
        P(),
    )
    out_specs = (
        P("dp", "seq", None),
        P("dp", "seq", None),
        P(("dp", "seq"), None),
        P(("dp", "seq"), None),
        P(None, ("dp", "seq")),
        P(("dp", "seq")),
        P(("dp", "seq")),
        P(),
        P(("dp", "seq"), None),
        P(("dp", "seq"), None),
        P(("dp", "seq"), None),
        P(("dp", "seq"), None),
        P(("dp", "seq"), None),
        P(("dp", "seq"), None),
        P(None, ("dp", "seq")),
        P(None, ("dp", "seq")),
        P(None, ("dp", "seq")),
        P(("dp", "seq")),
        P(("dp", "seq")),
        P(("dp", "seq")),
        P(("dp", "seq")),
        P(("dp", "seq")),
        P(("dp", "seq")),
        P(),
        P(),
        P(),
    )
    own_reduce = tuple(mesh.shape[a] for a in ("dp", "seq")) == (8, 4)
    step = functools.partial(body, own_reduce)
    return jax.shard_map(step, mesh=mesh, in_specs=in_specs, out_specs=out_specs, check_vma=False)
```

```python
import functools

import jax
import jax.numpy as jnp
from jax import lax
from jax.experimental import pallas as pl
from jax.experimental.pallas import tpu as pltpu
from jax.sharding import PartitionSpec as P

MESH = pl.DeviceIdType.MESH
bf = jnp.bfloat16
f32 = jnp.float32

DI = 3072
HEADS = 48
HEAD_DIM = 64
STATE = 128
KERNEL = 4
STEP = 3
CONV = 3328


highest = lax.Precision.HIGHEST
norm_eps = 1e-05
beta_one = 0.9
beta_two = 0.95
learn_rate = 0.01
decay_rate = 0.1
adam_eps = 1e-08


def from_behind(array, axis, by):
    size = lax.axis_size(axis)
    pairs = [(i, i + by) for i in range(size) if 0 <= i + by < size]
    return lax.ppermute(array, axis, pairs)


def entering(part, axis, combine, identity):
    place = lax.axis_index(axis)
    gathered = jax.tree.map(lambda a: lax.all_gather(a, axis), part)
    state = jax.tree.map(lambda a, e: jnp.zeros_like(a) + jnp.asarray(e, a.dtype), part, identity)

    def one(lap, state):
        return combine(
            state, jax.tree.map(lambda a: lax.dynamic_index_in_dim(a, lap, 0, False), gathered)
        )

    return lax.fori_loop(0, place, one, state)


def prefix(array, axis, combine, identity):
    size, here = (lax.axis_size(axis), lax.axis_index(axis))
    everything = jax.tree.map(
        lambda part, kind: lax.all_gather(part.astype(kind), axis),
        array,
        jax.tree.map(lambda a: jnp.bfloat16 if a.dtype == jnp.float32 else a.dtype, array),
    )
    start = jax.tree.map(
        lambda part, zero: jnp.broadcast_to(jnp.asarray(zero, part.dtype), part.shape),
        array,
        identity,
    )

    def lap(k, before):
        at = size - 1 - k
        reached = at > here
        new = combine(
            before, jax.tree.map(lambda part, own: part[at].astype(own.dtype), everything, array)
        )
        return jax.tree.map(lambda a, b: jnp.where(reached, a, b), new, before)

    return lax.fori_loop(0, size, lap, start)


def rms_scale(values, gain):
    return values * lax.rsqrt(jnp.mean(values * values, axis=-1, keepdims=True) + norm_eps) * gain


def adamw(weight, moment_one, moment_two, gradient, decay_on):
    one_new = beta_one * moment_one + (1.0 - beta_one) * gradient
    two_new = beta_two * moment_two + (1.0 - beta_two) * gradient * gradient
    mean_hat = one_new / (1.0 - beta_one**STEP)
    var_hat = two_new / (1.0 - beta_two**STEP)
    weight_new = weight - learn_rate * (
        mean_hat / (jnp.sqrt(var_hat) + adam_eps) + decay_on * weight
    )
    return (weight_new, one_new, two_new)


def fold_pair(earlier, later):
    decay_early, state_early = earlier
    decay_later, state_later = later
    return (decay_early * decay_later, decay_later[:, :, None, None] * state_early + state_later)


def intra_item(pieces):
    head_x, b_proj, c_proj, step_size, decay_sum = pieces
    length = decay_sum.shape[0]
    scores = jnp.dot(c_proj, b_proj.T, precision=highest)
    row_ids = lax.broadcasted_iota(jnp.int32, (length, length), 0)
    col_ids = lax.broadcasted_iota(jnp.int32, (length, length), 1)
    causal = (col_ids <= row_ids)[None, :, :]
    sums_by_head = decay_sum.T
    gap_sums = sums_by_head[:, :, None] - sums_by_head[:, None, :]
    decay_mat = jnp.exp(jnp.where(causal, gap_sums, -1e30))
    weights = scores[None, :, :] * decay_mat * step_size.T[:, None, :]
    return jnp.einsum("hts,shp->thp", weights, head_x, precision=highest)


def front(conv_in, previous, conv_weight, step_raw, head_weight):
    seq_count = conv_in.shape[0]
    length = conv_in.shape[1]
    padded = jnp.concatenate([previous, conv_in], axis=1)
    conv_out = conv_weight[KERNEL]
    for tap_index in range(KERNEL):
        conv_out = conv_out + conv_weight[tap_index] * padded[:, tap_index : tap_index + length, :]
    activated = jax.nn.silu(conv_out)
    head_x = activated[:, :, :DI].reshape(seq_count, length, HEADS, HEAD_DIM)
    b_proj = activated[:, :, DI : DI + STATE]
    c_proj = activated[:, :, DI + STATE :]
    step_size = jax.nn.softplus(step_raw + head_weight[2])
    decay_sum = jnp.cumsum(step_size * -jnp.exp(head_weight[0]), axis=1)
    last_sum = decay_sum[:, -1, :]
    tail_weight = jnp.exp(last_sum[:, None, :] - decay_sum) * step_size
    local_state = jnp.einsum("gsh,gshp,gsn->ghpn", tail_weight, head_x, b_proj, precision=highest)
    return (local_state, jnp.exp(last_sum), head_x, b_proj, c_proj, step_size, decay_sum)


def back(head_x, b_proj, c_proj, step_size, decay_sum, head_weight, gate_z, gate_weight, state_in):
    seq_count = gate_z.shape[0]
    length = gate_z.shape[1]
    inner_out = lax.map(jax.checkpoint(intra_item), (head_x, b_proj, c_proj, step_size, decay_sum))
    carried = jnp.exp(decay_sum)[..., None] * jnp.einsum(
        "gtn,ghpn->gthp", c_proj, state_in, precision=highest
    )
    mixed_y = inner_out + carried + head_weight[1][:, None] * head_x
    gated = mixed_y.reshape(seq_count, length, DI) * jax.nn.silu(gate_z)
    return rms_scale(gated, gate_weight)


def body(
    tokens,
    cotangent,
    in_proj,
    in_proj_mom,
    in_proj_var,
    out_proj,
    out_proj_mom,
    out_proj_var,
    conv_params,
    conv_mom,
    conv_var,
    norm_gain,
    norm_mom,
    norm_var,
    gate_gain,
    gate_mom,
    gate_var,
    head_params,
    head_mom,
    head_var,
):
    in_full, out_full = (
        lax.all_gather(in_proj.astype(jnp.bfloat16), ("dp", "seq"), axis=0, tiled=True),
        lax.all_gather(out_proj.astype(jnp.bfloat16), ("dp", "seq"), axis=0, tiled=True),
    )
    conv_full, norm_full, gate_full = (
        lax.all_gather(conv_params, ("dp", "seq"), axis=1, tiled=True),
        lax.all_gather(norm_gain, ("dp", "seq"), axis=0, tiled=True),
        lax.all_gather(gate_gain, ("dp", "seq"), axis=0, tiled=True),
    )
    length = tokens.shape[1]
    rim_start = length - (KERNEL - 1)
    inputs = tokens.astype(jnp.float32)
    normed_in, norm_pull = jax.vjp(rms_scale, inputs, norm_full)
    lowered = normed_in.astype(jnp.bfloat16)
    projected = jnp.einsum("gtd,dp->gtp", lowered, in_full, preferred_element_type=jnp.float32)
    gate_z = projected[:, :, :DI]
    conv_in = projected[:, :, DI : DI + CONV]
    step_raw = projected[:, :, DI + CONV :]
    previous = from_behind(conv_in[:, rim_start:, :], "seq", 1)
    front_out, front_pull = jax.vjp(front, conv_in, previous, conv_full, step_raw, head_params)
    local_state, decays, head_x, b_proj, c_proj, step_size, decay_sum = front_out
    unit_decay = jnp.ones_like(decays)
    zero_state = jnp.zeros_like(local_state)
    reached, state_in = entering((decays, local_state), "seq", fold_pair, (unit_decay, zero_state))
    out_normed, back_pull = jax.vjp(
        back, head_x, b_proj, c_proj, step_size, decay_sum, head_params, gate_z, gate_full, state_in
    )
    out_lowered = out_normed.astype(jnp.bfloat16)
    branch = jnp.einsum("gti,id->gtd", out_lowered, out_full, preferred_element_type=jnp.float32)
    block_out = (inputs + branch).astype(jnp.bfloat16)
    out_grad_local = jnp.einsum(
        "gti,gtd->id", out_lowered, cotangent, preferred_element_type=jnp.float32
    )
    d_normed = jnp.einsum("gtd,id->gti", cotangent, out_full, preferred_element_type=jnp.float32)
    (
        d_head_x,
        d_b_proj,
        d_c_proj,
        d_step,
        d_decay_sum,
        d_head_back,
        d_gate_z,
        d_gate_gain,
        d_state_in,
    ) = back_pull(d_normed)
    later_decay, d_state_out = prefix(
        (decays, d_state_in), "seq", fold_pair, (unit_decay, zero_state)
    )
    d_decays = jnp.sum(d_state_out * state_in, axis=(2, 3))
    d_conv_in, d_previous, d_conv, d_step_raw, d_head_front = front_pull(
        (d_state_out, d_decays, d_head_x, d_b_proj, d_c_proj, d_step, d_decay_sum)
    )
    returned = from_behind(d_previous.astype(jnp.bfloat16), "seq", -1).astype(d_previous.dtype)
    d_conv_in = jnp.concatenate(
        [d_conv_in[:, :rim_start, :], d_conv_in[:, rim_start:, :] + returned], axis=1
    )
    d_projected = jnp.concatenate([d_gate_z, d_conv_in, d_step_raw], axis=-1).astype(jnp.bfloat16)
    in_grad_local = jnp.einsum(
        "gtd,gtp->dp", lowered, d_projected, preferred_element_type=jnp.float32
    )
    d_normed_in = jnp.einsum(
        "gtp,dp->gtd", d_projected, in_full, preferred_element_type=jnp.float32
    )
    d_inputs, norm_grad_local = norm_pull(d_normed_in)
    tokens_grad = cotangent.astype(jnp.float32) + d_inputs
    head_grad = lax.psum(d_head_back + d_head_front, ("dp", "seq"))
    in_grad, out_grad, conv_grad, norm_grad, gate_grad = (
        lax.psum_scatter(in_grad_local, ("dp", "seq"), scatter_dimension=0, tiled=True),
        lax.psum_scatter(out_grad_local, ("dp", "seq"), scatter_dimension=0, tiled=True),
        lax.psum_scatter(d_conv, ("dp", "seq"), scatter_dimension=1, tiled=True),
        lax.psum_scatter(norm_grad_local, ("dp", "seq"), scatter_dimension=0, tiled=True),
        lax.psum_scatter(d_gate_gain, ("dp", "seq"), scatter_dimension=0, tiled=True),
    )
    in_new, in_mom_new, in_var_new = adamw(in_proj, in_proj_mom, in_proj_var, in_grad, decay_rate)
    out_new, out_mom_new, out_var_new = adamw(
        out_proj, out_proj_mom, out_proj_var, out_grad, decay_rate
    )
    conv_new, conv_mom_new, conv_var_new = adamw(
        conv_params, conv_mom, conv_var, conv_grad, decay_rate
    )
    norm_new, norm_mom_new, norm_var_new = adamw(norm_gain, norm_mom, norm_var, norm_grad, 0.0)
    gate_new, gate_mom_new, gate_var_new = adamw(gate_gain, gate_mom, gate_var, gate_grad, 0.0)
    head_new, head_mom_new, head_var_new = adamw(head_params, head_mom, head_var, head_grad, 0.0)
    return (
        block_out,
        tokens_grad,
        in_grad,
        out_grad,
        conv_grad,
        norm_grad,
        gate_grad,
        head_grad,
        in_new,
        in_mom_new,
        in_var_new,
        out_new,
        out_mom_new,
        out_var_new,
        conv_new,
        conv_mom_new,
        conv_var_new,
        norm_new,
        norm_mom_new,
        norm_var_new,
        gate_new,
        gate_mom_new,
        gate_var_new,
        head_new,
        head_mom_new,
        head_var_new,
    )


class Place:
    def __init__(self):
        self.dp = dp = lax.axis_index("dp")
        self.z = lax.axis_index("seq")
        self.c = c = lax.rem(dp, 2)
        self.x = x = lax.rem(dp // 2, 2)
        self.y = y = dp // 4
        self.line = dp * 4 + self.z
        self.core_peer = {"dp": dp + 1 - 2 * c}
        self.x_peer = {"dp": dp + 2 - 4 * x}
        self.y_peer = {"dp": dp + 4 - 8 * y}

    def z_peer(self, k):
        return {"seq": lax.rem(self.z + k, 4)}

    def any_peer(self, k):
        at = lax.rem(self.line + k, 32)
        return {"dp": at // 4, "seq": lax.rem(at, 4)}

    def near(self):
        return (self.core_peer, self.x_peer, self.y_peer, self.z_peer(1), self.z_peer(2), self.z_peer(3))


def greet(peers):
    bar = pltpu.get_barrier_semaphore()
    for peer in peers:
        pl.semaphore_signal(bar, inc=1, device_id=peer, device_id_type=MESH)
    pl.semaphore_wait(bar, len(peers))


def send(src, dst, out_sem, in_sem, peer):
    return pltpu.make_async_remote_copy(
        src_ref=src, dst_ref=dst, send_sem=out_sem, recv_sem=in_sem, device_id=peer, device_id_type=MESH
    )


class Gather:
    def __init__(self, me, n, src, w, sems, skew):
        self.me, self.n, self.src, self.w, self.sk, self.slots = me, n, src, w, skew, skew + 1
        self.rows = src.shape[2]
        self.o1, self.o2, self.o3, self.o4, self.i1, self.i2, self.i3, self.i4 = sems

    @staticmethod
    def sems(n, skew):
        D = pltpu.SemaphoreType.DMA
        return [D((skew + 1, 3)), D((skew + 1, 2)), D((skew + 1, 2)), D((skew + 1,)), D((n, 3)), D((n, 2)), D((n, 2)), D((n,))]

    def c1(self, i, s, k):
        m, w = self.me, self.w
        rows = pl.ds(pl.multiple_of(m.z * self.rows, 16), self.rows)
        return send(self.src.at[i], w.at[i, :, m.y, m.x, m.c, rows], self.o1.at[s, k - 1], self.i1.at[i, k - 1], m.z_peer(k))

    def c2(self, i, s, h):
        m, w = self.me, self.w
        part = w.at[i, h, m.y, m.x, m.c]
        return send(part, part, self.o2.at[s, h], self.i2.at[i, h], (m.y_peer, m.x_peer)[h])

    def c3(self, i, s, h):
        m, w = self.me, self.w
        part = w.at[i, 0, :, m.x, m.c] if h == 0 else w.at[i, 1, m.y, :, m.c]
        return send(part, part, self.o3.at[s, h], self.i3.at[i, h], (m.x_peer, m.y_peer)[h])

    def c4(self, i, s):
        m, w = self.me, self.w
        part = w.at[i, :, :, :, m.c]
        return send(part, part, self.o4.at[s], self.i4.at[i], m.core_peer)

    def step(self, it):
        n, sk, ns = self.n, self.sk, self.slots

        def stage(lag, body):
            @pl.when((it >= lag * sk) & (it < n + lag * sk))
            def _():
                i = it - lag * sk
                body(i, lax.rem(i, ns))

        def first(i, s):
            m = self.me
            @pl.when(i >= ns)
            def _():
                for k in (1, 2, 3): self.c1(i, s, k).wait_send()
            for k in (2, 1, 3): self.c1(i, s, k).start()
            rows = pl.ds(pl.multiple_of(m.z * self.rows, 16), self.rows)
            for h in range(2):
                self.w[i, h, m.y, m.x, m.c, rows] = self.src[i, h]

        def second(i, s):
            @pl.when(i >= ns)
            def _():
                for h in range(2): self.c2(i, s, h).wait_send()
            for k in (1, 2, 3): self.c1(i, s, k).wait_recv()
            for h in range(2): self.c2(i, s, h).start()

        def third(i, s):
            @pl.when(i >= ns)
            def _():
                for h in range(2): self.c3(i, s, h).wait_send()
            for h in range(2):
                self.c2(i, s, h).wait_recv()
                self.c3(i, s, h).start()

        def fourth(i, s):
            @pl.when(i >= ns)
            def _(): self.c4(i, s).wait_send()
            for h in range(2): self.c3(i, s, h).wait_recv()
            self.c4(i, s).start()

        stage(0, first); stage(1, second); stage(2, third); stage(3, fourth)

    def arrived(self, i):
        self.c4(i, 0).wait_recv()

    def finish(self):
        for j in range(self.slots):
            i = self.n - self.slots + j
            s = i % self.slots
            for k in (1, 2, 3): self.c1(i, s, k).wait_send()
            for h in range(2):
                self.c2(i, s, h).wait_send()
                self.c3(i, s, h).wait_send()
            self.c4(i, s).wait_send()


def windows(width, count):
    return [(o * width // 128) * 128 for o in range(count)]


def gather_call(src_in, src_out, small, tokens, edge, cotangent, collective_id, skew=2):
    NI, NO = src_in.shape[0], src_out.shape[0]
    T, DM = tokens.shape
    TE = T + 16
    DIN = 2 * 16 * 96

    def kernel(src_in, src_out, small_ref, tok_ref, edge_ref, cot_ref,
               proj_hbm, win_hbm, wout_hbm, low_ref, par_ref, dn_ref,
               win, wout, sm, low_e, edge_in, pbuf,
               *sems):
        gs, os_, (sm_out, sm_in, ed_out, ed_in, pb_sem, wi_sem, wo_sem) = sems[:8], sems[8:16], sems[16:]
        me = Place()
        bar = pltpu.get_barrier_semaphore()
        def sig(k, _):
            pl.semaphore_signal(bar, inc=1, device_id=me.any_peer(k), device_id_type=MESH)
            return 0
        lax.fori_loop(1, 32, sig, 0)
        pl.semaphore_wait(bar, 31)
        ga = Gather(me, NI, src_in, win, gs, skew)
        gb = Gather(me, NO, src_out, wout, os_, skew)

        def small_copy(k):
            return send(small_ref, sm.at[me.line], sm_out.at[k - 1], sm_in.at[k - 1], me.any_peer(k))
        def edge_copy():
            return send(edge_ref, edge_in, ed_out, ed_in, {"seq": lax.rem(me.z + 1, 4)})
        lax.fori_loop(1, 32, lambda k, _: (small_copy(k).start(), 0)[1], 0)
        edge_copy().start()
        sm[me.line] = small_ref[...]
        ga.step(0); ga.step(1)
        lax.fori_loop(1, 32, lambda k, _: (small_copy(k).wait(), 0)[1], 0)
        edge_copy().wait()
        par_ref[...] = jnp.zeros_like(par_ref)
        for o in range(32):
            for base, width, row, lo in ((0, 104, 5, 0), (3328, 48, 1, 5), (4864, 96, 1, 6)):
                at = base + (o * width // 128) * 128
                wd = min(256, {0: 3328, 3328: 4864, 4864: 7936}[base] - at)
                par_ref[:, at:at + wd] += sm[o][:, :wd]
        gain = par_ref[5:6, 3328:4864]
        keep = (me.z > 0).astype(f32)

        def norm(v):
            v = v.astype(f32)
            return (v * lax.rsqrt(jnp.mean(v * v, axis=-1, keepdims=True) + 1e-5) * gain).astype(bf)
        def nloop(t, _):
            r = pl.ds(pl.multiple_of(t * 64, 64), 64)
            v = norm(tok_ref[r])
            low_ref[r] = v
            low_e[r] = v
            return 0
        lax.fori_loop(0, T // 64, nloop, 0)
        low_e[T:] = norm(edge_in[...].astype(f32) * keep)

        def pcopy(i, s): return pltpu.make_async_copy(pbuf.at[s], proj_hbm.at[i], pb_sem.at[s])
        def wicopy(i): return pltpu.make_async_copy(win.at[i], win_hbm.at[i], wi_sem.at[i])
        def wocopy(i): return pltpu.make_async_copy(wout.at[i], wout_hbm.at[i], wo_sem.at[i])

        def loop(it, _):
            @pl.when(it >= 2)
            def _(): ga.step(it)
            gb.step(it - NI)
            @pl.when((it >= 4 * skew) & (it < NI + 4 * skew))
            def _():
                i = it - 4 * skew; s = lax.rem(i, 2)
                ga.arrived(i)
                wicopy(i).start()
                @pl.when(i >= 2)
                def _(): pcopy(i - 2, s).wait()
                w = jnp.concatenate([win[i, h].reshape(DM, 128) for h in range(2)], axis=1)
                pbuf[s] = jnp.dot(low_e[...], w, preferred_element_type=f32)
                pcopy(i, s).start()
            @pl.when(it >= NI + 4 * skew)
            def _():
                i = it - 4 * skew - NI
                gb.arrived(i)
                wocopy(i).start()
                for h in range(2):
                    a = cot_ref[:, pl.ds(pl.multiple_of(i * 256 + h * 128, 128), 128)]
                    def cols(q, _):
                        y = q // 4; x = lax.rem(q // 2, 2); c = lax.rem(q, 2)
                        r = lax.dot_general(a, wout[i, h, y, x, c], (((1,), (1,)), ((), ())), preferred_element_type=f32)
                        if h == 0:
                            @pl.when(i == 0)
                            def _(): dn_ref[q] = r
                            @pl.when(i > 0)
                            def _(): dn_ref[q] += r
                        else:
                            dn_ref[q] += r
                        return 0
                    lax.fori_loop(0, 8, cols, 0)
            return 0
        lax.fori_loop(0, NI + NO + 4 * skew, loop, 0)
        pcopy(NI - 2, NI % 2).wait()
        pcopy(NI - 1, (NI - 1) % 2).wait()
        lax.fori_loop(0, NI, lambda i, _: (wicopy(i).wait(), 0)[1], 0)
        lax.fori_loop(0, NO, lambda i, _: (wocopy(i).wait(), 0)[1], 0)
        ga.finish()
        gb.finish()

    V, D = pltpu.VMEM, pltpu.SemaphoreType.DMA
    S = jax.ShapeDtypeStruct
    vm, hb = pl.BlockSpec(memory_space=pltpu.VMEM), pl.BlockSpec(memory_space=pl.ANY)
    wi, wo = (NI, 2, 2, 2, 2, 192, 128), (NO, 2, 2, 2, 2, 384, 128)
    return pl.pallas_call(
        kernel,
        out_shape=(S((NI, TE, 256), f32), S(wi, bf), S(wo, bf), S((T, DM), bf), S((8, 7936), f32), S((8, T, 384), f32)),
        in_specs=[vm] * 6,
        out_specs=(hb, hb, hb, vm, vm, vm),
        scratch_shapes=[V(wi, bf), V(wo, bf), V((32, 8, 256), f32), V((TE, DM), bf), V((16, DM), bf), V((2, TE, 256), f32)]
        + Gather.sems(NI, skew) + Gather.sems(NO, skew)
        + [D((31,)), D((31,)), D, D, D((2,)), D((NI,)), D((NO,))],
        compiler_params=pltpu.CompilerParams(collective_id=collective_id, has_side_effects=True, vmem_limit_bytes=63 << 20),
        name="gather",
    )(src_in, src_out, small, tokens, edge, cotangent)


def arrange(in_proj, out_proj, conv_params, norm_gain, gate_gain, line):
    w = in_proj.astype(bf)
    w = jnp.concatenate([w[:, 3072:], jnp.zeros((48, 208), bf), w[:, :3072]], axis=1)
    src_in = w.reshape(48, 26, 2, 128).transpose(1, 2, 0, 3)
    src_out = out_proj.astype(bf).reshape(96, 6, 2, 128).transpose(1, 2, 0, 3)
    small = jnp.zeros((8, 256), f32)
    for rows, row, width in ((conv_params, 0, 104), (norm_gain[None], 5, 48), (gate_gain[None], 6, 96)):
        small = lax.dynamic_update_slice(small, rows, (row, lax.rem(line * width, 128)))
    return src_in, src_out, small


PAIRS = 24
NN, NT, TN_ = (((1,), (0,)), ((), ())), (((1,), (1,)), ((), ())), (((0,), (0,)), ((), ()))
PASSES = 3


def one(a, b, dims):
    return lax.dot_general(a, b, dims, preferred_element_type=f32)


def halves(a):
    hi = a.astype(bf)
    return hi, (a - hi.astype(f32)).astype(bf)


def mul(a, b, dims=NN):
    if PASSES == 1:
        return one(a.astype(bf), b.astype(bf), dims)
    ah, al = halves(a)
    bh, bl = halves(b)
    return one(ah, bh, dims) + (one(ah, bl, dims) + one(al, bh, dims))


def mul_exact(a, b, dims=NN, left=True):
    v = b if left else a
    h = v.astype(bf)
    r = v - h.astype(f32)
    m = r.astype(bf)
    l = (r - m.astype(f32)).astype(bf)
    if left:
        a = a.astype(bf)
        return one(a, h, dims) + (one(a, m, dims) + one(a, l, dims))
    b = b.astype(bf)
    return one(h, b, dims) + (one(m, b, dims) + one(l, b, dims))


def to_heads(a, spot):
    h, l = halves(a)
    return one(h, spot, NN) + one(l, spot, NN)


def rolled(a, j):
    return pltpu.roll(a, lax.rem(128 - 2 * j, 128), 1)


def spread(r):
    lane = lax.broadcasted_iota(jnp.int32, (r.shape[0], 128), 1)
    return jnp.where(lane < 64, r[:, 0:1], r[:, 1:2])


def masks(rows):
    lane = lax.broadcasted_iota(jnp.int32, (rows, 128), 1)
    return (lane < 64).astype(f32), (lane >= 64).astype(f32)


def spot_of(j):
    p = lax.broadcasted_iota(jnp.int32, (128, 128), 0)
    lane = lax.broadcasted_iota(jnp.int32, (128, 128), 1)
    return (lane == 2 * j + p // 64).astype(bf)


def fill_pad(pad, cin, halo):
    for g in range(2):
        pad[g, 5:8] = halo[8 * g:8 * g + 3]
        pad[g, 8:264] = cin[256 * g:256 * g + 256]


def conv(pad, taps):
    out = []
    for g in range(2):
        acc = taps[4:5]
        for k in range(4):
            acc = acc + taps[k:k + 1] * pad[g, 5 + k:261 + k]
        out.append(acc)
    return out


def sig(v):
    return 1.0 / (1.0 + jnp.exp(-v))


def causal(flip):
    r = lax.broadcasted_iota(jnp.int32, (128, 128), 0)
    c = lax.broadcasted_iota(jnp.int32, (128, 128), 1)
    return (r <= c) if flip else (c <= r)


class Chain:
    def __init__(self, me, by, got, part, out, out_sem, in_sem, keep):
        self.me, self.by, self.got, self.part, self.out, self.out_sem, self.in_sem, self.keep = me, by, got, part, out, out_sem, in_sem, keep
        self.place = me.z if by == 1 else 3 - me.z

    def copy(self, i):
        s = lax.rem(i, 3)
        return send(self.out.at[s], self.got.at[i], self.out_sem.at[s], self.in_sem.at[i], self.me.z_peer(1 if self.by == 1 else 3))

    def tile(self, i):
        @pl.when(self.place > 0)
        def _(): self.copy(i).wait_recv()

        @pl.when(self.place < 3)
        def _():
            @pl.when(i >= 3)
            def _(): self.copy(i - 3).wait_send()
            s = lax.rem(i, 3)
            for g in range(2):
                self.out[s, g] = (self.keep(i, g) * self.got[i, g].astype(f32) + self.part[i, g]).astype(bf)
            self.copy(i).start()

    def start(self):
        @pl.when(self.place == 0)
        def _(): self.got[...] = jnp.zeros_like(self.got)

    def step(self, j):
        lag = 2 * self.place
        @pl.when(j >= lag)
        def _(): self.tile(j - lag)

        @pl.when(j == PAIRS - 1)
        def _():
            lax.fori_loop(PAIRS - lag, PAIRS, lambda i, _: (self.tile(i), 0)[1], 0)
            @pl.when(self.place < 3)
            def _():
                for i in range(PAIRS - 3, PAIRS): self.copy(i).wait_send()

    @staticmethod
    def scratch():
        D = pltpu.SemaphoreType.DMA
        return [V((PAIRS, 2, 128, 128), bf), V((PAIRS, 2, 128, 128), f32), V((3, 2, 128, 128), bf), D((3,)), D((PAIRS,))]


def keeper(ds):
    def keep(i, g):
        end = 256 * g + 248
        return jnp.exp(spread(rolled(ds[end:end + 8], i))[7:8])
    return keep


V = pltpu.VMEM


def sf1_body(j, cin, halo, bcin, bchalo, raw, taps, bctaps, hp, x_o, yi_o, ent_o, step_o, ds_o, dst_o, b_o, c_o, pad, pad2, s_s, bt_s, got, part, out, out_sem, in_sem):
    me = Place()
    line = Chain(me, 1, got, part, out, out_sem, in_sem, keeper(ds_o))
    @pl.when(j == 0)
    def _():
        greet((me.z_peer(1), me.z_peer(3)))
        line.start()
        pre = raw[0] + hp[2:3]
        step = jnp.maximum(pre, 0.0) + jnp.log1p(jnp.exp(-jnp.abs(pre)))
        rate = step * -jnp.exp(hp[0:1])
        step_o[...] = step
        r = lax.broadcasted_iota(jnp.int32, (256, 256), 0)
        c = lax.broadcasted_iota(jnp.int32, (256, 256), 1)
        low = (c <= r).astype(bf)
        for g in range(2):
            ds_o[256 * g:256 * g + 256] = mul_exact(low, rate[256 * g:256 * g + 256])
        turned = ds_o[...].T
        for p in range(PAIRS):
            dst_o[p, 0:2] = turned[2 * p:2 * p + 2]
        fill_pad(pad2, bcin[0], bchalo[0])
        for g, co in enumerate(conv(pad2, bctaps)):
            act = co * sig(co)
            b, c = act[:, :128], act[:, 128:]
            b_o[256 * g:256 * g + 256] = b
            c_o[256 * g:256 * g + 256] = c
            bt_s[g] = b.T
            s_s[g, 0] = mul(c[:128], b[:128], NT)
            s_s[g, 1] = mul(c[128:], b[128:], NT)
            s_s[g, 2] = mul(c[128:], b[:128], NT)

    fill_pad(pad, cin[0], halo[0])
    rds = rolled(ds_o[...], j)
    dsc = spread(rds)
    stc = spread(rolled(step_o[...], j))
    m0, m1 = masks(128)
    ok = causal(False)
    for g, co in enumerate(conv(pad, taps)):
        b0 = 256 * g
        x = co * sig(co)
        x_o[b0:b0 + 256] = x
        xs = x * stc[b0:b0 + 256]
        d = dsc[b0:b0 + 256]
        ys = []
        for q in range(2):
            b = b0 + 128 * q
            w = []
            for h in range(2):
                gap = rds[b:b + 128, h:h + 1] - dst_o[j, h:h + 1, b:b + 128]
                w.append(s_s[g, q] * jnp.exp(jnp.where(ok, gap, -1e30)))
            xq = xs[128 * q:128 * q + 128]
            ys.append(mul(jnp.concatenate(w, 1), jnp.concatenate([xq * m0, xq * m1], 0)))
        mid = d[127:128]
        ys[1] = ys[1] + jnp.exp(d[128:] - mid) * mul(s_s[g, 2], jnp.exp(mid - d[:128]) * xs[:128])
        yi_o[b0:b0 + 128] = ys[0]
        yi_o[b0 + 128:b0 + 256] = ys[1]
        part[j, g] = mul(bt_s[g], jnp.exp(d[255:256] - d) * xs)
    line.step(j)

    @pl.when(j == PAIRS - 1)
    def _(): ent_o[...] = got[...]


def sf2_body(j, yi, x, ent, z, dn, gain, ds, c_r, hp, mixed_o, rq_o, a1, a2):
    @pl.when(j == 0)
    def _():
        a1[...] = jnp.zeros_like(a1)
        a2[...] = jnp.zeros_like(a2)
    dsc = spread(rolled(ds[...], j))
    skip = spread(rolled(hp[...], j))[1:2]
    for g in range(2):
        r = slice(256 * g, 256 * g + 256)
        car = jnp.exp(dsc[r]) * mul(c_r[r], ent[0, g].astype(f32))
        mixed = yi[r] + car + skip * x[r]
        mixed_o[r] = mixed
        zz = z[0, r]
        gated = mixed * (zz * sig(zz))
        a1[r] += gated * gated
        a2[r] += gain[6:7] * dn[0, r] * gated

    @pl.when(j == PAIRS - 1)
    def _():
        r = lax.rsqrt(jnp.sum(a1[...], axis=1, keepdims=True) * (1.0 / 3072) + 1e-5)
        k = r * r * r * (jnp.sum(a2[...], axis=1, keepdims=True) * (1.0 / 3072))
        rq_o[0] = jnp.broadcast_to(r, (512, 128))
        rq_o[1] = jnp.broadcast_to(k, (512, 128))


def sb1_body(j, mixed, z, dn, x, ent, gain, ds, step, dst, b_r, c_r, hp, rq,
             dxa_o, dz_o, ol_o, std_o, rows_o, dst_acc, dc_acc, dds_acc, xu_acc, st_s, ct_s, got, part, out, out_sem, in_sem):
    me = Place()
    line = Chain(me, -1, got, part, out, out_sem, in_sem, keeper(ds))
    @pl.when(j == 0)
    def _():
        greet((me.z_peer(1), me.z_peer(3)))
        line.start()
        for a in (dst_acc, dc_acc, dds_acc, xu_acc):
            a[...] = jnp.zeros_like(a)
        for g in range(2):
            b, c = b_r[256 * g:256 * g + 256], c_r[256 * g:256 * g + 256]
            st_s[g, 0] = mul(b[:128], c[:128], NT)
            st_s[g, 1] = mul(b[128:], c[128:], NT)
            st_s[g, 2] = mul(b[:128], c[128:], NT)
            ct_s[g] = c.T
    rds = rolled(ds[...], j)
    dsc = spread(rds)
    stc = spread(rolled(step[...], j))
    skip = spread(rolled(hp[...], j))[1:2]
    m0, m1 = masks(128)
    ok = causal(True)
    spot = spot_of(j)
    dgain = jnp.zeros((1, 128), f32)
    dskip = jnp.zeros((1, 128), f32)
    for g in range(2):
        r = slice(256 * g, 256 * g + 256)
        zz, mx, xx = z[0, r], mixed[r], x[r]
        s = sig(zz)
        sil = zz * s
        gated = mx * sil
        rr, kk = rq[0, r], rq[1, r]
        gr = gated * rr
        ol_o[r] = (gr * gain[6:7]).astype(bf)
        dgain += jnp.sum(dn[0, r] * gr, axis=0, keepdims=True)
        dg = rr * (gain[6:7] * dn[0, r]) - gated * kk
        dy = dg * sil
        dz_o[0, r] = (dg * mx * (s * (1.0 + zz * (1.0 - s)))).astype(bf)
        dskip += jnp.sum(dy * xx, axis=0, keepdims=True)
        d = dsc[r]
        eu = jnp.exp(d) * dy
        part[j, g] = mul(ct_s[g], eu)
        dc_acc[r] += mul(eu, ent[0, g].astype(f32), NT)
        dds_acc[r] += to_heads(dy * (mx - skip * xx), spot)
        xs = xx * stc[r]
        us = []
        for q in range(2):
            b = 256 * g + 128 * q
            e = []
            for h in range(2):
                gap = dst[j, h:h + 1, b:b + 128] - rds[b:b + 128, h:h + 1]
                e.append(jnp.exp(jnp.where(ok, gap, -1e30)))
            w = jnp.concatenate([st_s[g, q] * e[0], st_s[g, q] * e[1]], 1)
            lo = slice(128 * q, 128 * q + 128)
            dq, xq = dy[lo], xs[lo]
            us.append(mul(w, jnp.concatenate([dq * m0, dq * m1], 0)))
            gt = mul(jnp.concatenate([xq * m0, xq * m1], 0), dq, NT)
            dst_acc[g, q] += gt[:128] * e[0] + gt[128:] * e[1]
        mid = d[127:128]
        v = jnp.exp(mid - d[:128])
        ud = jnp.exp(d[128:] - mid) * dy[128:]
        us[0] = us[0] + v * mul(st_s[g, 2], ud)
        dst_acc[g, 2] += mul(v * xs[:128], ud, NT)
        u = jnp.concatenate(us, 0)
        xu_acc[r] += to_heads(xx * u, spot)
        dxa_o[r] = skip * dy + stc[r] * u
    rows_o[0, 0:1] = dgain
    rows_o[0, 1:2] = dskip
    rows_o[0, 2:8] = jnp.zeros((6, 128), f32)
    line.step(j)

    @pl.when(j == PAIRS - 1)
    def _(): std_o[...] = got[...]


def conv_back(pad, dpad, dco, taps):
    w = taps.shape[1]
    grads = []
    for k in range(4):
        grads.append(sum(jnp.sum(dco[g] * pad[g, 5 + k:261 + k], axis=0, keepdims=True) for g in range(2)))
    grads.append(sum(jnp.sum(dco[g], axis=0, keepdims=True) for g in range(2)))
    grads.append(jnp.zeros((3, w), f32))
    din, prev = [], []
    for g in range(2):
        dpad[g, 0:8] = jnp.zeros((8, w), f32)
        dpad[g, 8:264] = dco[g]
        dpad[g, 264:272] = jnp.zeros((8, w), f32)
        din.append(sum(taps[k:k + 1] * dpad[g, 11 - k:267 - k] for k in range(4)))
        prev.append(sum(taps[k:k + 1] * dpad[g, 3 - k:11 - k] for k in range(4)))
    return jnp.concatenate(grads, 0), din, prev


def sb2_body(j, dxa, x, cin, halo, taps, std, ent, bcin, bchalo, bctaps, raw, ds, step, b_r, c_r, hp, dst_acc, dc_acc, dds_acc, xu_acc,
             dcp_o, cg_o, hg_o, pad, pad2, dpad, dpad2, db_s, xut_s, de_s, prv, lst, got, out_sem, in_sem):
    me = Place()

    def edge(i):
        return send(prv.at[i], got.at[i], out_sem.at[i], in_sem.at[i], me.z_peer(3))

    def pass_edge(i, prev, din):
        for g in range(2):
            lst[i, 8 * g:8 * g + 8] = din[g][248:]
        prv[i] = jnp.concatenate(prev, 0).astype(bf)

        @pl.when(me.z > 0)
        def _(): edge(i).start()

    @pl.when(j == 0)
    def _():
        greet((me.z_peer(1), me.z_peer(3)))
        for a in (db_s, xut_s, de_s):
            a[...] = jnp.zeros_like(a)
    dsc = spread(rolled(ds[...], j))
    stc = spread(rolled(step[...], j))
    spot = spot_of(j)
    fill_pad(pad, cin[0], halo[0])
    dco = []
    for g, co in enumerate(conv(pad, taps)):
        r = slice(256 * g, 256 * g + 256)
        d, xx, st, e = dsc[r], x[r], std[0, g].astype(f32), ent[0, g].astype(f32)
        tail = jnp.exp(d[255:256] - d)
        ut = tail * mul(b_r[r], st)
        xut_s[r] += to_heads(xx * ut, spot)
        db_s[r] += mul(tail * stc[r] * xx, st, NT)
        row = jnp.sum(st * e, axis=0, keepdims=True)
        de_s[g] += to_heads(jnp.broadcast_to(row, (8, 128)), spot)
        dx = dxa[r] + stc[r] * ut
        s = sig(co)
        dco.append(dx * (s * (1.0 + co * (1.0 - s))))
    grads, din, prev = conv_back(pad, dpad, dco, taps)
    cg_o[j] = grads
    p = j // 2
    cols = pl.ds(pl.multiple_of(lax.rem(j, 2) * 128, 128), 128)
    for g in range(2):
        dcp_o[p, 256 * g:256 * g + 256, cols] = din[g].astype(bf)
    pass_edge(j, prev, din)

    @pl.when(j == PAIRS - 1)
    def _():
        fill_pad(pad2, bcin[0], bchalo[0])
        dco2 = []
        for g, co in enumerate(conv(pad2, bctaps)):
            r0 = 256 * g
            b, c = b_r[r0:r0 + 256], c_r[r0:r0 + 256]
            db, dc = db_s[r0:r0 + 256], dc_acc[r0:r0 + 256]
            db = db + jnp.concatenate([mul(dst_acc[g, 0], c[:128]) + mul(dst_acc[g, 2], c[128:]), mul(dst_acc[g, 1], c[128:])], 0)
            dc = dc + jnp.concatenate([mul(dst_acc[g, 0].T, b[:128]), mul(dst_acc[g, 1].T, b[128:]) + mul(dst_acc[g, 2].T, b[:128])], 0)
            s = sig(co)
            dco2.append(jnp.concatenate([db, dc], 1) * (s * (1.0 + co * (1.0 - s))))
        grads, din, prev = conv_back(pad2, dpad2, dco2, bctaps)
        cg_o[24] = grads[:, :128]
        cg_o[25] = grads[:, 128:]
        for g in range(2):
            dcp_o[12, 256 * g:256 * g + 256] = din[g].astype(bf)
        for h in range(2):
            lanes = slice(128 * h, 128 * h + 128)
            pass_edge(PAIRS + h, [a[:, lanes] for a in prev], [a[:, lanes] for a in din])
        st = step[...]
        xut = xut_s[...]
        speed = -jnp.exp(hp[0:1])
        dds = dds_acc[...] - st * (xu_acc[...] + xut)
        lane = lax.broadcasted_iota(jnp.int32, (512, 128), 1)
        tok = lax.broadcasted_iota(jnp.int32, (256, 128), 0)
        rr = lax.broadcasted_iota(jnp.int32, (256, 256), 0)
        cc = lax.broadcasted_iota(jnp.int32, (256, 256), 1)
        up = (cc >= rr).astype(bf)
        drate = []
        for g in range(2):
            r = slice(256 * g, 256 * g + 256)
            end = jnp.sum(st[r] * xut[r], axis=0, keepdims=True) + de_s[g][0:1] * jnp.exp(ds[256 * g + 255:256 * g + 256])
            drate.append(mul_exact(up, dds[r] + jnp.where(tok == 255, end, 0.0)))
        drate = jnp.concatenate(drate, 0)
        dstep = xu_acc[...] + xut + drate * speed
        draw = jnp.where(lane < 48, dstep * sig(raw[0] + hp[2:3]), 0.0)
        dcp_o[13, :, 0:128] = draw.astype(bf)
        dcp_o[13, :, 128:256] = jnp.zeros((512, 128), bf)
        hg_o[0:1] = jnp.sum(drate * st * speed, axis=0, keepdims=True)
        hg_o[1:2] = jnp.zeros((1, 128), f32)
        hg_o[2:3] = jnp.sum(draw, axis=0, keepdims=True)
        hg_o[3:8] = jnp.zeros((5, 128), f32)

        @pl.when(me.z < 3)
        def _():
            def patch(i, _):
                edge(i).wait_recv()
                at = pl.ds(pl.multiple_of(lax.rem(i, 2) * 128, 128), 128)
                for g in range(2):
                    rows = lst[i, 8 * g:8 * g + 8] + got[i, 8 * g:8 * g + 8].astype(f32)
                    dcp_o[i // 2, 256 * g + 248:256 * g + 256, at] = rows.astype(bf)
                return 0
            lax.fori_loop(0, PAIRS + 2, patch, 0)

        @pl.when(me.z > 0)
        def _(): lax.fori_loop(0, PAIRS + 2, lambda i, _: (edge(i).wait_send(), 0)[1], 0)


S = jax.ShapeDtypeStruct
V = pltpu.VMEM


def const(*shape):
    return pl.BlockSpec(shape, lambda j: (0,) * len(shape))


TILE = pl.BlockSpec((1, 512, 128), lambda j: (j // 2, 0, lax.rem(j, 2)))
HALO = pl.BlockSpec((1, 16, 128), lambda j: (j // 2, 32, lax.rem(j, 2)))
ZT = pl.BlockSpec((1, 512, 128), lambda j: (14 + j // 2, 0, lax.rem(j, 2)))
BC = pl.BlockSpec((1, 512, 256), lambda j: (12, 0, 0))
BCH = pl.BlockSpec((1, 16, 256), lambda j: (12, 32, 0))
RAW = pl.BlockSpec((1, 512, 128), lambda j: (13, 0, 0))
TAP = pl.BlockSpec((8, 128), lambda j: (0, j))
BCT = pl.BlockSpec((8, 256), lambda j: (0, 12))
GAIN = pl.BlockSpec((8, 128), lambda j: (0, 38 + j))
HP = const(8, 128)
COL = pl.BlockSpec((512, 128), lambda j: (0, j))
ST = pl.BlockSpec((1, 2, 128, 128), lambda j: (j, 0, 0, 0))
DN = pl.BlockSpec((1, 512, 128), lambda j: (j // 3, 0, lax.rem(j, 3)))
TOK = const(512, 128)
TOKT = const(24, 8, 512)


def call(body, name, in_specs, out_shape, out_specs, scratch, args, cid=None):
    def kernel(*refs):
        body(pl.program_id(0), *refs)
    return pl.pallas_call(
        kernel, grid=(PAIRS,), in_specs=in_specs, out_specs=out_specs, out_shape=out_shape, scratch_shapes=scratch,
        compiler_params=pltpu.CompilerParams(vmem_limit_bytes=60 << 20, collective_id=cid, has_side_effects=cid is not None), name=name,
    )(*args)


def sf1(proj, par, hp):
    return call(sf1_body, "sf1", [TILE, HALO, BC, BCH, RAW, TAP, BCT, HP],
        (S((512, 3072), f32), S((512, 3072), f32), S((24, 2, 128, 128), bf), S((512, 128), f32), S((512, 128), f32), S((24, 8, 512), f32), S((512, 128), f32), S((512, 128), f32)),
        (COL, COL, const(24, 2, 128, 128), TOK, TOK, TOKT, TOK, TOK),
        [V((2, 264, 128), f32), V((2, 264, 256), f32), V((2, 3, 128, 128), f32), V((2, 128, 256), f32)] + Chain.scratch(),
        (proj, proj, proj, proj, proj, par, par, hp), 4)


def sf2(yi, x, ent, proj, dn, par, ds, c, hp):
    return call(sf2_body, "sf2", [COL, COL, ST, ZT, DN, GAIN, TOK, TOK, HP],
        (S((512, 3072), f32), S((2, 512, 128), f32)), (COL, const(2, 512, 128)),
        [V((512, 128), f32), V((512, 128), f32)],
        (yi, x, ent, proj, dn, par, ds, c, hp))


def sb1(mixed, proj, dn, x, ent, par, ds, step, dst, b, c, hp, rq):
    return call(sb1_body, "sb1", [COL, ZT, DN, COL, ST, GAIN, TOK, TOK, TOKT, TOK, TOK, HP, const(2, 512, 128)],
        (S((512, 3072), f32), S((12, 512, 256), bf), S((512, 3072), bf), S((24, 2, 128, 128), bf), S((24, 8, 128), f32),
         S((2, 3, 128, 128), f32), S((512, 128), f32), S((512, 128), f32), S((512, 128), f32)),
        (COL, pl.BlockSpec((1, 512, 128), lambda j: (j // 2, 0, lax.rem(j, 2))), COL, const(24, 2, 128, 128), pl.BlockSpec((1, 8, 128), lambda j: (j, 0, 0)),
         const(2, 3, 128, 128), TOK, TOK, TOK),
        [V((2, 3, 128, 128), f32), V((2, 128, 256), f32)] + Chain.scratch(),
        (mixed, proj, dn, x, ent, par, ds, step, dst, b, c, hp, rq), 5)


def sb2(dxa, x, proj, par, std, ent, ds, step, b, c, hp, acc):
    return call(sb2_body, "sb2", [COL, COL, TILE, HALO, TAP, ST, ST, BC, BCH, BCT, RAW, TOK, TOK, TOK, TOK, HP, const(2, 3, 128, 128), TOK, TOK, TOK],
        (S((14, 512, 256), bf), S((26, 8, 128), f32), S((8, 128), f32)),
        (const(14, 512, 256), const(26, 8, 128), HP),
        [V((2, 264, 128), f32), V((2, 264, 256), f32), V((2, 272, 128), f32), V((2, 272, 256), f32), V((512, 128), f32), V((512, 128), f32), V((2, 8, 128), f32),
         V((26, 16, 128), bf), V((26, 16, 128), f32), V((26, 16, 128), bf), pltpu.SemaphoreType.DMA((26,)), pltpu.SemaphoreType.DMA((26,))],
        (dxa, x, proj, proj, par, std, ent, proj, proj, par, proj, ds, step, b, c, hp) + tuple(acc), 6)


class Reduce:
    def __init__(self, me, n, rows, refs, skew):
        self.me, self.n, self.rows, self.sk, self.slots = me, n, rows, skew, skew + 1
        (self.own0, self.own1, self.own2, self.own3, self.s0, self.s1, self.s2, self.s3, self.r0, self.r1, self.r2, self.r3,
         self.o0, self.o1, self.o2, self.o3, self.i0, self.i1, self.i2, self.i3) = refs

    @staticmethod
    def scratch(n, rows, skew):
        V, D, k = pltpu.VMEM, pltpu.SemaphoreType.DMA, skew + 1
        z = 4 * rows
        return [V((k, 2, 2, 2, z, 128), f32), V((k, 2, 2, z, 128), f32), V((k, 2, z, 128), f32), V((k, 2, rows, 128), f32),
                V((k, 2, 2, 2, z, 128), bf), V((k, 2, 2, z, 128), bf), V((k, 2, z, 128), bf), V((k, 3, 2, rows, 128), bf),
                V((n, 2, 2, 2, z, 128), bf), V((n, 2, 2, z, 128), bf), V((n, 2, z, 128), bf), V((n, 3, 2, rows, 128), bf),
                D((k,)), D((k, 2)), D((k, 2)), D((k, 3)), D((n,)), D((n, 2)), D((n, 2)), D((n, 3))]

    def c0(self, i, s):
        return send(self.s0.at[s], self.r0.at[i], self.o0.at[s], self.i0.at[i], self.me.core_peer)

    def c1(self, i, s, h):
        return send(self.s1.at[s, h], self.r1.at[i, h], self.o1.at[s, h], self.i1.at[i, h], (self.me.x_peer, self.me.y_peer)[h])

    def c2(self, i, s, h):
        return send(self.s2.at[s, h], self.r2.at[i, h], self.o2.at[s, h], self.i2.at[i, h], (self.me.y_peer, self.me.x_peer)[h])

    def c3(self, i, s, k):
        return send(self.s3.at[s, k - 1], self.r3.at[i, k - 1], self.o3.at[s, k - 1], self.i3.at[i, k - 1], self.me.z_peer(k))

    def step(self, it, product, out_ref):
        n, sk, ns, R = self.n, self.sk, self.slots, self.rows
        me, x, y, z, c = self.me, self.me.x, self.me.y, self.me.z, self.me.c

        def stage(lag, body):
            @pl.when((it >= lag * sk) & (it < n + lag * sk))
            def _():
                i = it - lag * sk
                body(i, lax.rem(i, ns))

        def zero(i, s):
            @pl.when(i >= ns)
            def _(): self.c0(i, s).wait_send()
            part = product(i, 1 - c).astype(bf)
            for h in range(2):
                self.s0[s, h] = part[..., h * 128:(h + 1) * 128]
            self.c0(i, s).start()
            part = product(i, c)
            for h in range(2):
                self.own0[s, h] = part[..., h * 128:(h + 1) * 128]

        def first(i, s):
            own0, r0, own1 = self.own0, self.r0, self.own1
            @pl.when(i >= ns)
            def _():
                for h in range(2): self.c1(i, s, h).wait_send()
            self.c0(i, s).wait_recv()
            for a in range(2):
                self.s1[s, 0, a] = (own0[s, 0, a, 1 - x] + r0[i, 0, a, 1 - x].astype(f32)).astype(bf)
            self.c1(i, s, 0).start()
            self.s1[s, 1] = (own0[s, 1, 1 - y] + r0[i, 1, 1 - y].astype(f32)).astype(bf)
            self.c1(i, s, 1).start()
            for a in range(2):
                own1[s, 0, a] = own0[s, 0, a, x] + r0[i, 0, a, x].astype(f32)
            own1[s, 1] = own0[s, 1, y] + r0[i, 1, y].astype(f32)

        def second(i, s):
            own1, r1 = self.own1, self.r1
            @pl.when(i >= ns)
            def _():
                for h in range(2): self.c2(i, s, h).wait_send()
            for h, g in ((0, y), (1, x)):
                self.c1(i, s, h).wait_recv()
                self.s2[s, h] = (own1[s, h, 1 - g] + r1[i, h, 1 - g].astype(f32)).astype(bf)
                self.c2(i, s, h).start()
                self.own2[s, h] = own1[s, h, g] + r1[i, h, g].astype(f32)

        def third(i, s):
            own2, r2 = self.own2, self.r2
            @pl.when(i >= ns)
            def _():
                for k in (1, 2, 3): self.c3(i, s, k).wait_send()
            for h in range(2): self.c2(i, s, h).wait_recv()
            for k in (2, 1, 3):
                rows = pl.ds(pl.multiple_of(lax.rem(z + k, 4) * R, 16), R)
                for h in range(2):
                    self.s3[s, k - 1, h] = (own2[s, h, rows] + r2[i, h, rows].astype(f32)).astype(bf)
                self.c3(i, s, k).start()
            rows = pl.ds(pl.multiple_of(z * R, 16), R)
            for h in range(2):
                self.own3[s, h] = own2[s, h, rows] + r2[i, h, rows].astype(f32)

        def last(i, s):
            for k in (1, 2, 3): self.c3(i, s, k).wait_recv()
            acc = self.own3[s]
            for k in range(3): acc = acc + self.r3[i, k].astype(f32)
            out_ref[i] = acc

        stage(0, zero); stage(1, first); stage(2, second); stage(3, third); stage(4, last)

    def finish(self):
        for j in range(self.slots):
            i = self.n - self.slots + j
            s = i % self.slots
            self.c0(i, s).wait_send()
            for h in range(2):
                self.c1(i, s, h).wait_send()
                self.c2(i, s, h).wait_send()
            for k in (1, 2, 3): self.c3(i, s, k).wait_send()


def prod(lhs_ref, c, rhs, R):
    lhs = lhs_ref[:, c].reshape(16 * R, 512)
    return jnp.dot(lhs, rhs, preferred_element_type=f32).reshape(2, 2, 4 * R, 256)


def out_call(out_low, out_low_t, cot, tokens, wout, collective_id, skew=2):
    n, R = 6, 96

    def kernel(ol, lhs, cot_ref, tok, w_hbm, sums, blk, wbuf, wsem, *refs):
        me = Place()
        greet(me.near())
        red = Reduce(me, n, R, refs, skew)
        def wcopy(i): return pltpu.make_async_copy(w_hbm.at[i], wbuf.at[lax.rem(i, 2)], wsem.at[lax.rem(i, 2)])
        wcopy(0).start()

        def cols(i): return pl.ds(pl.multiple_of(i * 256, 256), 256)
        def loop(it, _):
            red.step(it, lambda i, c: prod(lhs, c, cot_ref[:, cols(i)], R), sums)
            @pl.when(it < n)
            def _():
                wcopy(it).wait()
                @pl.when(it + 1 < n)
                def _(): wcopy(it + 1).start()
                s = lax.rem(it, 2)
                w = jnp.concatenate([wbuf[s, h].reshape(3072, 128) for h in range(2)], axis=1)
                branch = jnp.dot(ol[...], w, preferred_element_type=f32)
                blk[:, cols(it)] = (tok[:, cols(it)].astype(f32) + branch).astype(bf)
            return 0
        lax.fori_loop(0, n + 4 * skew, loop, 0)
        red.finish()

    V, D, Sd = pltpu.VMEM, pltpu.SemaphoreType.DMA, jax.ShapeDtypeStruct
    vm = pl.BlockSpec(memory_space=pltpu.VMEM)
    return pl.pallas_call(
        kernel, out_shape=(Sd((n, 2, R, 128), f32), Sd((512, 1536), bf)),
        in_specs=[vm] * 4 + [pl.BlockSpec(memory_space=pl.ANY)], out_specs=(vm, vm),
        scratch_shapes=[V((2, 2, 2, 2, 2, 384, 128), bf), D((2,))] + Reduce.scratch(n, R, skew),
        compiler_params=pltpu.CompilerParams(collective_id=collective_id, has_side_effects=True, vmem_limit_bytes=63 << 20), name="outgrad",
    )(out_low, out_low_t.reshape(4, 2, 384, 512), cot, tokens, wout)


def in_call(low_t, dcp, dz, win, tok, cot, par, cg, rows, hg, collective_id, skew=2):
    n, R = 26, 48

    def kernel(lhs, dcp_ref, dz_ref, w_hbm, tok, cot, par_ref, cg_ref, rows_ref, hg_ref, sums, tg, small_o,
               wbuf, wsem, dp, dn, flat, mail, box, m_out, m_in, *refs):
        me = Place()
        bar = pltpu.get_barrier_semaphore()
        def sig(k, _):
            pl.semaphore_signal(bar, inc=1, device_id=me.any_peer(k), device_id_type=MESH)
            return 0
        lax.fori_loop(1, 32, sig, 0)
        pl.semaphore_wait(bar, 31)
        red = Reduce(me, n, R, refs, skew)
        def wcopy(i): return pltpu.make_async_copy(w_hbm.at[i], wbuf.at[lax.rem(i, 2)], wsem.at[lax.rem(i, 2)])
        wcopy(0).start()
        def post(k):
            to = lax.rem(me.line + k, 32)
            return send(mail.at[to], box.at[k - 1], m_out.at[k - 1], m_in.at[k - 1], me.any_peer(k))

        def tail():
            gain = par_ref[5:6, 3328:4864]
            def block(t, acc):
                r = pl.ds(pl.multiple_of(t * 64, 64), 64)
                xf = tok[r].astype(f32)
                h = lax.rsqrt(jnp.mean(xf * xf, axis=-1, keepdims=True) + 1e-5)
                d = dn[r]
                gd = d * gain
                tg[r] = cot[r].astype(f32) + (h * gd - xf * (h * h * h * jnp.mean(gd * xf, axis=-1, keepdims=True)))
                return acc + jnp.sum(d * xf * h, axis=0, keepdims=True)
            norm = lax.fori_loop(0, 8, block, jnp.zeros((1, 1536), f32))
            flat[...] = jnp.zeros_like(flat)
            for j in range(26):
                flat[0:5, 128 * j:128 * j + 128] = cg_ref[j, 0:5]
            flat[5:6, 0:1536] = norm
            for j in range(24):
                flat[6:7, 128 * j:128 * j + 128] = rows_ref[j, 0:1]
            for o in range(32):
                b = [(o * w // 128) * 128 for w in (104, 48, 96)]
                mail[o, 0:5] = flat[0:5, b[0]:b[0] + 256]
                mail[o, 5:6] = flat[5:6, b[1]:b[1] + 256]
                mail[o, 6:7] = flat[6:7, b[2]:b[2] + 256]
                mail[o, 7:8] = hg_ref[0:1]
            lax.fori_loop(1, 32, lambda k, _: (post(k).start(), 0)[1], 0)

        def loop(it, _):
            @pl.when(it < 14)
            def _(): dp[...] = dcp_ref[lax.rem(it, 14)]
            @pl.when((it >= 14) & (it < n))
            def _(): dp[...] = dz_ref[lax.rem(it + 12 - 14, 12)]
            red.step(it, lambda i, c: prod(lhs, c, dp[...], R), sums)
            @pl.when(it < n)
            def _():
                wcopy(it).wait()
                @pl.when(it + 1 < n)
                def _(): wcopy(it + 1).start()
                s = lax.rem(it, 2)
                w = jnp.concatenate([wbuf[s, h].reshape(1536, 128) for h in range(2)], axis=1)
                r = lax.dot_general(dp[...], w, (((1,), (1,)), ((), ())), preferred_element_type=f32)
                @pl.when(it == 0)
                def _(): dn[...] = r
                @pl.when(it > 0)
                def _(): dn[...] += r
            @pl.when(it == n)
            def _(): tail()
            return 0
        lax.fori_loop(0, n + 4 * skew, loop, 0)
        small_o[...] = mail[me.line]
        def take(k, _):
            post(k).wait()
            small_o[...] += box[k - 1]
            return 0
        lax.fori_loop(1, 32, take, 0)
        red.finish()

    V, D, Sd = pltpu.VMEM, pltpu.SemaphoreType.DMA, jax.ShapeDtypeStruct
    vm = pl.BlockSpec(memory_space=pltpu.VMEM)
    return pl.pallas_call(
        kernel, out_shape=(Sd((n, 2, R, 128), f32), Sd((512, 1536), f32), Sd((8, 256), f32)),
        in_specs=[vm] * 3 + [pl.BlockSpec(memory_space=pl.ANY)] + [vm] * 6, out_specs=(vm, vm, vm),
        scratch_shapes=[V((2, 2, 2, 2, 2, 192, 128), bf), D((2,)), V((512, 256), bf), V((512, 1536), f32), V((8, 3584), f32), V((32, 8, 256), f32), V((31, 8, 256), f32), D((31,)), D((31,))]
        + Reduce.scratch(n, R, skew),
        compiler_params=pltpu.CompilerParams(collective_id=collective_id, has_side_effects=True, vmem_limit_bytes=63 << 20), name="ingrad",
    )(low_t.reshape(4, 2, 192, 512), dcp, dz, win, tok, cot, par, cg, rows, hg)


def fast(adamw, tokens, cotangent, in_proj, in_mom, in_var, out_proj, out_mom, out_var, conv_params, conv_mom, conv_var,
         norm_gain, norm_mom, norm_var, gate_gain, gate_mom, gate_var, head_params, head_mom, head_var):
    line = lax.axis_index("dp") * 4 + lax.axis_index("seq")
    src_in, src_out, small = arrange(in_proj, out_proj, conv_params, norm_gain, gate_gain, line)
    edge = jnp.pad(tokens[:, 253:], ((0, 0), (0, 5), (0, 0))).reshape(16, 1536)
    tok, cot = tokens.reshape(512, 1536), cotangent.reshape(512, 1536)
    proj, win, wout, low, par, dn = gather_call(src_in, src_out, small, tok, edge, cot, 1)
    hp = jnp.pad(head_params, ((0, 5), (0, 80)))
    x, yi, ent, step, ds, dst, b, c = sf1(proj, par, hp)
    mixed, rq = sf2(yi, x, ent, proj, dn, par, ds, c, hp)
    dxa, dz, ol, std, rows, *acc = sb1(mixed, proj, dn, x, ent, par, ds, step, dst, b, c, hp, rq)
    dcp, cg, hg = sb2(dxa, x, proj, par, std, ent, ds, step, b, c, hp, acc)
    out_sums, block = out_call(ol, ol.T, cot, tok, wout, 2)
    skip = jnp.sum(rows[:, 1].reshape(48, 64), axis=1)
    heads = jnp.pad(jnp.concatenate([hg[0, :48], skip, hg[2, :48]])[None], ((0, 7), (0, 112)))
    in_sums, tokens_grad, small_sum = in_call(low.T, dcp, dz, win, tok, cot, par, cg, rows, heads, 3)
    out_grad = out_sums.transpose(2, 0, 1, 3).reshape(96, 1536)
    in_sums = in_sums.transpose(2, 0, 1, 3).reshape(48, 6656)
    in_grad = jnp.concatenate([in_sums[:, 3584:], in_sums[:, :3376]], axis=1)
    tokens_grad = tokens_grad.reshape(2, 256, 1536)
    mine = lambda row, n, w: lax.dynamic_slice(small_sum, (row, lax.rem(line * w, 128)), (n, w))
    conv_grad, norm_grad, gate_grad = mine(0, 5, 104), mine(5, 1, 48)[0], mine(6, 1, 96)[0]
    head_grad = small_sum[7, :144].reshape(3, 48)
    res = [(in_proj, in_mom, in_var, in_grad, 0.1), (out_proj, out_mom, out_var, out_grad, 0.1), (conv_params, conv_mom, conv_var, conv_grad, 0.1),
           (norm_gain, norm_mom, norm_var, norm_grad, 0.0), (gate_gain, gate_mom, gate_var, gate_grad, 0.0), (head_params, head_mom, head_var, head_grad, 0.0)]
    new = [v for a in res for v in adamw(*a)]
    return (block.reshape(2, 256, 1536), tokens_grad, in_grad, out_grad, conv_grad, norm_grad, gate_grad, head_grad, *new)


def solution(mesh):
    in_specs = (
        P("dp", "seq", None),
        P("dp", "seq", None),
        P(("dp", "seq"), None),
        P(("dp", "seq"), None),
        P(("dp", "seq"), None),
        P(("dp", "seq"), None),
        P(("dp", "seq"), None),
        P(("dp", "seq"), None),
        P(None, ("dp", "seq")),
        P(None, ("dp", "seq")),
        P(None, ("dp", "seq")),
        P(("dp", "seq")),
        P(("dp", "seq")),
        P(("dp", "seq")),
        P(("dp", "seq")),
        P(("dp", "seq")),
        P(("dp", "seq")),
        P(),
        P(),
        P(),
    )
    out_specs = (
        P("dp", "seq", None),
        P("dp", "seq", None),
        P(("dp", "seq"), None),
        P(("dp", "seq"), None),
        P(None, ("dp", "seq")),
        P(("dp", "seq")),
        P(("dp", "seq")),
        P(),
        P(("dp", "seq"), None),
        P(("dp", "seq"), None),
        P(("dp", "seq"), None),
        P(("dp", "seq"), None),
        P(("dp", "seq"), None),
        P(("dp", "seq"), None),
        P(None, ("dp", "seq")),
        P(None, ("dp", "seq")),
        P(None, ("dp", "seq")),
        P(("dp", "seq")),
        P(("dp", "seq")),
        P(("dp", "seq")),
        P(("dp", "seq")),
        P(("dp", "seq")),
        P(("dp", "seq")),
        P(),
        P(),
        P(),
    )
    own = tuple(mesh.shape[a] for a in ("dp", "seq")) == (8, 4)
    step = functools.partial(fast, adamw) if own else body
    return jax.shard_map(step, mesh=mesh, in_specs=in_specs, out_specs=out_specs, check_vma=False)
```

```python
import functools

import jax
import jax.numpy as jnp
from jax import lax
from jax.experimental import pallas as pl
from jax.experimental.pallas import tpu as pltpu
from jax.sharding import PartitionSpec as P

MESH = pl.DeviceIdType.MESH
bf = jnp.bfloat16
f32 = jnp.float32

DI = 3072
HEADS = 48
HEAD_DIM = 64
STATE = 128
KERNEL = 4
STEP = 3
CONV = 3328


highest = lax.Precision.HIGHEST
norm_eps = 1e-05
beta_one = 0.9
beta_two = 0.95
learn_rate = 0.01
decay_rate = 0.1
adam_eps = 1e-08


def from_behind(array, axis, by):
    size = lax.axis_size(axis)
    pairs = [(i, i + by) for i in range(size) if 0 <= i + by < size]
    return lax.ppermute(array, axis, pairs)


def entering(part, axis, combine, identity):
    place = lax.axis_index(axis)
    gathered = jax.tree.map(lambda a: lax.all_gather(a, axis), part)
    state = jax.tree.map(lambda a, e: jnp.zeros_like(a) + jnp.asarray(e, a.dtype), part, identity)

    def one(lap, state):
        return combine(
            state, jax.tree.map(lambda a: lax.dynamic_index_in_dim(a, lap, 0, False), gathered)
        )

    return lax.fori_loop(0, place, one, state)


def prefix(array, axis, combine, identity):
    size, here = (lax.axis_size(axis), lax.axis_index(axis))
    everything = jax.tree.map(
        lambda part, kind: lax.all_gather(part.astype(kind), axis),
        array,
        jax.tree.map(lambda a: jnp.bfloat16 if a.dtype == jnp.float32 else a.dtype, array),
    )
    start = jax.tree.map(
        lambda part, zero: jnp.broadcast_to(jnp.asarray(zero, part.dtype), part.shape),
        array,
        identity,
    )

    def lap(k, before):
        at = size - 1 - k
        reached = at > here
        new = combine(
            before, jax.tree.map(lambda part, own: part[at].astype(own.dtype), everything, array)
        )
        return jax.tree.map(lambda a, b: jnp.where(reached, a, b), new, before)

    return lax.fori_loop(0, size, lap, start)


def rms_scale(values, gain):
    return values * lax.rsqrt(jnp.mean(values * values, axis=-1, keepdims=True) + norm_eps) * gain


def adamw(weight, moment_one, moment_two, gradient, decay_on):
    one_new = beta_one * moment_one + (1.0 - beta_one) * gradient
    two_new = beta_two * moment_two + (1.0 - beta_two) * gradient * gradient
    mean_hat = one_new / (1.0 - beta_one**STEP)
    var_hat = two_new / (1.0 - beta_two**STEP)
    weight_new = weight - learn_rate * (
        mean_hat / (jnp.sqrt(var_hat) + adam_eps) + decay_on * weight
    )
    return (weight_new, one_new, two_new)


def fold_pair(earlier, later):
    decay_early, state_early = earlier
    decay_later, state_later = later
    return (decay_early * decay_later, decay_later[:, :, None, None] * state_early + state_later)


def intra_item(pieces):
    head_x, b_proj, c_proj, step_size, decay_sum = pieces
    length = decay_sum.shape[0]
    scores = jnp.dot(c_proj, b_proj.T, precision=highest)
    row_ids = lax.broadcasted_iota(jnp.int32, (length, length), 0)
    col_ids = lax.broadcasted_iota(jnp.int32, (length, length), 1)
    causal = (col_ids <= row_ids)[None, :, :]
    sums_by_head = decay_sum.T
    gap_sums = sums_by_head[:, :, None] - sums_by_head[:, None, :]
    decay_mat = jnp.exp(jnp.where(causal, gap_sums, -1e30))
    weights = scores[None, :, :] * decay_mat * step_size.T[:, None, :]
    return jnp.einsum("hts,shp->thp", weights, head_x, precision=highest)


def front(conv_in, previous, conv_weight, step_raw, head_weight):
    seq_count = conv_in.shape[0]
    length = conv_in.shape[1]
    padded = jnp.concatenate([previous, conv_in], axis=1)
    conv_out = conv_weight[KERNEL]
    for tap_index in range(KERNEL):
        conv_out = conv_out + conv_weight[tap_index] * padded[:, tap_index : tap_index + length, :]
    activated = jax.nn.silu(conv_out)
    head_x = activated[:, :, :DI].reshape(seq_count, length, HEADS, HEAD_DIM)
    b_proj = activated[:, :, DI : DI + STATE]
    c_proj = activated[:, :, DI + STATE :]
    step_size = jax.nn.softplus(step_raw + head_weight[2])
    decay_sum = jnp.cumsum(step_size * -jnp.exp(head_weight[0]), axis=1)
    last_sum = decay_sum[:, -1, :]
    tail_weight = jnp.exp(last_sum[:, None, :] - decay_sum) * step_size
    local_state = jnp.einsum("gsh,gshp,gsn->ghpn", tail_weight, head_x, b_proj, precision=highest)
    return (local_state, jnp.exp(last_sum), head_x, b_proj, c_proj, step_size, decay_sum)


def back(head_x, b_proj, c_proj, step_size, decay_sum, head_weight, gate_z, gate_weight, state_in):
    seq_count = gate_z.shape[0]
    length = gate_z.shape[1]
    inner_out = lax.map(jax.checkpoint(intra_item), (head_x, b_proj, c_proj, step_size, decay_sum))
    carried = jnp.exp(decay_sum)[..., None] * jnp.einsum(
        "gtn,ghpn->gthp", c_proj, state_in, precision=highest
    )
    mixed_y = inner_out + carried + head_weight[1][:, None] * head_x
    gated = mixed_y.reshape(seq_count, length, DI) * jax.nn.silu(gate_z)
    return rms_scale(gated, gate_weight)


def body(
    tokens,
    cotangent,
    in_proj,
    in_proj_mom,
    in_proj_var,
    out_proj,
    out_proj_mom,
    out_proj_var,
    conv_params,
    conv_mom,
    conv_var,
    norm_gain,
    norm_mom,
    norm_var,
    gate_gain,
    gate_mom,
    gate_var,
    head_params,
    head_mom,
    head_var,
):
    in_full, out_full = (
        lax.all_gather(in_proj.astype(jnp.bfloat16), ("dp", "seq"), axis=0, tiled=True),
        lax.all_gather(out_proj.astype(jnp.bfloat16), ("dp", "seq"), axis=0, tiled=True),
    )
    conv_full, norm_full, gate_full = (
        lax.all_gather(conv_params, ("dp", "seq"), axis=1, tiled=True),
        lax.all_gather(norm_gain, ("dp", "seq"), axis=0, tiled=True),
        lax.all_gather(gate_gain, ("dp", "seq"), axis=0, tiled=True),
    )
    length = tokens.shape[1]
    rim_start = length - (KERNEL - 1)
    inputs = tokens.astype(jnp.float32)
    normed_in, norm_pull = jax.vjp(rms_scale, inputs, norm_full)
    lowered = normed_in.astype(jnp.bfloat16)
    projected = jnp.einsum("gtd,dp->gtp", lowered, in_full, preferred_element_type=jnp.float32)
    gate_z = projected[:, :, :DI]
    conv_in = projected[:, :, DI : DI + CONV]
    step_raw = projected[:, :, DI + CONV :]
    previous = from_behind(conv_in[:, rim_start:, :], "seq", 1)
    front_out, front_pull = jax.vjp(front, conv_in, previous, conv_full, step_raw, head_params)
    local_state, decays, head_x, b_proj, c_proj, step_size, decay_sum = front_out
    unit_decay = jnp.ones_like(decays)
    zero_state = jnp.zeros_like(local_state)
    reached, state_in = entering((decays, local_state), "seq", fold_pair, (unit_decay, zero_state))
    out_normed, back_pull = jax.vjp(
        back, head_x, b_proj, c_proj, step_size, decay_sum, head_params, gate_z, gate_full, state_in
    )
    out_lowered = out_normed.astype(jnp.bfloat16)
    branch = jnp.einsum("gti,id->gtd", out_lowered, out_full, preferred_element_type=jnp.float32)
    block_out = (inputs + branch).astype(jnp.bfloat16)
    out_grad_local = jnp.einsum(
        "gti,gtd->id", out_lowered, cotangent, preferred_element_type=jnp.float32
    )
    d_normed = jnp.einsum("gtd,id->gti", cotangent, out_full, preferred_element_type=jnp.float32)
    (
        d_head_x,
        d_b_proj,
        d_c_proj,
        d_step,
        d_decay_sum,
        d_head_back,
        d_gate_z,
        d_gate_gain,
        d_state_in,
    ) = back_pull(d_normed)
    later_decay, d_state_out = prefix(
        (decays, d_state_in), "seq", fold_pair, (unit_decay, zero_state)
    )
    d_decays = jnp.sum(d_state_out * state_in, axis=(2, 3))
    d_conv_in, d_previous, d_conv, d_step_raw, d_head_front = front_pull(
        (d_state_out, d_decays, d_head_x, d_b_proj, d_c_proj, d_step, d_decay_sum)
    )
    returned = from_behind(d_previous.astype(jnp.bfloat16), "seq", -1).astype(d_previous.dtype)
    d_conv_in = jnp.concatenate(
        [d_conv_in[:, :rim_start, :], d_conv_in[:, rim_start:, :] + returned], axis=1
    )
    d_projected = jnp.concatenate([d_gate_z, d_conv_in, d_step_raw], axis=-1).astype(jnp.bfloat16)
    in_grad_local = jnp.einsum(
        "gtd,gtp->dp", lowered, d_projected, preferred_element_type=jnp.float32
    )
    d_normed_in = jnp.einsum(
        "gtp,dp->gtd", d_projected, in_full, preferred_element_type=jnp.float32
    )
    d_inputs, norm_grad_local = norm_pull(d_normed_in)
    tokens_grad = cotangent.astype(jnp.float32) + d_inputs
    head_grad = lax.psum(d_head_back + d_head_front, ("dp", "seq"))
    in_grad, out_grad, conv_grad, norm_grad, gate_grad = (
        lax.psum_scatter(in_grad_local, ("dp", "seq"), scatter_dimension=0, tiled=True),
        lax.psum_scatter(out_grad_local, ("dp", "seq"), scatter_dimension=0, tiled=True),
        lax.psum_scatter(d_conv, ("dp", "seq"), scatter_dimension=1, tiled=True),
        lax.psum_scatter(norm_grad_local, ("dp", "seq"), scatter_dimension=0, tiled=True),
        lax.psum_scatter(d_gate_gain, ("dp", "seq"), scatter_dimension=0, tiled=True),
    )
    in_new, in_mom_new, in_var_new = adamw(in_proj, in_proj_mom, in_proj_var, in_grad, decay_rate)
    out_new, out_mom_new, out_var_new = adamw(
        out_proj, out_proj_mom, out_proj_var, out_grad, decay_rate
    )
    conv_new, conv_mom_new, conv_var_new = adamw(
        conv_params, conv_mom, conv_var, conv_grad, decay_rate
    )
    norm_new, norm_mom_new, norm_var_new = adamw(norm_gain, norm_mom, norm_var, norm_grad, 0.0)
    gate_new, gate_mom_new, gate_var_new = adamw(gate_gain, gate_mom, gate_var, gate_grad, 0.0)
    head_new, head_mom_new, head_var_new = adamw(head_params, head_mom, head_var, head_grad, 0.0)
    return (
        block_out,
        tokens_grad,
        in_grad,
        out_grad,
        conv_grad,
        norm_grad,
        gate_grad,
        head_grad,
        in_new,
        in_mom_new,
        in_var_new,
        out_new,
        out_mom_new,
        out_var_new,
        conv_new,
        conv_mom_new,
        conv_var_new,
        norm_new,
        norm_mom_new,
        norm_var_new,
        gate_new,
        gate_mom_new,
        gate_var_new,
        head_new,
        head_mom_new,
        head_var_new,
    )


class Place:
    def __init__(self):
        self.dp = dp = lax.axis_index("dp")
        self.z = lax.axis_index("seq")
        self.c = c = lax.rem(dp, 2)
        self.x = x = lax.rem(dp // 2, 2)
        self.y = y = dp // 4
        self.line = dp * 4 + self.z
        self.core_peer = {"dp": dp + 1 - 2 * c}
        self.x_peer = {"dp": dp + 2 - 4 * x}
        self.y_peer = {"dp": dp + 4 - 8 * y}

    def z_peer(self, k):
        return {"seq": lax.rem(self.z + k, 4)}

    def any_peer(self, k):
        at = lax.rem(self.line + k, 32)
        return {"dp": at // 4, "seq": lax.rem(at, 4)}

    def near(self):
        return (self.core_peer, self.x_peer, self.y_peer, self.z_peer(1), self.z_peer(2), self.z_peer(3))


def greet(peers):
    bar = pltpu.get_barrier_semaphore()
    for peer in peers:
        pl.semaphore_signal(bar, inc=1, device_id=peer, device_id_type=MESH)
    pl.semaphore_wait(bar, len(peers))


def send(src, dst, out_sem, in_sem, peer):
    return pltpu.make_async_remote_copy(
        src_ref=src, dst_ref=dst, send_sem=out_sem, recv_sem=in_sem, device_id=peer, device_id_type=MESH
    )


class Gather:
    def __init__(self, me, n, src, w, sems, skew):
        self.me, self.n, self.src, self.w, self.sk, self.slots = me, n, src, w, skew, skew + 1
        self.rows = src.shape[2]
        self.o1, self.o2, self.o3, self.o4, self.i1, self.i2, self.i3, self.i4 = sems

    @staticmethod
    def sems(n, skew):
        D = pltpu.SemaphoreType.DMA
        return [D((skew + 1, 3)), D((skew + 1, 2)), D((skew + 1, 2)), D((skew + 1,)), D((n, 3)), D((n, 2)), D((n, 2)), D((n,))]

    def c1(self, i, s, k):
        m, w = self.me, self.w
        rows = pl.ds(pl.multiple_of(m.z * self.rows, 16), self.rows)
        return send(self.src.at[i], w.at[i, :, m.y, m.x, m.c, rows], self.o1.at[s, k - 1], self.i1.at[i, k - 1], m.z_peer(k))

    def c2(self, i, s, h):
        m, w = self.me, self.w
        part = w.at[i, h, m.y, m.x, m.c]
        return send(part, part, self.o2.at[s, h], self.i2.at[i, h], (m.y_peer, m.x_peer)[h])

    def c3(self, i, s, h):
        m, w = self.me, self.w
        part = w.at[i, 0, :, m.x, m.c] if h == 0 else w.at[i, 1, m.y, :, m.c]
        return send(part, part, self.o3.at[s, h], self.i3.at[i, h], (m.x_peer, m.y_peer)[h])

    def c4(self, i, s):
        m, w = self.me, self.w
        part = w.at[i, :, :, :, m.c]
        return send(part, part, self.o4.at[s], self.i4.at[i], m.core_peer)

    def step(self, it):
        n, sk, ns = self.n, self.sk, self.slots

        def stage(lag, body):
            @pl.when((it >= lag * sk) & (it < n + lag * sk))
            def _():
                i = it - lag * sk
                body(i, lax.rem(i, ns))

        def first(i, s):
            m = self.me
            @pl.when(i >= ns)
            def _():
                for k in (1, 2, 3): self.c1(i, s, k).wait_send()
            for k in (2, 1, 3): self.c1(i, s, k).start()
            rows = pl.ds(pl.multiple_of(m.z * self.rows, 16), self.rows)
            for h in range(2):
                self.w[i, h, m.y, m.x, m.c, rows] = self.src[i, h]

        def second(i, s):
            @pl.when(i >= ns)
            def _():
                for h in range(2): self.c2(i, s, h).wait_send()
            for k in (1, 2, 3): self.c1(i, s, k).wait_recv()
            for h in range(2): self.c2(i, s, h).start()

        def third(i, s):
            @pl.when(i >= ns)
            def _():
                for h in range(2): self.c3(i, s, h).wait_send()
            for h in range(2):
                self.c2(i, s, h).wait_recv()
                self.c3(i, s, h).start()

        def fourth(i, s):
            @pl.when(i >= ns)
            def _(): self.c4(i, s).wait_send()
            for h in range(2): self.c3(i, s, h).wait_recv()
            self.c4(i, s).start()

        stage(0, first); stage(1, second); stage(2, third); stage(3, fourth)

    def arrived(self, i):
        self.c4(i, 0).wait_recv()

    def finish(self):
        for j in range(self.slots):
            i = self.n - self.slots + j
            s = i % self.slots
            for k in (1, 2, 3): self.c1(i, s, k).wait_send()
            for h in range(2):
                self.c2(i, s, h).wait_send()
                self.c3(i, s, h).wait_send()
            self.c4(i, s).wait_send()


def windows(width, count):
    return [(o * width // 128) * 128 for o in range(count)]


def gather_call(src_in, src_out, small, tokens, edge, cotangent, collective_id, skew=2):
    NI, NO = src_in.shape[0], src_out.shape[0]
    T, DM = tokens.shape
    TE = T + 16
    DIN = 2 * 16 * 96

    def kernel(src_in, src_out, small_ref, tok_ref, edge_ref, cot_ref,
               proj_hbm, win_hbm, wout_hbm, low_ref, par_ref, dn_ref,
               win, wout, sm, low_e, edge_in, pbuf,
               *sems):
        gs, os_, (sm_out, sm_in, ed_out, ed_in, pb_sem, wi_sem, wo_sem) = sems[:8], sems[8:16], sems[16:]
        me = Place()
        bar = pltpu.get_barrier_semaphore()
        def sig(k, _):
            pl.semaphore_signal(bar, inc=1, device_id=me.any_peer(k), device_id_type=MESH)
            return 0
        lax.fori_loop(1, 32, sig, 0)
        pl.semaphore_wait(bar, 31)
        ga = Gather(me, NI, src_in, win, gs, skew)
        gb = Gather(me, NO, src_out, wout, os_, skew)

        def small_copy(k):
            return send(small_ref, sm.at[me.line], sm_out.at[k - 1], sm_in.at[k - 1], me.any_peer(k))
        def edge_copy():
            return send(edge_ref, edge_in, ed_out, ed_in, {"seq": lax.rem(me.z + 1, 4)})
        lax.fori_loop(1, 32, lambda k, _: (small_copy(k).start(), 0)[1], 0)
        edge_copy().start()
        sm[me.line] = small_ref[...]
        ga.step(0); ga.step(1)
        lax.fori_loop(1, 32, lambda k, _: (small_copy(k).wait(), 0)[1], 0)
        edge_copy().wait()
        par_ref[...] = jnp.zeros_like(par_ref)
        for o in range(32):
            for base, width, row, lo in ((0, 104, 5, 0), (3328, 48, 1, 5), (4864, 96, 1, 6)):
                at = base + (o * width // 128) * 128
                wd = min(256, {0: 3328, 3328: 4864, 4864: 7936}[base] - at)
                par_ref[:, at:at + wd] += sm[o][:, :wd]
        gain = par_ref[5:6, 3328:4864]
        keep = (me.z > 0).astype(f32)

        def norm(v):
            v = v.astype(f32)
            return (v * lax.rsqrt(jnp.mean(v * v, axis=-1, keepdims=True) + 1e-5) * gain).astype(bf)
        def nloop(t, _):
            r = pl.ds(pl.multiple_of(t * 64, 64), 64)
            v = norm(tok_ref[r])
            low_ref[r] = v
            low_e[r] = v
            return 0
        lax.fori_loop(0, T // 64, nloop, 0)
        low_e[T:] = norm(edge_in[...].astype(f32) * keep)

        def pcopy(i, s): return pltpu.make_async_copy(pbuf.at[s], proj_hbm.at[i], pb_sem.at[s])
        def wicopy(i): return pltpu.make_async_copy(win.at[i], win_hbm.at[i], wi_sem.at[i])
        def wocopy(i): return pltpu.make_async_copy(wout.at[i], wout_hbm.at[i], wo_sem.at[i])

        def loop(it, _):
            @pl.when(it >= 2)
            def _(): ga.step(it)
            gb.step(it - NI)
            @pl.when((it >= 4 * skew) & (it < NI + 4 * skew))
            def _():
                i = it - 4 * skew; s = lax.rem(i, 2)
                ga.arrived(i)
                wicopy(i).start()
                @pl.when(i >= 2)
                def _(): pcopy(i - 2, s).wait()
                w = jnp.concatenate([win[i, h].reshape(DM, 128) for h in range(2)], axis=1)
                pbuf[s] = jnp.dot(low_e[...], w, preferred_element_type=f32)
                pcopy(i, s).start()
            @pl.when(it >= NI + 4 * skew)
            def _():
                i = it - 4 * skew - NI
                gb.arrived(i)
                wocopy(i).start()
                for h in range(2):
                    a = cot_ref[:, pl.ds(pl.multiple_of(i * 256 + h * 128, 128), 128)]
                    def cols(q, _):
                        y = q // 4; x = lax.rem(q // 2, 2); c = lax.rem(q, 2)
                        r = lax.dot_general(a, wout[i, h, y, x, c], (((1,), (1,)), ((), ())), preferred_element_type=f32)
                        for t in range(3):
                            rt = r[:, 128 * t:128 * t + 128]
                            if h == 0:
                                @pl.when(i == 0)
                                def _(): dn_ref[3 * q + t] = rt
                                @pl.when(i > 0)
                                def _(): dn_ref[3 * q + t] += rt
                            else:
                                dn_ref[3 * q + t] += rt
                        return 0
                    lax.fori_loop(0, 8, cols, 0)
            return 0
        lax.fori_loop(0, NI + NO + 4 * skew, loop, 0)
        pcopy(NI - 2, NI % 2).wait()
        pcopy(NI - 1, (NI - 1) % 2).wait()
        lax.fori_loop(0, NI, lambda i, _: (wicopy(i).wait(), 0)[1], 0)
        lax.fori_loop(0, NO, lambda i, _: (wocopy(i).wait(), 0)[1], 0)
        ga.finish()
        gb.finish()

    V, D = pltpu.VMEM, pltpu.SemaphoreType.DMA
    S = jax.ShapeDtypeStruct
    vm, hb = pl.BlockSpec(memory_space=pltpu.VMEM), pl.BlockSpec(memory_space=pl.ANY)
    wi, wo = (NI, 2, 2, 2, 2, 192, 128), (NO, 2, 2, 2, 2, 384, 128)
    return pl.pallas_call(
        kernel,
        out_shape=(S((NI, TE, 256), f32), S(wi, bf), S(wo, bf), S((T, DM), bf), S((8, 7936), f32), S((24, T, 128), f32)),
        in_specs=[vm] * 6,
        out_specs=(hb, hb, hb, vm, vm, vm),
        scratch_shapes=[V(wi, bf), V(wo, bf), V((32, 8, 256), f32), V((TE, DM), bf), V((16, DM), bf), V((2, TE, 256), f32)]
        + Gather.sems(NI, skew) + Gather.sems(NO, skew)
        + [D((31,)), D((31,)), D, D, D((2,)), D((NI,)), D((NO,))],
        compiler_params=pltpu.CompilerParams(collective_id=collective_id, has_side_effects=True, vmem_limit_bytes=63 << 20),
        name="gather",
    )(src_in, src_out, small, tokens, edge, cotangent)


def arrange(in_proj, out_proj, conv_params, norm_gain, gate_gain, line):
    w = in_proj.astype(bf)
    w = jnp.concatenate([w[:, 3072:], jnp.zeros((48, 208), bf), w[:, :3072]], axis=1)
    src_in = w.reshape(48, 26, 2, 128).transpose(1, 2, 0, 3)
    src_out = out_proj.astype(bf).reshape(96, 6, 2, 128).transpose(1, 2, 0, 3)
    small = jnp.zeros((8, 256), f32)
    for rows, row, width in ((conv_params, 0, 104), (norm_gain[None], 5, 48), (gate_gain[None], 6, 96)):
        small = lax.dynamic_update_slice(small, rows, (row, lax.rem(line * width, 128)))
    return src_in, src_out, small


TILES = 12
NN, NT, TN_ = (((1,), (0,)), ((), ())), (((1,), (1,)), ((), ())), (((0,), (0,)), ((), ()))


def one(a, b, dims):
    return lax.dot_general(a, b, dims, preferred_element_type=f32)


def halves(a):
    hi = a.astype(bf)
    return hi, (a - hi.astype(f32)).astype(bf)


def cross(a, b, dims=NN):
    (ah, al), (bh, bl) = (v if isinstance(v, tuple) else (v, None) for v in (a, b))
    out = one(ah, bh, dims)
    if bl is not None:
        out = out + one(ah, bl, dims)
    if al is not None:
        out = out + one(al, bh, dims)
    return out


def mul(a, b, dims=NN):
    return cross(*(v if isinstance(v, tuple) or v.dtype == bf else halves(v) for v in (a, b)), dims)


def mul_exact(a, b, dims=NN, left=True):
    v = b if left else a
    h = v.astype(bf)
    r = v - h.astype(f32)
    m = r.astype(bf)
    l = (r - m.astype(f32)).astype(bf)
    if left:
        a = a.astype(bf)
        return one(a, h, dims) + (one(a, m, dims) + one(a, l, dims))
    b = b.astype(bf)
    return one(h, b, dims) + (one(m, b, dims) + one(l, b, dims))


def to_heads(a, spot):
    return cross(halves(a), spot)


def rolled(a, j):
    return pltpu.roll(a, lax.rem(128 - 4 * j, 128), 1)


def spread(r):
    lane = lax.broadcasted_iota(jnp.int32, (r.shape[0], 128), 1)
    return jnp.concatenate([jnp.where(lane < 64, r[:, h:h + 1], r[:, h + 1:h + 2]) for h in (0, 2)], 1)


def by_head(v):
    lane = lax.broadcasted_iota(jnp.int32, v.shape, 1)
    zero = jnp.zeros_like(v)
    return jnp.concatenate([jnp.where(lane < 64, v, zero), jnp.where(lane >= 64, v, zero)], 0)


def heads_apart(pair):
    return tuple(by_head(v.astype(f32)).astype(bf) for v in pair)


def part_of(pair, *index):
    return tuple(v[index] for v in pair)


def spot_of(j):
    p = lax.broadcasted_iota(jnp.int32, (256, 128), 0)
    lane = lax.broadcasted_iota(jnp.int32, (256, 128), 1)
    return (lane == 4 * j + p // 64).astype(bf)


def fill_pad(pad, cin, halo):
    for g in range(2):
        pad[g, 5:8] = halo[8 * g:8 * g + 3]
        pad[g, 8:264] = cin[256 * g:256 * g + 256]


def conv(pad, taps):
    out = []
    for g in range(2):
        acc = taps[4:5]
        for k in range(4):
            acc = acc + taps[k:k + 1] * pad[g, 5 + k:261 + k]
        out.append(acc)
    return out


def sig(v):
    return 1.0 / (1.0 + jnp.exp(-v))


def causal(flip):
    r = lax.broadcasted_iota(jnp.int32, (128, 128), 0)
    c = lax.broadcasted_iota(jnp.int32, (128, 128), 1)
    return (r <= c) if flip else (c <= r)


class Chain:
    def __init__(self, me, by, got, part, out, out_sem, in_sem, keep, lag):
        self.lag = lag
        self.me, self.by, self.got, self.part, self.out, self.out_sem, self.in_sem, self.keep = me, by, got, part, out, out_sem, in_sem, keep
        self.place = me.z if by == 1 else 3 - me.z

    def copy(self, i):
        s = lax.rem(i, 3)
        return send(self.out.at[s], self.got.at[i], self.out_sem.at[s], self.in_sem.at[i], self.me.z_peer(1 if self.by == 1 else 3))

    def tile(self, i):
        @pl.when(self.place > 0)
        def _(): self.copy(i).wait_recv()

        @pl.when(self.place < 3)
        def _():
            @pl.when(i >= 3)
            def _(): self.copy(i - 3).wait_send()
            s = lax.rem(i, 3)
            for g in range(2):
                self.out[s, g] = (self.keep(i, g) * self.got[i, g].astype(f32) + self.part[i, g]).astype(bf)
            self.copy(i).start()

    def start(self):
        @pl.when(self.place == 0)
        def _(): self.got[...] = jnp.zeros_like(self.got)

    def step(self, j, drain):
        lag = self.lag * self.place
        @pl.when((j >= lag) & (j < TILES + lag))
        def _(): self.tile(j - lag)

        if drain:
            @pl.when(j == TILES - 1)
            def _():
                lax.fori_loop(TILES - lag, TILES, lambda i, _: (self.tile(i), 0)[1], 0)

    def finish(self):
        @pl.when(self.place < 3)
        def _():
            for i in range(TILES - 3, TILES): self.copy(i).wait_send()

    @staticmethod
    def scratch():
        D = pltpu.SemaphoreType.DMA
        return [V((TILES, 2, 128, 256), bf), V((TILES, 2, 128, 256), f32), V((3, 2, 128, 256), bf), D((3,)), D((TILES,))]


def keeper(ds):
    def keep(i, g):
        end = 256 * g + 248
        return jnp.exp(spread(rolled(ds[end:end + 8], i))[7:8])
    return keep


V = pltpu.VMEM


def sf1_body(j, cin, halo, bcin, bchalo, raw, taps, bctaps, hp, x_o, yi_o, ent_o, step_o, ds_o, dst_o, b_o, c_o, pad, pad2, s_s, bt_s, got, part, out, out_sem, in_sem):
    me = Place()
    line = Chain(me, 1, got, part, out, out_sem, in_sem, keeper(ds_o), 1)
    @pl.when(j == 0)
    def _():
        greet((me.z_peer(1), me.z_peer(3)))
        line.start()
        pre = raw[0] + hp[2:3]
        step = jnp.maximum(pre, 0.0) + jnp.log1p(jnp.exp(-jnp.abs(pre)))
        rate = step * -jnp.exp(hp[0:1])
        step_o[...] = step
        r = lax.broadcasted_iota(jnp.int32, (256, 256), 0)
        c = lax.broadcasted_iota(jnp.int32, (256, 256), 1)
        low = (c <= r).astype(bf)
        for g in range(2):
            ds_o[256 * g:256 * g + 256] = mul_exact(low, rate[256 * g:256 * g + 256])
        turned = ds_o[...].T
        for p in range(TILES):
            dst_o[p, 0:4] = turned[4 * p:4 * p + 4]
        fill_pad(pad2, bcin[0], bchalo[0])
        for g, co in enumerate(conv(pad2, bctaps)):
            act = co * sig(co)
            b, c = act[:, :128], act[:, 128:]
            b_o[256 * g:256 * g + 256] = b
            c_o[256 * g:256 * g + 256] = c
            bt_s[g] = b.T
            s_s[g, 0] = mul(c[:128], b[:128], NT)
            s_s[g, 1] = mul(c[128:], b[128:], NT)
            s_s[g, 2] = mul(c[128:], b[:128], NT)

    fill_pad(pad, cin[0], halo[0])
    rds = rolled(ds_o[...], j)
    dsc = spread(rds)
    stc = spread(rolled(step_o[...], j))
    ok = causal(False)
    for g, co in enumerate(conv(pad, taps)):
        b0 = 256 * g
        x = co * sig(co)
        x_o[b0:b0 + 256] = x
        xs = x * stc[b0:b0 + 256]
        xp = halves(xs)
        d = dsc[b0:b0 + 256]
        ys = []
        for q in range(2):
            b = b0 + 128 * q
            y = []
            for m in range(2):
                w = []
                for h in (2 * m, 2 * m + 1):
                    gap = rds[b:b + 128, h:h + 1] - dst_o[j, h:h + 1, b:b + 128]
                    w.append(s_s[g, q] * jnp.exp(jnp.where(ok, gap, -1e30)))
                y.append(mul(jnp.concatenate(w, 1), heads_apart(part_of(xp, slice(128 * q, 128 * q + 128), slice(128 * m, 128 * m + 128)))))
            ys.append(jnp.concatenate(y, 1))
        mid = d[127:128]
        ys[1] = ys[1] + jnp.exp(d[128:] - mid) * mul(s_s[g, 2], jnp.exp(mid - d[:128]) * xs[:128])
        yi_o[b0:b0 + 128] = ys[0]
        yi_o[b0 + 128:b0 + 256] = ys[1]
        part[j, g] = mul(bt_s[g], jnp.exp(d[255:256] - d) * xs)
    line.step(j, True)

    @pl.when(j == TILES - 1)
    def _():
        line.finish()
        ent_o[...] = got[...]


def sf2_body(j, yi, x, ent, z, dn, gain, ds, c_r, hp, mixed_o, rq_o, a1, a2):
    @pl.when(j == 0)
    def _():
        a1[...] = jnp.zeros_like(a1)
        a2[...] = jnp.zeros_like(a2)
    dsc = spread(rolled(ds[...], j))
    skip = spread(rolled(hp[...], j))[1:2]
    for g in range(2):
        r = slice(256 * g, 256 * g + 256)
        car = jnp.exp(dsc[r]) * mul(c_r[r], ent[0, g])
        mixed = yi[r] + car + skip * x[r]
        mixed_o[r] = mixed
        zz = z[0, r]
        gated = mixed * (zz * sig(zz))
        a1[r] += gated * gated
        a2[r] += gain[6:7] * jnp.concatenate([dn[0, r], dn[1, r]], 1) * gated

    @pl.when(j == TILES - 1)
    def _():
        r = lax.rsqrt(jnp.sum(a1[...], axis=1, keepdims=True) * (1.0 / 3072) + 1e-5)
        k = r * r * r * (jnp.sum(a2[...], axis=1, keepdims=True) * (1.0 / 3072))
        rq_o[0] = jnp.broadcast_to(r, (512, 128))
        rq_o[1] = jnp.broadcast_to(k, (512, 128))


def sb1_start(b_r, c_r, dst_acc, dc_acc, dds_acc, xu_acc, st_s, ct_s):
    for a in (dst_acc, dc_acc, dds_acc, xu_acc):
        a[...] = jnp.zeros_like(a)
    for g in range(2):
        b, c = b_r[256 * g:256 * g + 256], c_r[256 * g:256 * g + 256]
        st_s[g, 0] = mul(b[:128], c[:128], NT)
        st_s[g, 1] = mul(b[128:], c[128:], NT)
        st_s[g, 2] = mul(b[:128], c[128:], NT)
        ct_s[g] = c.T


def sb1_tile(j, mixed, z, dn, x, ent, gain, ds, step, dst, hp, rq, dxa_s, dz_o, dz_s, ol_o, lhs_s, rows_o,
             dst_acc, dc_acc, dds_acc, xu_acc, st_s, ct_s, part):
    rds = rolled(ds[...], j)
    dsc = spread(rds)
    stc = spread(rolled(step[...], j))
    skip = spread(rolled(hp[...], j))[1:2]
    ok = causal(True)
    spot = spot_of(j)
    dgain = jnp.zeros((1, 256), f32)
    turned = []
    dskip = jnp.zeros((1, 256), f32)
    for g in range(2):
        r = slice(256 * g, 256 * g + 256)
        zz, mx, xx = z[0, r], mixed[r], x[r]
        dnr = jnp.concatenate([dn[0, r], dn[1, r]], 1)
        s = sig(zz)
        sil = zz * s
        gated = mx * sil
        rr, kk = (jnp.concatenate([rq[k, r]] * 2, 1) for k in (0, 1))
        gr = gated * rr
        ol = gr * gain[6:7]
        ol_o[r] = ol.astype(bf)
        turned.append(ol.T.astype(bf))
        dgain += jnp.sum(dnr * gr, axis=0, keepdims=True)
        dg = rr * (gain[6:7] * dnr) - gated * kk
        dy = dg * sil
        dz = (dg * mx * (s * (1.0 + zz * (1.0 - s)))).astype(bf)
        dz_o[0, r] = dz
        dz_s[r] = dz
        dskip += jnp.sum(dy * xx, axis=0, keepdims=True)
        d = dsc[r]
        eu = halves(jnp.exp(d) * dy)
        part[j, g] = mul(ct_s[g], eu)
        dc_acc[r] += mul(eu, ent[j, g], NT)
        dds_acc[r] += to_heads(dy * (mx - skip * xx), spot)
        xs = xx * stc[r]
        dp, xp = halves(dy), halves(xs)
        us = []
        for q in range(2):
            b = 256 * g + 128 * q
            lo = slice(128 * q, 128 * q + 128)
            u, acc = [], 0.0
            for m in range(2):
                e = []
                for h in (2 * m, 2 * m + 1):
                    gap = dst[j, h:h + 1, b:b + 128] - rds[b:b + 128, h:h + 1]
                    e.append(jnp.exp(jnp.where(ok, gap, -1e30)))
                w = jnp.concatenate([st_s[g, q] * e[0], st_s[g, q] * e[1]], 1)
                cols = slice(128 * m, 128 * m + 128)
                dh = heads_apart(part_of(dp, lo, cols))
                u.append(mul(w, dh))
                gt = mul(part_of(xp, lo, cols), dh, NT)
                acc = acc + (gt[:, :128] * e[0] + gt[:, 128:] * e[1])
            dst_acc[g, q] += acc
            us.append(jnp.concatenate(u, 1))
        mid = d[127:128]
        v = jnp.exp(mid - d[:128])
        ud = halves(jnp.exp(d[128:] - mid) * dy[128:])
        us[0] = us[0] + v * mul(st_s[g, 2], ud)
        dst_acc[g, 2] += mul(v * xs[:128], ud, NT)
        u = jnp.concatenate(us, 0)
        xu_acc[r] += to_heads(xx * u, spot)
        dxa_s[j, r] = skip * dy + stc[r] * u
    rows_o[j, 0:1] = dgain
    rows_o[j, 1:2] = dskip
    rows_o[j, 2:8] = jnp.zeros((6, 256), f32)
    turned = jnp.concatenate(turned, 1)
    for k in range(16):
        at = 16 * j + k
        q = at // 3
        owner, sub = q // 2, lax.rem(q, 2)
        rows = pl.ds(pl.multiple_of(lax.rem(at, 3) * 16, 16), 16)
        lhs_s[1 + sub, owner // 8, lax.rem(owner // 4, 2), lax.rem(owner, 4), rows] = turned[16 * k:16 * k + 16]


def conv_back(pad, dpad, dco, taps):
    w = taps.shape[1]
    grads = []
    for k in range(4):
        grads.append(sum(jnp.sum(dco[g] * pad[g, 5 + k:261 + k], axis=0, keepdims=True) for g in range(2)))
    grads.append(sum(jnp.sum(dco[g], axis=0, keepdims=True) for g in range(2)))
    grads.append(jnp.zeros((3, w), f32))
    din, prev = [], []
    for g in range(2):
        dpad[g, 0:8] = jnp.zeros((8, w), f32)
        dpad[g, 8:264] = dco[g]
        dpad[g, 264:272] = jnp.zeros((8, w), f32)
        din.append(sum(taps[k:k + 1] * dpad[g, 11 - k:267 - k] for k in range(4)))
        prev.append(sum(taps[k:k + 1] * dpad[g, 3 - k:11 - k] for k in range(4)))
    return jnp.concatenate(grads, 0), din, prev


def sb2_make(me, dcp_o, cg_o, hg_o, pad, pad2, dpad, dpad2, db_s, xut_s, de_s, prv, lst, edge_in, e_out, e_in):
    def edge(i):
        return send(prv.at[i], edge_in.at[i], e_out.at[i], e_in.at[i], me.z_peer(3))

    def pass_edge(i, prev, din):
        for g in range(2):
            lst[i, 8 * g:8 * g + 8] = din[g][248:]
        prv[i] = jnp.concatenate(prev, 0).astype(bf)

        @pl.when(me.z > 0)
        def _(): edge(i).start()

    def start():
        for a in (db_s, xut_s, de_s):
            a[...] = jnp.zeros_like(a)

    def tile(j, dxa_s, x, cin, halo, taps, got, ent, ds, step, b_r):
        dsc = spread(rolled(ds[...], j))
        stc = spread(rolled(step[...], j))
        spot = spot_of(j)
        fill_pad(pad, cin[0], halo[0])
        dco = []
        for g, co in enumerate(conv(pad, taps)):
            r = slice(256 * g, 256 * g + 256)
            d, xx, st, e = dsc[r], x[r], got[j, g], ent[j, g]
            tail = jnp.exp(d[255:256] - d)
            ut = tail * mul(b_r[r], st)
            xut_s[r] += to_heads(xx * ut, spot)
            db_s[r] += mul(tail * stc[r] * xx, st, NT)
            row = jnp.sum(st.astype(f32) * e.astype(f32), axis=0, keepdims=True)
            de_s[g] += to_heads(jnp.broadcast_to(row, (8, 256)), spot)
            dx = dxa_s[j, r] + stc[r] * ut
            s = sig(co)
            dco.append(dx * (s * (1.0 + co * (1.0 - s))))
        grads, din, prev = conv_back(pad, dpad, dco, taps)
        cg_o[j] = grads
        for g in range(2):
            dcp_o[j, 256 * g:256 * g + 256] = din[g].astype(bf)
        pass_edge(j, prev, din)

    def final(bcin, bchalo, bctaps, raw, ds, step, b_r, c_r, hp, dst_acc, dc_acc, dds_acc, xu_acc):
        fill_pad(pad2, bcin[0], bchalo[0])
        dco2 = []
        for g, co in enumerate(conv(pad2, bctaps)):
            r0 = 256 * g
            b, c = b_r[r0:r0 + 256], c_r[r0:r0 + 256]
            db, dc = db_s[r0:r0 + 256], dc_acc[r0:r0 + 256]
            db = db + jnp.concatenate([mul(dst_acc[g, 0], c[:128]) + mul(dst_acc[g, 2], c[128:]), mul(dst_acc[g, 1], c[128:])], 0)
            dc = dc + jnp.concatenate([mul(dst_acc[g, 0].T, b[:128]), mul(dst_acc[g, 1].T, b[128:]) + mul(dst_acc[g, 2].T, b[:128])], 0)
            s = sig(co)
            dco2.append(jnp.concatenate([db, dc], 1) * (s * (1.0 + co * (1.0 - s))))
        grads, din, prev = conv_back(pad2, dpad2, dco2, bctaps)
        cg_o[12] = grads
        for g in range(2):
            dcp_o[12, 256 * g:256 * g + 256] = din[g].astype(bf)
        pass_edge(TILES, prev, din)
        st = step[...]
        xut = xut_s[...]
        speed = -jnp.exp(hp[0:1])
        dds = dds_acc[...] - st * (xu_acc[...] + xut)
        lane = lax.broadcasted_iota(jnp.int32, (512, 128), 1)
        tok = lax.broadcasted_iota(jnp.int32, (256, 128), 0)
        rr = lax.broadcasted_iota(jnp.int32, (256, 256), 0)
        cc = lax.broadcasted_iota(jnp.int32, (256, 256), 1)
        up = (cc >= rr).astype(bf)
        drate = []
        for g in range(2):
            r = slice(256 * g, 256 * g + 256)
            end = jnp.sum(st[r] * xut[r], axis=0, keepdims=True) + de_s[g][0:1] * jnp.exp(ds[256 * g + 255:256 * g + 256])
            drate.append(mul_exact(up, dds[r] + jnp.where(tok == 255, end, 0.0)))
        drate = jnp.concatenate(drate, 0)
        dstep = xu_acc[...] + xut + drate * speed
        draw = jnp.where(lane < 48, dstep * sig(raw[0] + hp[2:3]), 0.0)
        dcp_o[13, :, 0:128] = draw.astype(bf)
        dcp_o[13, :, 128:256] = jnp.zeros((512, 128), bf)
        hg_o[0:1] = jnp.sum(drate * st * speed, axis=0, keepdims=True)
        hg_o[1:2] = jnp.zeros((1, 128), f32)
        hg_o[2:3] = jnp.sum(draw, axis=0, keepdims=True)
        hg_o[3:8] = jnp.zeros((5, 128), f32)

        @pl.when(me.z < 3)
        def _():
            def patch(i, _):
                edge(i).wait_recv()
                for g in range(2):
                    rows = lst[i, 8 * g:8 * g + 8] + edge_in[i, 8 * g:8 * g + 8].astype(f32)
                    dcp_o[i, 256 * g + 248:256 * g + 256] = rows.astype(bf)
                return 0
            lax.fori_loop(0, TILES + 1, patch, 0)

        @pl.when(me.z > 0)
        def _(): lax.fori_loop(0, TILES + 1, lambda i, _: (edge(i).wait_send(), 0)[1], 0)

    return start, tile, final


S = jax.ShapeDtypeStruct
V = pltpu.VMEM


def const(*shape):
    return pl.BlockSpec(shape, lambda j: (0,) * len(shape), pipeline_mode=pl.Buffered(1))


TILE = pl.BlockSpec((1, 512, 256), lambda j: (j, 0, 0))
HALO = pl.BlockSpec((1, 16, 256), lambda j: (j, 32, 0))
ZT = pl.BlockSpec((1, 512, 256), lambda j: (14 + j, 0, 0))
BC = pl.BlockSpec((1, 512, 256), lambda j: (12, 0, 0), pipeline_mode=pl.Buffered(1))
BCH = pl.BlockSpec((1, 16, 256), lambda j: (12, 32, 0), pipeline_mode=pl.Buffered(1))
RAW = pl.BlockSpec((1, 512, 128), lambda j: (13, 0, 0), pipeline_mode=pl.Buffered(1))
TAP = pl.BlockSpec((8, 256), lambda j: (0, j))
BCT = pl.BlockSpec((8, 256), lambda j: (0, 12), pipeline_mode=pl.Buffered(1))
GAIN = pl.BlockSpec((8, 256), lambda j: (0, 19 + j))
HP = const(8, 128)
COL = pl.BlockSpec((512, 256), lambda j: (0, j))
ST = pl.BlockSpec((1, 2, 128, 256), lambda j: (j, 0, 0, 0))
DN = pl.BlockSpec((2, 512, 128), lambda j: (j, 0, 0))
TOK = const(512, 128)
TOKT = const(12, 8, 512)


def call(body, name, in_specs, out_shape, out_specs, scratch, args, cid=None):
    def kernel(*refs):
        body(pl.program_id(0), *refs)
    return pl.pallas_call(
        kernel, grid=(TILES,), in_specs=in_specs, out_specs=out_specs, out_shape=out_shape, scratch_shapes=scratch,
        compiler_params=pltpu.CompilerParams(vmem_limit_bytes=60 << 20, collective_id=cid, has_side_effects=cid is not None), name=name,
    )(*args)


def sf1(proj, par, hp):
    return call(sf1_body, "sf1", [TILE, HALO, BC, BCH, RAW, TAP, BCT, HP],
        (S((512, 3072), f32), S((512, 3072), f32), S((12, 2, 128, 256), bf), S((512, 128), f32), S((512, 128), f32), S((12, 8, 512), f32), S((512, 128), f32), S((512, 128), f32)),
        (COL, COL, const(12, 2, 128, 256), TOK, TOK, TOKT, TOK, TOK),
        [V((2, 264, 256), f32), V((2, 264, 256), f32), V((2, 3, 128, 128), f32), V((2, 128, 256), f32)] + Chain.scratch(),
        (proj, proj, proj, proj, proj, par, par, hp), 4)


def sf2(yi, x, ent, proj, dn, par, ds, c, hp):
    return call(sf2_body, "sf2", [COL, COL, ST, ZT, DN, GAIN, TOK, TOK, HP],
        (S((512, 3072), f32), S((2, 512, 128), f32)), (COL, const(2, 512, 128)),
        [V((512, 256), f32), V((512, 256), f32)],
        (yi, x, ent, proj, dn, par, ds, c, hp))


class Reduce:
    def __init__(self, me, n, rows, refs, skew):
        self.me, self.n, self.rows, self.sk, self.slots, self.ring = me, n, rows, skew, skew + 1, skew + 2
        (self.own0, self.own1, self.own2, self.own3, self.s0, self.s1, self.s2, self.s3, self.r0, self.r1, self.r2, self.r3,
         self.o0, self.o1, self.o2, self.o3, self.i0, self.i1, self.i2, self.i3, self.free) = refs

    @staticmethod
    def scratch(n, rows, skew):
        V, D, k = pltpu.VMEM, pltpu.SemaphoreType.DMA, skew + 1
        z = 4 * rows
        return [V((k, 2, 2, 2, z, 128), f32), V((k, 2, 2, z, 128), f32), V((k, 2, z, 128), f32), V((k, 2, rows, 128), f32),
                V((k, 2, 2, 2, z, 128), f32), V((k, 2, 2, z, 128), bf), V((k, 2, z, 128), bf), V((k, 3, 2, rows, 128), bf),
                V((skew + 2, 2, 2, 2, z, 128), f32), V((n, 2, 2, z, 128), bf), V((n, 2, z, 128), bf), V((n, 3, 2, rows, 128), bf),
                D((k,)), D((k, 2)), D((k, 2)), D((k, 3)), D((n,)), D((n, 2)), D((n, 2)), D((n, 3)), pltpu.SemaphoreType.REGULAR]

    def c0(self, i, s):
        return send(self.s0.at[s], self.r0.at[lax.rem(i, self.ring)], self.o0.at[s], self.i0.at[i], self.me.core_peer)

    def c1(self, i, s, h):
        return send(self.s1.at[s, h], self.r1.at[i, h], self.o1.at[s, h], self.i1.at[i, h], (self.me.x_peer, self.me.y_peer)[h])

    def c2(self, i, s, h):
        return send(self.s2.at[s, h], self.r2.at[i, h], self.o2.at[s, h], self.i2.at[i, h], (self.me.y_peer, self.me.x_peer)[h])

    def c3(self, i, s, k):
        return send(self.s3.at[s, k - 1], self.r3.at[i, k - 1], self.o3.at[s, k - 1], self.i3.at[i, k - 1], self.me.z_peer(k))

    def step(self, it, product, out_ref):
        n, sk, ns, R = self.n, self.sk, self.slots, self.rows
        me, x, y, z, c = self.me, self.me.x, self.me.y, self.me.z, self.me.c

        def stage(lag, body):
            @pl.when((it >= lag * sk) & (it < n + lag * sk))
            def _():
                i = it - lag * sk
                body(i, lax.rem(i, ns))

        def zero(i, s):
            @pl.when(i >= ns)
            def _(): self.c0(i, s).wait_send()
            part = product(i, 1 - c)
            for h in range(2):
                self.s0[s, h] = part[..., h * 128:(h + 1) * 128]
            @pl.when(i >= self.ring)
            def _(): pl.semaphore_wait(self.free, 1)
            self.c0(i, s).start()
            part = product(i, c)
            for h in range(2):
                self.own0[s, h] = part[..., h * 128:(h + 1) * 128]

        def first(i, s):
            own0, r0, own1 = self.own0, self.r0, self.own1
            q = lax.rem(i, self.ring)
            @pl.when(i >= ns)
            def _():
                for h in range(2): self.c1(i, s, h).wait_send()
            self.c0(i, s).wait_recv()
            for a in range(2):
                self.s1[s, 0, a] = (own0[s, 0, a, 1 - x] + r0[q, 0, a, 1 - x]).astype(bf)
            self.c1(i, s, 0).start()
            self.s1[s, 1] = (own0[s, 1, 1 - y] + r0[q, 1, 1 - y]).astype(bf)
            self.c1(i, s, 1).start()
            for a in range(2):
                own1[s, 0, a] = own0[s, 0, a, x] + r0[q, 0, a, x]
            own1[s, 1] = own0[s, 1, y] + r0[q, 1, y]
            pl.semaphore_signal(self.free, inc=1, device_id=me.core_peer, device_id_type=MESH)

        def second(i, s):
            own1, r1 = self.own1, self.r1
            @pl.when(i >= ns)
            def _():
                for h in range(2): self.c2(i, s, h).wait_send()
            for h, g in ((0, y), (1, x)):
                self.c1(i, s, h).wait_recv()
                self.s2[s, h] = (own1[s, h, 1 - g] + r1[i, h, 1 - g].astype(f32)).astype(bf)
                self.c2(i, s, h).start()
                self.own2[s, h] = own1[s, h, g] + r1[i, h, g].astype(f32)

        def third(i, s):
            own2, r2 = self.own2, self.r2
            @pl.when(i >= ns)
            def _():
                for k in (1, 2, 3): self.c3(i, s, k).wait_send()
            for h in range(2): self.c2(i, s, h).wait_recv()
            for k in (2, 1, 3):
                rows = pl.ds(pl.multiple_of(lax.rem(z + k, 4) * R, 16), R)
                for h in range(2):
                    self.s3[s, k - 1, h] = (own2[s, h, rows] + r2[i, h, rows].astype(f32)).astype(bf)
                self.c3(i, s, k).start()
            rows = pl.ds(pl.multiple_of(z * R, 16), R)
            for h in range(2):
                self.own3[s, h] = own2[s, h, rows] + r2[i, h, rows].astype(f32)

        def last(i, s):
            for k in (1, 2, 3): self.c3(i, s, k).wait_recv()
            acc = self.own3[s]
            for k in range(3): acc = acc + self.r3[i, k].astype(f32)
            out_ref[i] = acc

        if product is not None:
            stage(0, zero)
        stage(1, first); stage(2, second); stage(3, third); stage(4, last)

    def finish(self):
        for j in range(self.slots):
            i = self.n - self.slots + j
            s = i % self.slots
            self.c0(i, s).wait_send()
            for h in range(2):
                self.c1(i, s, h).wait_send()
                self.c2(i, s, h).wait_send()
            for k in (1, 2, 3): self.c3(i, s, k).wait_send()
        pl.semaphore_wait(self.free, self.ring)


def one_time(*shape):
    return pl.BlockSpec(shape, lambda j: (0,) * len(shape), pipeline_mode=pl.Buffered(1))


def phase_one(j):
    return jnp.minimum(j, TILES - 1)


def phase_two(j):
    return jnp.maximum(j - TILES, 0)


def back_call(mixed, proj, dn, x, par, ent, ds, step, dst, b, c, hp, rq, low_t, cot, collective_id):
    n, R, sk = 24, 48, 1

    def kernel(mixed, z, dn, x, gain, cin, halo, taps, ent, ds, step, dst, b_r, c_r, hp, rq, bcin, bchalo, bctaps, raw, low_t, cot,
               dz_o, ol_o, dcp_o, cg_o, hg_o, rows_o, sums,
               dst_acc, dc_acc, dds_acc, xu_acc, st_s, ct_s, got, part, out, out_sem, in_sem,
               pad, pad2, dpad, dpad2, db_s, xut_s, de_s, prv, lst, edge_in, e_out, e_in,
               dxa_s, dz_s, rhs, lhs_s, *refs):
        j = pl.program_id(0)
        me = Place()
        line = Chain(me, -1, got, part, out, out_sem, in_sem, keeper(ds), 1)
        red = Reduce(me, n, R, refs, sk)
        two_start, two_tile, two_final = sb2_make(me, dcp_o, cg_o, hg_o, pad, pad2, dpad, dpad2, db_s, xut_s, de_s, prv, lst, edge_in, e_out, e_in)

        def rs(it):
            outer = it // 12
            li = outer * (1 + lax.rem(it, 2))
            @pl.when(it < 12)
            def _(): rhs[...] = dz_s[...]
            @pl.when((it >= 12) & (it < n))
            def _(): rhs[...] = cot[:, pl.ds(pl.multiple_of((it - 12) // 2 * 256, 256), 256)]
            red.step(it, lambda i, c: jnp.dot(lhs_s[li, :, c].reshape(16 * R, 512), rhs[...], preferred_element_type=f32).reshape(2, 2, 4 * R, 256), sums)

        @pl.when(j == 0)
        def _():
            greet(me.near())
            line.start()
            sb1_start(b_r, c_r, dst_acc, dc_acc, dds_acc, xu_acc, st_s, ct_s)
            lhs_s[0] = low_t[...]

        @pl.when(j < TILES)
        def _():
            sb1_tile(j, mixed, z, dn, x, ent, gain, ds, step, dst, hp, rq, dxa_s, dz_o, dz_s, ol_o, lhs_s, rows_o,
                     dst_acc, dc_acc, dds_acc, xu_acc, st_s, ct_s, part)
        line.step(j, False)

        @pl.when(j == TILES)
        def _(): two_start()

        @pl.when(j >= TILES)
        def _(): two_tile(j - TILES, dxa_s, x, cin, halo, taps, got, ent, ds, step, b_r)

        rs(j)

        @pl.when(j == 2 * TILES - 1)
        def _():
            two_final(bcin, bchalo, bctaps, raw, ds, step, b_r, c_r, hp, dst_acc, dc_acc, dds_acc, xu_acc)
            line.finish()
            lax.fori_loop(n, n + 4 * sk, lambda it, _: (rs_drain(red, it, sums), 0)[1], 0)
            red.finish()

    D = pltpu.SemaphoreType.DMA
    p1, p2 = phase_one, phase_two
    xt = lambda j: jnp.where(j < TILES, j, j - TILES)
    tok = one_time(512, 128)
    in_specs = [
        pl.BlockSpec((512, 256), lambda j: (0, p1(j))),
        pl.BlockSpec((1, 512, 256), lambda j: (14 + p1(j), 0, 0)),
        pl.BlockSpec((2, 512, 128), lambda j: (p1(j), 0, 0)),
        pl.BlockSpec((512, 256), lambda j: (0, xt(j))),
        pl.BlockSpec((8, 256), lambda j: (0, 19 + p1(j))),
        pl.BlockSpec((1, 512, 256), lambda j: (p2(j), 0, 0)),
        pl.BlockSpec((1, 16, 256), lambda j: (p2(j), 32, 0)),
        pl.BlockSpec((8, 256), lambda j: (0, p2(j))),
        one_time(12, 2, 128, 256), tok, tok, one_time(12, 8, 512), tok, tok, one_time(8, 128), one_time(2, 512, 128),
        BC, BCH, BCT, RAW, one_time(4, 2, 4, 48, 512), one_time(512, 1536),
    ]
    out_specs = (
        pl.BlockSpec((1, 512, 256), lambda j: (p1(j), 0, 0)),
        pl.BlockSpec((512, 256), lambda j: (0, p1(j))),
        one_time(14, 512, 256), one_time(13, 8, 256), one_time(8, 128), one_time(12, 8, 256), one_time(24, 2, 48, 128),
    )
    out_shape = (S((12, 512, 256), bf), S((512, 3072), bf), S((14, 512, 256), bf), S((13, 8, 256), f32), S((8, 128), f32), S((12, 8, 256), f32), S((24, 2, 48, 128), f32))
    scratch = (
        [V((2, 3, 128, 128), f32), V((512, 128), f32), V((512, 128), f32), V((512, 128), f32), V((2, 3, 128, 128), f32), V((2, 128, 256), f32)]
        + Chain.scratch()
        + [V((2, 264, 256), f32), V((2, 264, 256), f32), V((2, 272, 256), f32), V((2, 272, 256), f32), V((512, 128), f32), V((512, 128), f32), V((2, 8, 128), f32),
           V((13, 16, 256), bf), V((13, 16, 256), f32), V((13, 16, 256), bf), D((13,)), D((13,))]
        + [V((12, 512, 256), f32), V((512, 256), bf), V((512, 256), bf), V((3, 4, 2, 4, 48, 512), bf)]
        + Reduce.scratch(n, R, sk)
    )
    return pl.pallas_call(
        kernel, grid=(2 * TILES,), in_specs=in_specs, out_specs=out_specs, out_shape=out_shape, scratch_shapes=scratch,
        compiler_params=pltpu.CompilerParams(vmem_limit_bytes=63 << 20, collective_id=collective_id, has_side_effects=True), name="back",
    )(mixed, proj, dn, x, par, proj, proj, par, ent, ds, step, dst, b, c, hp, rq, proj, proj, par, proj, low_t.reshape(4, 2, 4, 48, 512), cot)


def rs_drain(red, it, sums):
    red.step(it, None, sums)


def end_call(low_t, dcp, dz, ol, win, wout, tok, cot, par, cg, rows, hg, collective_id, skew=2):
    n, R = 14, 48

    def kernel(lhs, dcp_ref, dz_ref, ol_ref, win_hbm, wout_hbm, tok, cot, par_ref, cg_ref, rows_ref, hg_ref, sums, blk, tg, small_o,
               wbuf, wsem, obuf, osem, dn, flat, mail, box, m_out, m_in, *refs):
        me = Place()
        def wcopy(t, p): return pltpu.make_async_copy(win_hbm.at[p], wbuf.at[lax.rem(t, 2), 0 if p is t else 1], wsem.at[lax.rem(t, 2), 0 if p is t else 1])
        def ocopy(i): return pltpu.make_async_copy(wout_hbm.at[i], obuf.at[lax.rem(i, 2)], osem.at[lax.rem(i, 2)])
        def fetch(t):
            wcopy(t, t).start()
            @pl.when(t < 12)
            def _(): wcopy(t, t + 14).start()
        fetch(jnp.int32(0))
        ocopy(jnp.int32(0)).start()
        ocopy(jnp.int32(1)).start()
        bar = pltpu.get_barrier_semaphore()
        def sg(k, _):
            pl.semaphore_signal(bar, inc=1, device_id=me.any_peer(k), device_id_type=MESH)
            return 0
        lax.fori_loop(1, 32, sg, 0)
        pl.semaphore_wait(bar, 31)
        red = Reduce(me, n, R, refs, skew)
        def post(k):
            to = lax.rem(me.line + k, 32)
            return send(mail.at[to], box.at[k - 1], m_out.at[k - 1], m_in.at[k - 1], me.any_peer(k))

        def tail():
            gain = par_ref[5:6, 3328:4864]
            def block(t, acc):
                r = pl.ds(pl.multiple_of(t * 64, 64), 64)
                xf = tok[r].astype(f32)
                h = lax.rsqrt(jnp.mean(xf * xf, axis=-1, keepdims=True) + 1e-5)
                d = dn[r]
                gd = d * gain
                tg[r] = cot[r].astype(f32) + (h * gd - xf * (h * h * h * jnp.mean(gd * xf, axis=-1, keepdims=True)))
                return acc + jnp.sum(d * xf * h, axis=0, keepdims=True)
            norm = lax.fori_loop(0, 8, block, jnp.zeros((1, 1536), f32))
            flat[...] = jnp.zeros_like(flat)
            for j in range(13):
                flat[0:5, 256 * j:256 * j + 256] = cg_ref[j, 0:5]
            flat[5:6, 0:1536] = norm
            for j in range(12):
                flat[6:7, 256 * j:256 * j + 256] = rows_ref[j, 0:1]
            for o in range(32):
                b = [(o * w // 128) * 128 for w in (104, 48, 96)]
                mail[o, 0:5] = flat[0:5, b[0]:b[0] + 256]
                mail[o, 5:6] = flat[5:6, b[1]:b[1] + 256]
                mail[o, 6:7] = flat[6:7, b[2]:b[2] + 256]
                mail[o, 7:8] = hg_ref[0:1]
            lax.fori_loop(1, 32, lambda k, _: (post(k).start(), 0)[1], 0)

        def dgrad(t, q, dp):
            s = lax.rem(t, 2)
            w = jnp.concatenate([wbuf[s, q, h].reshape(1536, 128) for h in range(2)], axis=1)
            return lax.dot_general(dp, w, (((1,), (1,)), ((), ())), preferred_element_type=f32)

        def loop(it, _):
            red.step(it, lambda i, c: jnp.dot(lhs[:, c].reshape(16 * R, 512), dcp_ref[i], preferred_element_type=f32).reshape(2, 2, 4 * R, 256), sums)
            @pl.when(it < n)
            def _():
                @pl.when(it + 1 < n)
                def _(): fetch(it + 1)
                wcopy(it, it).wait()
                r = dgrad(it, 0, dcp_ref[it])
                @pl.when(it == 0)
                def _(): dn[...] = r
                @pl.when(it > 0)
                def _(): dn[...] += r
            @pl.when(it < 12)
            def _():
                wcopy(it, it + 14).wait()
                dn[...] += dgrad(it, 1, dz_ref[it])
            @pl.when(it == n)
            def _(): tail()
            @pl.when((it >= n) & (it < n + 6))
            def _():
                i = it - n
                ocopy(i).wait()
                s = lax.rem(i, 2)
                w = jnp.concatenate([obuf[s, h].reshape(3072, 128) for h in range(2)], axis=1)
                at = pl.ds(pl.multiple_of(i * 256, 256), 256)
                blk[:, at] = (tok[:, at].astype(f32) + jnp.dot(ol_ref[...], w, preferred_element_type=f32)).astype(bf)
                @pl.when(i + 2 < 6)
                def _(): ocopy(i + 2).start()
            return 0
        lax.fori_loop(0, n + 4 * skew, loop, 0)
        small_o[...] = mail[me.line]
        def take(k, _):
            post(k).wait()
            small_o[...] += box[k - 1]
            return 0
        lax.fori_loop(1, 32, take, 0)
        red.finish()

    D, Sd = pltpu.SemaphoreType.DMA, jax.ShapeDtypeStruct
    vm, hb = pl.BlockSpec(memory_space=pltpu.VMEM), pl.BlockSpec(memory_space=pl.ANY)
    return pl.pallas_call(
        kernel, out_shape=(Sd((n, 2, R, 128), f32), Sd((512, 1536), bf), Sd((512, 1536), f32), Sd((8, 256), f32)),
        in_specs=[vm] * 4 + [hb] * 2 + [vm] * 6, out_specs=(vm, vm, vm, vm),
        scratch_shapes=[V((2, 2, 2, 2, 2, 2, 192, 128), bf), D((2, 2)), V((2, 2, 2, 2, 2, 384, 128), bf), D((2,)),
                        V((512, 1536), f32), V((8, 3584), f32), V((32, 8, 256), f32), V((31, 8, 256), f32), D((31,)), D((31,))]
        + Reduce.scratch(n, R, skew),
        compiler_params=pltpu.CompilerParams(collective_id=collective_id, has_side_effects=True, vmem_limit_bytes=63 << 20), name="end",
    )(low_t.reshape(4, 2, 192, 512), dcp, dz, ol, win, wout, tok, cot, par, cg, rows, hg)


def fast(adamw, tokens, cotangent, in_proj, in_mom, in_var, out_proj, out_mom, out_var, conv_params, conv_mom, conv_var,
         norm_gain, norm_mom, norm_var, gate_gain, gate_mom, gate_var, head_params, head_mom, head_var):
    line = lax.axis_index("dp") * 4 + lax.axis_index("seq")
    src_in, src_out, small = arrange(in_proj, out_proj, conv_params, norm_gain, gate_gain, line)
    edge = jnp.pad(tokens[:, 253:], ((0, 0), (0, 5), (0, 0))).reshape(16, 1536)
    tok, cot = tokens.reshape(512, 1536), cotangent.reshape(512, 1536)
    proj, win, wout, low, par, dn = gather_call(src_in, src_out, small, tok, edge, cot, 1)
    hp = jnp.pad(head_params, ((0, 5), (0, 80)))
    x, yi, ent, step, ds, dst, b, c = sf1(proj, par, hp)
    mixed, rq = sf2(yi, x, ent, proj, dn, par, ds, c, hp)
    low_t = low.T
    dz, ol, dcp, cg, hg, rows, sums = back_call(mixed, proj, dn, x, par, ent, ds, step, dst, b, c, hp, rq, low_t, cot, 5)
    skip = jnp.sum(rows[:, 1].reshape(48, 64), axis=1)
    heads = jnp.pad(jnp.concatenate([hg[0, :48], skip, hg[2, :48]])[None], ((0, 7), (0, 112)))
    last, block, tokens_grad, small_sum = end_call(low_t, dcp, dz, ol, win, wout, tok, cot, par, cg, rows, heads, 3)
    out_grad = sums[12:].reshape(6, 2, 2, 48, 128).transpose(1, 3, 0, 2, 4).reshape(96, 1536)
    in_grad = jnp.concatenate([sums[:12].transpose(2, 0, 1, 3).reshape(48, 3072), last.transpose(2, 0, 1, 3).reshape(48, 3584)[:, :304 + 3072]], axis=1)
    tokens_grad = tokens_grad.reshape(2, 256, 1536)
    mine = lambda row, n, w: lax.dynamic_slice(small_sum, (row, lax.rem(line * w, 128)), (n, w))
    conv_grad, norm_grad, gate_grad = mine(0, 5, 104), mine(5, 1, 48)[0], mine(6, 1, 96)[0]
    head_grad = small_sum[7, :144].reshape(3, 48)
    res = [(in_proj, in_mom, in_var, in_grad, 0.1), (out_proj, out_mom, out_var, out_grad, 0.1), (conv_params, conv_mom, conv_var, conv_grad, 0.1),
           (norm_gain, norm_mom, norm_var, norm_grad, 0.0), (gate_gain, gate_mom, gate_var, gate_grad, 0.0), (head_params, head_mom, head_var, head_grad, 0.0)]
    new = [v for a in res for v in adamw(*a)]
    return (block.reshape(2, 256, 1536), tokens_grad, in_grad, out_grad, conv_grad, norm_grad, gate_grad, head_grad, *new)


def solution(mesh):
    in_specs = (
        P("dp", "seq", None),
        P("dp", "seq", None),
        P(("dp", "seq"), None),
        P(("dp", "seq"), None),
        P(("dp", "seq"), None),
        P(("dp", "seq"), None),
        P(("dp", "seq"), None),
        P(("dp", "seq"), None),
        P(None, ("dp", "seq")),
        P(None, ("dp", "seq")),
        P(None, ("dp", "seq")),
        P(("dp", "seq")),
        P(("dp", "seq")),
        P(("dp", "seq")),
        P(("dp", "seq")),
        P(("dp", "seq")),
        P(("dp", "seq")),
        P(),
        P(),
        P(),
    )
    out_specs = (
        P("dp", "seq", None),
        P("dp", "seq", None),
        P(("dp", "seq"), None),
        P(("dp", "seq"), None),
        P(None, ("dp", "seq")),
        P(("dp", "seq")),
        P(("dp", "seq")),
        P(),
        P(("dp", "seq"), None),
        P(("dp", "seq"), None),
        P(("dp", "seq"), None),
        P(("dp", "seq"), None),
        P(("dp", "seq"), None),
        P(("dp", "seq"), None),
        P(None, ("dp", "seq")),
        P(None, ("dp", "seq")),
        P(None, ("dp", "seq")),
        P(("dp", "seq")),
        P(("dp", "seq")),
        P(("dp", "seq")),
        P(("dp", "seq")),
        P(("dp", "seq")),
        P(("dp", "seq")),
        P(),
        P(),
        P(),
    )
    own = tuple(mesh.shape[a] for a in ("dp", "seq")) == (8, 4)
    step = functools.partial(fast, adamw) if own else body
    return jax.shard_map(step, mesh=mesh, in_specs=in_specs, out_specs=out_specs, check_vma=False)
```

```python
import functools

import jax
import jax.numpy as jnp
from jax import lax
from jax.experimental import pallas as pl
from jax.experimental.pallas import tpu as pltpu
from jax.sharding import PartitionSpec as P

MESH = pl.DeviceIdType.MESH
bf = jnp.bfloat16
f32 = jnp.float32

DI = 3072
HEADS = 48
HEAD_DIM = 64
STATE = 128
KERNEL = 4
STEP = 3
CONV = 3328


highest = lax.Precision.HIGHEST
norm_eps = 1e-05
beta_one = 0.9
beta_two = 0.95
learn_rate = 0.01
decay_rate = 0.1
adam_eps = 1e-08


def from_behind(array, axis, by):
    size = lax.axis_size(axis)
    pairs = [(i, i + by) for i in range(size) if 0 <= i + by < size]
    return lax.ppermute(array, axis, pairs)


def entering(part, axis, combine, identity):
    place = lax.axis_index(axis)
    gathered = jax.tree.map(lambda a: lax.all_gather(a, axis), part)
    state = jax.tree.map(lambda a, e: jnp.zeros_like(a) + jnp.asarray(e, a.dtype), part, identity)

    def one(lap, state):
        return combine(
            state, jax.tree.map(lambda a: lax.dynamic_index_in_dim(a, lap, 0, False), gathered)
        )

    return lax.fori_loop(0, place, one, state)


def prefix(array, axis, combine, identity):
    size, here = (lax.axis_size(axis), lax.axis_index(axis))
    everything = jax.tree.map(
        lambda part, kind: lax.all_gather(part.astype(kind), axis),
        array,
        jax.tree.map(lambda a: jnp.bfloat16 if a.dtype == jnp.float32 else a.dtype, array),
    )
    start = jax.tree.map(
        lambda part, zero: jnp.broadcast_to(jnp.asarray(zero, part.dtype), part.shape),
        array,
        identity,
    )

    def lap(k, before):
        at = size - 1 - k
        reached = at > here
        new = combine(
            before, jax.tree.map(lambda part, own: part[at].astype(own.dtype), everything, array)
        )
        return jax.tree.map(lambda a, b: jnp.where(reached, a, b), new, before)

    return lax.fori_loop(0, size, lap, start)


def rms_scale(values, gain):
    return values * lax.rsqrt(jnp.mean(values * values, axis=-1, keepdims=True) + norm_eps) * gain


def adamw(weight, moment_one, moment_two, gradient, decay_on):
    one_new = beta_one * moment_one + (1.0 - beta_one) * gradient
    two_new = beta_two * moment_two + (1.0 - beta_two) * gradient * gradient
    mean_hat = one_new / (1.0 - beta_one**STEP)
    var_hat = two_new / (1.0 - beta_two**STEP)
    weight_new = weight - learn_rate * (
        mean_hat / (jnp.sqrt(var_hat) + adam_eps) + decay_on * weight
    )
    return (weight_new, one_new, two_new)


def fold_pair(earlier, later):
    decay_early, state_early = earlier
    decay_later, state_later = later
    return (decay_early * decay_later, decay_later[:, :, None, None] * state_early + state_later)


def intra_item(pieces):
    head_x, b_proj, c_proj, step_size, decay_sum = pieces
    length = decay_sum.shape[0]
    scores = jnp.dot(c_proj, b_proj.T, precision=highest)
    row_ids = lax.broadcasted_iota(jnp.int32, (length, length), 0)
    col_ids = lax.broadcasted_iota(jnp.int32, (length, length), 1)
    causal = (col_ids <= row_ids)[None, :, :]
    sums_by_head = decay_sum.T
    gap_sums = sums_by_head[:, :, None] - sums_by_head[:, None, :]
    decay_mat = jnp.exp(jnp.where(causal, gap_sums, -1e30))
    weights = scores[None, :, :] * decay_mat * step_size.T[:, None, :]
    return jnp.einsum("hts,shp->thp", weights, head_x, precision=highest)


def front(conv_in, previous, conv_weight, step_raw, head_weight):
    seq_count = conv_in.shape[0]
    length = conv_in.shape[1]
    padded = jnp.concatenate([previous, conv_in], axis=1)
    conv_out = conv_weight[KERNEL]
    for tap_index in range(KERNEL):
        conv_out = conv_out + conv_weight[tap_index] * padded[:, tap_index : tap_index + length, :]
    activated = jax.nn.silu(conv_out)
    head_x = activated[:, :, :DI].reshape(seq_count, length, HEADS, HEAD_DIM)
    b_proj = activated[:, :, DI : DI + STATE]
    c_proj = activated[:, :, DI + STATE :]
    step_size = jax.nn.softplus(step_raw + head_weight[2])
    decay_sum = jnp.cumsum(step_size * -jnp.exp(head_weight[0]), axis=1)
    last_sum = decay_sum[:, -1, :]
    tail_weight = jnp.exp(last_sum[:, None, :] - decay_sum) * step_size
    local_state = jnp.einsum("gsh,gshp,gsn->ghpn", tail_weight, head_x, b_proj, precision=highest)
    return (local_state, jnp.exp(last_sum), head_x, b_proj, c_proj, step_size, decay_sum)


def back(head_x, b_proj, c_proj, step_size, decay_sum, head_weight, gate_z, gate_weight, state_in):
    seq_count = gate_z.shape[0]
    length = gate_z.shape[1]
    inner_out = lax.map(jax.checkpoint(intra_item), (head_x, b_proj, c_proj, step_size, decay_sum))
    carried = jnp.exp(decay_sum)[..., None] * jnp.einsum(
        "gtn,ghpn->gthp", c_proj, state_in, precision=highest
    )
    mixed_y = inner_out + carried + head_weight[1][:, None] * head_x
    gated = mixed_y.reshape(seq_count, length, DI) * jax.nn.silu(gate_z)
    return rms_scale(gated, gate_weight)


def body(
    tokens,
    cotangent,
    in_proj,
    in_proj_mom,
    in_proj_var,
    out_proj,
    out_proj_mom,
    out_proj_var,
    conv_params,
    conv_mom,
    conv_var,
    norm_gain,
    norm_mom,
    norm_var,
    gate_gain,
    gate_mom,
    gate_var,
    head_params,
    head_mom,
    head_var,
):
    in_full, out_full = (
        lax.all_gather(in_proj.astype(jnp.bfloat16), ("dp", "seq"), axis=0, tiled=True),
        lax.all_gather(out_proj.astype(jnp.bfloat16), ("dp", "seq"), axis=0, tiled=True),
    )
    conv_full, norm_full, gate_full = (
        lax.all_gather(conv_params, ("dp", "seq"), axis=1, tiled=True),
        lax.all_gather(norm_gain, ("dp", "seq"), axis=0, tiled=True),
        lax.all_gather(gate_gain, ("dp", "seq"), axis=0, tiled=True),
    )
    length = tokens.shape[1]
    rim_start = length - (KERNEL - 1)
    inputs = tokens.astype(jnp.float32)
    normed_in, norm_pull = jax.vjp(rms_scale, inputs, norm_full)
    lowered = normed_in.astype(jnp.bfloat16)
    projected = jnp.einsum("gtd,dp->gtp", lowered, in_full, preferred_element_type=jnp.float32)
    gate_z = projected[:, :, :DI]
    conv_in = projected[:, :, DI : DI + CONV]
    step_raw = projected[:, :, DI + CONV :]
    previous = from_behind(conv_in[:, rim_start:, :], "seq", 1)
    front_out, front_pull = jax.vjp(front, conv_in, previous, conv_full, step_raw, head_params)
    local_state, decays, head_x, b_proj, c_proj, step_size, decay_sum = front_out
    unit_decay = jnp.ones_like(decays)
    zero_state = jnp.zeros_like(local_state)
    reached, state_in = entering((decays, local_state), "seq", fold_pair, (unit_decay, zero_state))
    out_normed, back_pull = jax.vjp(
        back, head_x, b_proj, c_proj, step_size, decay_sum, head_params, gate_z, gate_full, state_in
    )
    out_lowered = out_normed.astype(jnp.bfloat16)
    branch = jnp.einsum("gti,id->gtd", out_lowered, out_full, preferred_element_type=jnp.float32)
    block_out = (inputs + branch).astype(jnp.bfloat16)
    out_grad_local = jnp.einsum(
        "gti,gtd->id", out_lowered, cotangent, preferred_element_type=jnp.float32
    )
    d_normed = jnp.einsum("gtd,id->gti", cotangent, out_full, preferred_element_type=jnp.float32)
    (
        d_head_x,
        d_b_proj,
        d_c_proj,
        d_step,
        d_decay_sum,
        d_head_back,
        d_gate_z,
        d_gate_gain,
        d_state_in,
    ) = back_pull(d_normed)
    later_decay, d_state_out = prefix(
        (decays, d_state_in), "seq", fold_pair, (unit_decay, zero_state)
    )
    d_decays = jnp.sum(d_state_out * state_in, axis=(2, 3))
    d_conv_in, d_previous, d_conv, d_step_raw, d_head_front = front_pull(
        (d_state_out, d_decays, d_head_x, d_b_proj, d_c_proj, d_step, d_decay_sum)
    )
    returned = from_behind(d_previous.astype(jnp.bfloat16), "seq", -1).astype(d_previous.dtype)
    d_conv_in = jnp.concatenate(
        [d_conv_in[:, :rim_start, :], d_conv_in[:, rim_start:, :] + returned], axis=1
    )
    d_projected = jnp.concatenate([d_gate_z, d_conv_in, d_step_raw], axis=-1).astype(jnp.bfloat16)
    in_grad_local = jnp.einsum(
        "gtd,gtp->dp", lowered, d_projected, preferred_element_type=jnp.float32
    )
    d_normed_in = jnp.einsum(
        "gtp,dp->gtd", d_projected, in_full, preferred_element_type=jnp.float32
    )
    d_inputs, norm_grad_local = norm_pull(d_normed_in)
    tokens_grad = cotangent.astype(jnp.float32) + d_inputs
    head_grad = lax.psum(d_head_back + d_head_front, ("dp", "seq"))
    in_grad, out_grad, conv_grad, norm_grad, gate_grad = (
        lax.psum_scatter(in_grad_local, ("dp", "seq"), scatter_dimension=0, tiled=True),
        lax.psum_scatter(out_grad_local, ("dp", "seq"), scatter_dimension=0, tiled=True),
        lax.psum_scatter(d_conv, ("dp", "seq"), scatter_dimension=1, tiled=True),
        lax.psum_scatter(norm_grad_local, ("dp", "seq"), scatter_dimension=0, tiled=True),
        lax.psum_scatter(d_gate_gain, ("dp", "seq"), scatter_dimension=0, tiled=True),
    )
    in_new, in_mom_new, in_var_new = adamw(in_proj, in_proj_mom, in_proj_var, in_grad, decay_rate)
    out_new, out_mom_new, out_var_new = adamw(
        out_proj, out_proj_mom, out_proj_var, out_grad, decay_rate
    )
    conv_new, conv_mom_new, conv_var_new = adamw(
        conv_params, conv_mom, conv_var, conv_grad, decay_rate
    )
    norm_new, norm_mom_new, norm_var_new = adamw(norm_gain, norm_mom, norm_var, norm_grad, 0.0)
    gate_new, gate_mom_new, gate_var_new = adamw(gate_gain, gate_mom, gate_var, gate_grad, 0.0)
    head_new, head_mom_new, head_var_new = adamw(head_params, head_mom, head_var, head_grad, 0.0)
    return (
        block_out,
        tokens_grad,
        in_grad,
        out_grad,
        conv_grad,
        norm_grad,
        gate_grad,
        head_grad,
        in_new,
        in_mom_new,
        in_var_new,
        out_new,
        out_mom_new,
        out_var_new,
        conv_new,
        conv_mom_new,
        conv_var_new,
        norm_new,
        norm_mom_new,
        norm_var_new,
        gate_new,
        gate_mom_new,
        gate_var_new,
        head_new,
        head_mom_new,
        head_var_new,
    )


class Place:
    def __init__(self):
        self.dp = dp = lax.axis_index("dp")
        self.z = lax.axis_index("seq")
        self.c = c = lax.rem(dp, 2)
        self.x = x = lax.rem(dp // 2, 2)
        self.y = y = dp // 4
        self.line = dp * 4 + self.z
        self.core_peer = {"dp": dp + 1 - 2 * c}
        self.x_peer = {"dp": dp + 2 - 4 * x}
        self.y_peer = {"dp": dp + 4 - 8 * y}

    def z_peer(self, k):
        return {"seq": lax.rem(self.z + k, 4)}

    def any_peer(self, k):
        at = lax.rem(self.line + k, 32)
        return {"dp": at // 4, "seq": lax.rem(at, 4)}

    def near(self):
        return (self.core_peer, self.x_peer, self.y_peer, self.z_peer(1), self.z_peer(2), self.z_peer(3))


def greet(peers):
    bar = pltpu.get_barrier_semaphore()
    for peer in peers:
        pl.semaphore_signal(bar, inc=1, device_id=peer, device_id_type=MESH)
    pl.semaphore_wait(bar, len(peers))


def send(src, dst, out_sem, in_sem, peer):
    return pltpu.make_async_remote_copy(
        src_ref=src, dst_ref=dst, send_sem=out_sem, recv_sem=in_sem, device_id=peer, device_id_type=MESH
    )


class Gather:
    def __init__(self, me, n, src, w, sems, skew, base=0):
        self.base = base
        self.me, self.n, self.src, self.w, self.sk, self.slots = me, n, src, w, skew, skew + 1
        self.rows = src.shape[2]
        self.o1, self.o2, self.o3, self.o4, self.i1, self.i2, self.i3, self.i4, self.own = sems

    @staticmethod
    def sems(n, skew):
        D = pltpu.SemaphoreType.DMA
        return [D((skew + 1, 3)), D((skew + 1, 2)), D((skew + 1, 2)), D((skew + 1,)), D((n, 3)), D((n, 2)), D((n, 2)), D((n,)), D((skew + 1,))]

    def mine(self, i, s):
        m = self.me
        rows = pl.ds(pl.multiple_of(m.z * self.rows, 16), self.rows)
        return pltpu.make_async_copy(self.src.at[self.base + i], self.w.at[self.base + i, :, m.y, m.x, m.c, rows], self.own.at[s])

    def c1(self, i, s, k):
        m, w = self.me, self.w
        rows = pl.ds(pl.multiple_of(m.z * self.rows, 16), self.rows)
        return send(self.src.at[self.base + i], w.at[self.base + i, :, m.y, m.x, m.c, rows], self.o1.at[s, k - 1], self.i1.at[i, k - 1], m.z_peer(k))

    def c2(self, i, s, h):
        m, w = self.me, self.w
        part = w.at[self.base + i, h, m.y, m.x, m.c]
        return send(part, part, self.o2.at[s, h], self.i2.at[i, h], (m.y_peer, m.x_peer)[h])

    def c3(self, i, s, h):
        m, w = self.me, self.w
        part = w.at[self.base + i, 0, :, m.x, m.c] if h == 0 else w.at[self.base + i, 1, m.y, :, m.c]
        return send(part, part, self.o3.at[s, h], self.i3.at[i, h], (m.x_peer, m.y_peer)[h])

    def c4(self, i, s):
        m, w = self.me, self.w
        part = w.at[self.base + i, :, :, :, m.c]
        return send(part, part, self.o4.at[s], self.i4.at[i], m.core_peer)

    def step(self, it):
        n, sk, ns = self.n, self.sk, self.slots

        def stage(lag, body):
            @pl.when((it >= lag * sk) & (it < n + lag * sk))
            def _():
                i = it - lag * sk
                body(i, lax.rem(i, ns))

        def first(i, s):
            m = self.me
            @pl.when(i >= ns)
            def _():
                for k in (1, 2, 3): self.c1(i, s, k).wait_send()
            self.mine(i, s).start()
            for k in (2, 1, 3): self.c1(i, s, k).start()

        def second(i, s):
            @pl.when(i >= ns)
            def _():
                for h in range(2): self.c2(i, s, h).wait_send()
            self.mine(i, s).wait()
            for k in (1, 2, 3): self.c1(i, s, k).wait_recv()
            for h in range(2): self.c2(i, s, h).start()

        def third(i, s):
            @pl.when(i >= ns)
            def _():
                for h in range(2): self.c3(i, s, h).wait_send()
            for h in range(2):
                self.c2(i, s, h).wait_recv()
                self.c3(i, s, h).start()

        def fourth(i, s):
            @pl.when(i >= ns)
            def _(): self.c4(i, s).wait_send()
            for h in range(2): self.c3(i, s, h).wait_recv()
            self.c4(i, s).start()

        stage(0, first); stage(1, second); stage(2, third); stage(3, fourth)

    def arrived(self, i):
        self.c4(i, 0).wait_recv()

    def finish(self):
        for j in range(self.slots):
            i = self.n - self.slots + j
            s = i % self.slots
            for k in (1, 2, 3): self.c1(i, s, k).wait_send()
            for h in range(2):
                self.c2(i, s, h).wait_send()
                self.c3(i, s, h).wait_send()
            self.c4(i, s).wait_send()


def arrange(in_proj, out_proj, conv_params, norm_gain, gate_gain, line):
    w = in_proj.astype(bf)
    w = jnp.concatenate([w[:, 6400:], jnp.zeros((48, 208), bf), w[:, 6144:6400], w[:, 3072:6144], w[:, :3072]], axis=1)
    src_in = w.reshape(48, 26, 2, 128).transpose(1, 2, 0, 3)
    src_out = out_proj.astype(bf).reshape(96, 6, 2, 128).transpose(1, 2, 0, 3)
    small = jnp.zeros((8, 256), f32)
    for rows, row, width in ((conv_params, 0, 104), (norm_gain[None], 5, 48), (gate_gain[None], 6, 96)):
        small = lax.dynamic_update_slice(small, rows, (row, lax.rem(line * width, 128)))
    return src_in, src_out, small


TILES = 12
NN, NT, TN_ = (((1,), (0,)), ((), ())), (((1,), (1,)), ((), ())), (((0,), (0,)), ((), ()))


def one(a, b, dims):
    return lax.dot_general(a, b, dims, preferred_element_type=f32)


def halves(a):
    hi = a.astype(bf)
    return hi, (a - hi.astype(f32)).astype(bf)


def cross(a, b, dims=NN):
    (ah, al), (bh, bl) = (v if isinstance(v, tuple) else (v, None) for v in (a, b))
    out = one(ah, bh, dims)
    if bl is not None:
        out = out + one(ah, bl, dims)
    if al is not None:
        out = out + one(al, bh, dims)
    return out


def mul(a, b, dims=NN):
    return cross(*(v if isinstance(v, tuple) or v.dtype == bf else halves(v) for v in (a, b)), dims)


def mul_exact(a, b, dims=NN, left=True):
    v = b if left else a
    h = v.astype(bf)
    r = v - h.astype(f32)
    m = r.astype(bf)
    l = (r - m.astype(f32)).astype(bf)
    if left:
        a = a.astype(bf)
        return one(a, h, dims) + (one(a, m, dims) + one(a, l, dims))
    b = b.astype(bf)
    return one(h, b, dims) + (one(m, b, dims) + one(l, b, dims))


def to_heads(a, spot):
    return cross(halves(a), spot)


def rolled(a, j):
    return pltpu.roll(a, lax.rem(128 - 4 * j, 128), 1)


def spread(r):
    lane = lax.broadcasted_iota(jnp.int32, (r.shape[0], 128), 1)
    return jnp.concatenate([jnp.where(lane < 64, r[:, h:h + 1], r[:, h + 1:h + 2]) for h in (0, 2)], 1)


def by_head(v):
    lane = lax.broadcasted_iota(jnp.int32, v.shape, 1)
    zero = jnp.zeros_like(v)
    return jnp.concatenate([jnp.where(lane < 64, v, zero), jnp.where(lane >= 64, v, zero)], 0)


def heads_apart(pair):
    return tuple(by_head(v.astype(f32)).astype(bf) for v in pair)


def part_of(pair, *index):
    return tuple(v[index] for v in pair)


def spot_of(j):
    p = lax.broadcasted_iota(jnp.int32, (256, 128), 0)
    lane = lax.broadcasted_iota(jnp.int32, (256, 128), 1)
    return (lane == 4 * j + p // 64).astype(bf)


def fill_pad(pad, cin, halo):
    for g in range(2):
        pad[g, 5:8] = halo[8 * g:8 * g + 3]
        pad[g, 8:264] = cin[256 * g:256 * g + 256]


def conv(pad, taps):
    out = []
    for g in range(2):
        acc = taps[4:5]
        for k in range(4):
            acc = acc + taps[k:k + 1] * pad[g, 5 + k:261 + k]
        out.append(acc)
    return out


def sig(v):
    return 1.0 / (1.0 + jnp.exp(-v))


def causal(flip):
    r = lax.broadcasted_iota(jnp.int32, (128, 128), 0)
    c = lax.broadcasted_iota(jnp.int32, (128, 128), 1)
    return (r <= c) if flip else (c <= r)


class Chain:
    def __init__(self, me, by, got, part, out, out_sem, in_sem, keep):
        self.me, self.by, self.got, self.part, self.out, self.out_sem, self.in_sem, self.keep = me, by, got, part, out, out_sem, in_sem, keep
        self.place = me.z if by == 1 else 3 - me.z

    def copy(self, i):
        s = lax.rem(i, 3)
        return send(self.out.at[s], self.got.at[i], self.out_sem.at[s], self.in_sem.at[i], self.me.z_peer(1 if self.by == 1 else 3))

    def tile(self, i):
        @pl.when(self.place > 0)
        def _(): self.copy(i).wait_recv()

        @pl.when(self.place < 3)
        def _():
            @pl.when(i >= 3)
            def _(): self.copy(i - 3).wait_send()
            s = lax.rem(i, 3)
            for g in range(2):
                self.out[s, g] = (self.keep(i, g) * self.got[i, g].astype(f32) + self.part[i, g]).astype(bf)
            self.copy(i).start()

    def start(self):
        @pl.when(self.place == 0)
        def _(): self.got[...] = jnp.zeros_like(self.got)

    def every_other(self, i):
        u = i - self.place
        @pl.when((u >= 0) & (u < 2 * TILES) & (lax.rem(u, 2) == 0))
        def _(): self.tile(u // 2)

    def four_of_seven(self, i):
        u = i - self.place
        m = lax.rem(u, 7)
        t = 4 * (u // 7) + (m + 1) // 2
        @pl.when((u >= 0) & (t < TILES) & ((m == 0) | (lax.rem(m, 2) == 1)))
        def _(): self.tile(t)

    def finish(self):
        @pl.when(self.place < 3)
        def _():
            for i in range(TILES - 3, TILES): self.copy(i).wait_send()

    @staticmethod
    def scratch():
        D = pltpu.SemaphoreType.DMA
        return [V((TILES, 2, 128, 256), bf), V((TILES, 2, 128, 256), f32), V((3, 2, 128, 256), bf), D((3,)), D((TILES,))]


def keeper(ds):
    def keep(i, g):
        end = 256 * g + 248
        return jnp.exp(spread(rolled(ds[end:end + 8], i))[7:8])
    return keep


V = pltpu.VMEM


def sb1_start(b_r, c_r, dst_acc, dc_acc, dds_acc, xu_acc, st_s, ct_s):
    for a in (dst_acc, dc_acc, dds_acc, xu_acc):
        a[...] = jnp.zeros_like(a)
    for g in range(2):
        b, c = b_r[256 * g:256 * g + 256], c_r[256 * g:256 * g + 256]
        st_s[g, 0] = mul(b[:128], c[:128], NT)
        st_s[g, 1] = mul(b[128:], c[128:], NT)
        st_s[g, 2] = mul(b[:128], c[128:], NT)
        ct_s[g] = c.T


def sb1_tile(j, mixed, z, dn, x, ent, gain, ds, step, dst, hp, rq, dxa_s, dz_o, dz_s, ol_o, lhs_s, rows_o,
             dst_acc, dc_acc, dds_acc, xu_acc, st_s, ct_s, part):
    rds = rolled(ds[...], j)
    dsc = spread(rds)
    stc = spread(rolled(step[...], j))
    skip = spread(rolled(hp[...], j))[1:2]
    ok = causal(True)
    spot = spot_of(j)
    dgain = jnp.zeros((1, 256), f32)
    turned = []
    dskip = jnp.zeros((1, 256), f32)
    for g in range(2):
        r = slice(256 * g, 256 * g + 256)
        zz, mx, xx = z[0, r], mixed[0, r], x[0, r]
        dnr = jnp.concatenate([dn[0, r], dn[1, r]], 1)
        s = sig(zz)
        sil = zz * s
        gated = mx * sil
        rr, kk = (jnp.concatenate([rq[k, r]] * 2, 1) for k in (0, 1))
        gr = gated * rr
        ol = gr * gain[6:7]
        ol_o[r] = ol.astype(bf)
        turned.append(ol.T.astype(bf))
        dgain += jnp.sum(dnr * gr, axis=0, keepdims=True)
        dg = rr * (gain[6:7] * dnr) - gated * kk
        dy = dg * sil
        dz = (dg * mx * (s * (1.0 + zz * (1.0 - s)))).astype(bf)
        dz_o[0, r] = dz
        dz_s[r] = dz
        dskip += jnp.sum(dy * xx, axis=0, keepdims=True)
        d = dsc[r]
        eu = halves(jnp.exp(d) * dy)
        part[j, g] = mul(ct_s[g], eu)
        dc_acc[r] += mul(eu, ent[j, g], NT)
        dds_acc[r] += to_heads(dy * (mx - skip * xx), spot)
        xs = xx * stc[r]
        dp, xp = halves(dy), halves(xs)
        us = []
        for q in range(2):
            b = 256 * g + 128 * q
            lo = slice(128 * q, 128 * q + 128)
            u, acc = [], 0.0
            for m in range(2):
                e = []
                for h in (2 * m, 2 * m + 1):
                    gap = dst[j, h:h + 1, b:b + 128] - rds[b:b + 128, h:h + 1]
                    e.append(jnp.exp(jnp.where(ok, gap, -1e30)))
                w = jnp.concatenate([st_s[g, q] * e[0], st_s[g, q] * e[1]], 1)
                cols = slice(128 * m, 128 * m + 128)
                dh = heads_apart(part_of(dp, lo, cols))
                u.append(mul(w, dh))
                gt = mul(part_of(xp, lo, cols), dh, NT)
                acc = acc + (gt[:, :128] * e[0] + gt[:, 128:] * e[1])
            dst_acc[g, q] += acc
            us.append(jnp.concatenate(u, 1))
        mid = d[127:128]
        v = jnp.exp(mid - d[:128])
        ud = halves(jnp.exp(d[128:] - mid) * dy[128:])
        us[0] = us[0] + v * mul(st_s[g, 2], ud)
        dst_acc[g, 2] += mul(v * xs[:128], ud, NT)
        u = jnp.concatenate(us, 0)
        xu_acc[r] += to_heads(xx * u, spot)
        dxa_s[j, r] = skip * dy + stc[r] * u
    rows_o[j, 0:1] = dgain
    rows_o[j, 1:2] = dskip
    rows_o[j, 2:8] = jnp.zeros((6, 256), f32)
    turned = jnp.concatenate(turned, 1)
    for k in range(16):
        at = 16 * j + k
        q = at // 3
        owner, sub = q // 2, lax.rem(q, 2)
        rows = pl.ds(pl.multiple_of(lax.rem(at, 3) * 16, 16), 16)
        lhs_s[1 + sub, owner // 8, lax.rem(owner // 4, 2), lax.rem(owner, 4), rows] = turned[16 * k:16 * k + 16]


def conv_back(pad, dpad, dco, taps):
    w = taps.shape[1]
    grads = []
    for k in range(4):
        grads.append(sum(jnp.sum(dco[g] * pad[g, 5 + k:261 + k], axis=0, keepdims=True) for g in range(2)))
    grads.append(sum(jnp.sum(dco[g], axis=0, keepdims=True) for g in range(2)))
    grads.append(jnp.zeros((3, w), f32))
    din, prev = [], []
    for g in range(2):
        dpad[g, 0:8] = jnp.zeros((8, w), f32)
        dpad[g, 8:264] = dco[g]
        dpad[g, 264:272] = jnp.zeros((8, w), f32)
        din.append(sum(taps[k:k + 1] * dpad[g, 11 - k:267 - k] for k in range(4)))
        prev.append(sum(taps[k:k + 1] * dpad[g, 3 - k:11 - k] for k in range(4)))
    return jnp.concatenate(grads, 0), din, prev


def sb2_make(me, dcp_o, cg_o, hg_o, pad, pad2, dpad, dpad2, db_s, xut_s, de_s, prv, lst, edge_in, e_out, e_in):
    def edge(i):
        return send(prv.at[i], edge_in.at[i], e_out.at[i], e_in.at[i], me.z_peer(3))

    def pass_edge(i, prev, din):
        for g in range(2):
            lst[i, 8 * g:8 * g + 8] = din[g][248:]
        prv[i] = jnp.concatenate(prev, 0).astype(bf)

        @pl.when(me.z > 0)
        def _(): edge(i).start()

    def start():
        for a in (db_s, xut_s, de_s):
            a[...] = jnp.zeros_like(a)

    def tile(j, dxa_s, x, cin, halo, taps, got, ent, ds, step, b_r):
        dsc = spread(rolled(ds[...], j))
        stc = spread(rolled(step[...], j))
        spot = spot_of(j)
        fill_pad(pad, cin[0], halo[0])
        dco = []
        for g, co in enumerate(conv(pad, taps)):
            r = slice(256 * g, 256 * g + 256)
            d, xx, st, e = dsc[r], x[0, r], got[j, g], ent[j, g]
            tail = jnp.exp(d[255:256] - d)
            ut = tail * mul(b_r[r], st)
            xut_s[r] += to_heads(xx * ut, spot)
            db_s[r] += mul(tail * stc[r] * xx, st, NT)
            row = jnp.sum(st.astype(f32) * e.astype(f32), axis=0, keepdims=True)
            de_s[g] += to_heads(jnp.broadcast_to(row, (8, 256)), spot)
            dx = dxa_s[j, r] + stc[r] * ut
            s = sig(co)
            dco.append(dx * (s * (1.0 + co * (1.0 - s))))
        grads, din, prev = conv_back(pad, dpad, dco, taps)
        cg_o[j] = grads
        for g in range(2):
            dcp_o[j + 2, 256 * g:256 * g + 256] = din[g].astype(bf)
        pass_edge(j, prev, din)

    def final(bcin, bchalo, bctaps, raw, ds, step, b_r, c_r, hp, dst_acc, dc_acc, dds_acc, xu_acc):
        fill_pad(pad2, bcin[0], bchalo[0])
        dco2 = []
        for g, co in enumerate(conv(pad2, bctaps)):
            r0 = 256 * g
            b, c = b_r[r0:r0 + 256], c_r[r0:r0 + 256]
            db, dc = db_s[r0:r0 + 256], dc_acc[r0:r0 + 256]
            db = db + jnp.concatenate([mul(dst_acc[g, 0], c[:128]) + mul(dst_acc[g, 2], c[128:]), mul(dst_acc[g, 1], c[128:])], 0)
            dc = dc + jnp.concatenate([mul(dst_acc[g, 0].T, b[:128]), mul(dst_acc[g, 1].T, b[128:]) + mul(dst_acc[g, 2].T, b[:128])], 0)
            s = sig(co)
            dco2.append(jnp.concatenate([db, dc], 1) * (s * (1.0 + co * (1.0 - s))))
        grads, din, prev = conv_back(pad2, dpad2, dco2, bctaps)
        cg_o[12] = grads
        for g in range(2):
            dcp_o[1, 256 * g:256 * g + 256] = din[g].astype(bf)
        pass_edge(TILES, prev, din)
        st = step[...]
        xut = xut_s[...]
        speed = -jnp.exp(hp[0:1])
        dds = dds_acc[...] - st * (xu_acc[...] + xut)
        lane = lax.broadcasted_iota(jnp.int32, (512, 128), 1)
        tok = lax.broadcasted_iota(jnp.int32, (256, 128), 0)
        rr = lax.broadcasted_iota(jnp.int32, (256, 256), 0)
        cc = lax.broadcasted_iota(jnp.int32, (256, 256), 1)
        up = (cc >= rr).astype(bf)
        drate = []
        for g in range(2):
            r = slice(256 * g, 256 * g + 256)
            end = jnp.sum(st[r] * xut[r], axis=0, keepdims=True) + de_s[g][0:1] * jnp.exp(ds[256 * g + 255:256 * g + 256])
            drate.append(mul_exact(up, dds[r] + jnp.where(tok == 255, end, 0.0)))
        drate = jnp.concatenate(drate, 0)
        dstep = xu_acc[...] + xut + drate * speed
        draw = jnp.where(lane < 48, dstep * sig(raw[0] + hp[2:3]), 0.0)
        dcp_o[0, :, 0:128] = draw.astype(bf)
        dcp_o[0, :, 128:256] = jnp.zeros((512, 128), bf)
        hg_o[0:1] = jnp.sum(drate * st * speed, axis=0, keepdims=True)
        hg_o[1:2] = jnp.zeros((1, 128), f32)
        hg_o[2:3] = jnp.sum(draw, axis=0, keepdims=True)
        hg_o[3:8] = jnp.zeros((5, 128), f32)

        @pl.when(me.z < 3)
        def _():
            def patch(i, _):
                edge(i).wait_recv()
                for g in range(2):
                    rows = lst[i, 8 * g:8 * g + 8] + edge_in[i, 8 * g:8 * g + 8].astype(f32)
                    dcp_o[jnp.where(i < TILES, i + 2, 1), 256 * g + 248:256 * g + 256] = rows.astype(bf)
                return 0
            lax.fori_loop(0, TILES + 1, patch, 0)

        @pl.when(me.z > 0)
        def _(): lax.fori_loop(0, TILES + 1, lambda i, _: (edge(i).wait_send(), 0)[1], 0)

    return start, tile, final


S = jax.ShapeDtypeStruct
V = pltpu.VMEM


def const(*shape):
    return pl.BlockSpec(shape, lambda j: (0,) * len(shape), pipeline_mode=pl.Buffered(1))


BC = pl.BlockSpec((1, 512, 256), lambda j: (1, 0, 0), pipeline_mode=pl.Buffered(1))
BCH = pl.BlockSpec((1, 16, 256), lambda j: (1, 32, 0), pipeline_mode=pl.Buffered(1))
RAW = pl.BlockSpec((1, 512, 128), lambda j: (0, 0, 0), pipeline_mode=pl.Buffered(1))
BCT = pl.BlockSpec((8, 256), lambda j: (0, 12), pipeline_mode=pl.Buffered(1))


class Reduce:
    def __init__(self, me, n, rows, refs, skew):
        self.me, self.n, self.rows, self.sk, self.slots, self.ring = me, n, rows, skew, skew + 1, skew + 2
        (self.own0, self.own1, self.own2, self.own3, self.s0, self.s1, self.s2, self.s3, self.r0, self.r1, self.r2, self.r3,
         self.o0, self.o1, self.o2, self.o3, self.i0, self.i1, self.i2, self.i3, self.free) = refs

    @staticmethod
    def scratch(n, rows, skew):
        V, D, k = pltpu.VMEM, pltpu.SemaphoreType.DMA, skew + 1
        z = 4 * rows
        return [V((k, 2, 2, 2, z, 128), f32), V((k, 2, 2, z, 128), f32), V((k, 2, z, 128), f32), V((k, 2, rows, 128), f32),
                V((k, 2, 2, 2, z, 128), f32), V((k, 2, 2, z, 128), bf), V((k, 2, z, 128), bf), V((k, 3, 2, rows, 128), bf),
                V((skew + 2, 2, 2, 2, z, 128), f32), V((n, 2, 2, z, 128), bf), V((n, 2, z, 128), bf), V((n, 3, 2, rows, 128), bf),
                D((k,)), D((k, 2)), D((k, 2)), D((k, 3)), D((n,)), D((n, 2)), D((n, 2)), D((n, 3)), pltpu.SemaphoreType.REGULAR]

    def c0(self, i, s):
        return send(self.s0.at[s], self.r0.at[lax.rem(i, self.ring)], self.o0.at[s], self.i0.at[i], self.me.core_peer)

    def c1(self, i, s, h):
        return send(self.s1.at[s, h], self.r1.at[i, h], self.o1.at[s, h], self.i1.at[i, h], (self.me.x_peer, self.me.y_peer)[h])

    def c2(self, i, s, h):
        return send(self.s2.at[s, h], self.r2.at[i, h], self.o2.at[s, h], self.i2.at[i, h], (self.me.y_peer, self.me.x_peer)[h])

    def c3(self, i, s, k):
        return send(self.s3.at[s, k - 1], self.r3.at[i, k - 1], self.o3.at[s, k - 1], self.i3.at[i, k - 1], self.me.z_peer(k))

    def step(self, it, product, out_ref):
        n, sk, ns, R = self.n, self.sk, self.slots, self.rows
        me, x, y, z, c = self.me, self.me.x, self.me.y, self.me.z, self.me.c

        def stage(lag, body):
            @pl.when((it >= lag * sk) & (it < n + lag * sk))
            def _():
                i = it - lag * sk
                body(i, lax.rem(i, ns))

        def zero(i, s):
            @pl.when(i >= ns)
            def _(): self.c0(i, s).wait_send()
            part = product(i, 1 - c)
            for h in range(2):
                self.s0[s, h] = part[..., h * 128:(h + 1) * 128]
            @pl.when(i >= self.ring)
            def _(): pl.semaphore_wait(self.free, 1)
            self.c0(i, s).start()
            part = product(i, c)
            for h in range(2):
                self.own0[s, h] = part[..., h * 128:(h + 1) * 128]

        def first(i, s):
            own0, r0, own1 = self.own0, self.r0, self.own1
            q = lax.rem(i, self.ring)
            @pl.when(i >= ns)
            def _():
                for h in range(2): self.c1(i, s, h).wait_send()
            self.c0(i, s).wait_recv()
            for a in range(2):
                self.s1[s, 0, a] = (own0[s, 0, a, 1 - x] + r0[q, 0, a, 1 - x]).astype(bf)
            self.c1(i, s, 0).start()
            self.s1[s, 1] = (own0[s, 1, 1 - y] + r0[q, 1, 1 - y]).astype(bf)
            self.c1(i, s, 1).start()
            for a in range(2):
                own1[s, 0, a] = own0[s, 0, a, x] + r0[q, 0, a, x]
            own1[s, 1] = own0[s, 1, y] + r0[q, 1, y]
            pl.semaphore_signal(self.free, inc=1, device_id=me.core_peer, device_id_type=MESH)

        def second(i, s):
            own1, r1 = self.own1, self.r1
            @pl.when(i >= ns)
            def _():
                for h in range(2): self.c2(i, s, h).wait_send()
            for h, g in ((0, y), (1, x)):
                self.c1(i, s, h).wait_recv()
                self.s2[s, h] = (own1[s, h, 1 - g] + r1[i, h, 1 - g].astype(f32)).astype(bf)
                self.c2(i, s, h).start()
                self.own2[s, h] = own1[s, h, g] + r1[i, h, g].astype(f32)

        def third(i, s):
            own2, r2 = self.own2, self.r2
            @pl.when(i >= ns)
            def _():
                for k in (1, 2, 3): self.c3(i, s, k).wait_send()
            for h in range(2): self.c2(i, s, h).wait_recv()
            for k in (2, 1, 3):
                rows = pl.ds(pl.multiple_of(lax.rem(z + k, 4) * R, 16), R)
                for h in range(2):
                    self.s3[s, k - 1, h] = (own2[s, h, rows] + r2[i, h, rows].astype(f32)).astype(bf)
                self.c3(i, s, k).start()
            rows = pl.ds(pl.multiple_of(z * R, 16), R)
            for h in range(2):
                self.own3[s, h] = own2[s, h, rows] + r2[i, h, rows].astype(f32)

        def last(i, s):
            for k in (1, 2, 3): self.c3(i, s, k).wait_recv()
            acc = self.own3[s]
            for k in range(3): acc = acc + self.r3[i, k].astype(f32)
            out_ref[i] = acc

        if product is not None:
            stage(0, zero)
        stage(1, first); stage(2, second); stage(3, third); stage(4, last)

    def finish(self):
        for j in range(self.slots):
            i = self.n - self.slots + j
            s = i % self.slots
            self.c0(i, s).wait_send()
            for h in range(2):
                self.c1(i, s, h).wait_send()
                self.c2(i, s, h).wait_send()
            for k in (1, 2, 3): self.c3(i, s, k).wait_send()
        pl.semaphore_wait(self.free, self.ring)


def one_time(*shape):
    return pl.BlockSpec(shape, lambda j: (0,) * len(shape), pipeline_mode=pl.Buffered(1))


def phase_one(j):
    return jnp.minimum(j, TILES - 1)


def phase_two(j):
    return jnp.maximum(j - TILES, 0)


def back_call(mixed, proj, dn, x, par, ent, ds, step, dst, b, c, hp, rq, low_t, cot, collective_id):
    n, R, sk = 24, 48, 1

    def kernel(mixed, z, dn, x, gain, cin, halo, taps, ent, ds, step, dst, b_r, c_r, hp, rq, bcin, bchalo, bctaps, raw, low_t, cot,
               dz_o, ol_o, dcp_o, cg_o, hg_o, rows_o, sums,
               dst_acc, dc_acc, dds_acc, xu_acc, st_s, ct_s, got, part, out, out_sem, in_sem,
               pad, pad2, dpad, dpad2, db_s, xut_s, de_s, prv, lst, edge_in, e_out, e_in,
               dxa_s, dz_s, rhs, lhs_s, *refs):
        j = pl.program_id(0)
        me = Place()
        line = Chain(me, -1, got, part, out, out_sem, in_sem, keeper(ds))
        red = Reduce(me, n, R, refs, sk)
        two_start, two_tile, two_final = sb2_make(me, dcp_o, cg_o, hg_o, pad, pad2, dpad, dpad2, db_s, xut_s, de_s, prv, lst, edge_in, e_out, e_in)

        def rs(it):
            outer = it // 12
            li = outer * (1 + lax.rem(it, 2))
            @pl.when(it < 12)
            def _(): rhs[...] = dz_s[...]
            @pl.when((it >= 12) & (it < n))
            def _(): rhs[...] = cot[:, pl.ds(pl.multiple_of((it - 12) // 2 * 256, 256), 256)]
            red.step(it, lambda i, c: jnp.dot(lhs_s[li, :, c].reshape(16 * R, 512), rhs[...], preferred_element_type=f32).reshape(2, 2, 4 * R, 256), sums)

        @pl.when(j == 0)
        def _():
            greet(me.near())
            line.start()
            sb1_start(b_r, c_r, dst_acc, dc_acc, dds_acc, xu_acc, st_s, ct_s)
            lhs_s[0] = low_t[...]

        @pl.when(j < TILES)
        def _():
            sb1_tile(j, mixed, z, dn, x, ent, gain, ds, step, dst, hp, rq, dxa_s, dz_o, dz_s, ol_o, lhs_s, rows_o,
                     dst_acc, dc_acc, dds_acc, xu_acc, st_s, ct_s, part)
        line.four_of_seven(j)

        @pl.when(j == TILES)
        def _(): two_start()

        @pl.when(j >= TILES)
        def _(): two_tile(j - TILES, dxa_s, x, cin, halo, taps, got, ent, ds, step, b_r)

        rs(j)

        @pl.when(j == 2 * TILES - 1)
        def _():
            two_final(bcin, bchalo, bctaps, raw, ds, step, b_r, c_r, hp, dst_acc, dc_acc, dds_acc, xu_acc)
            line.finish()
            lax.fori_loop(n, n + 4 * sk, lambda it, _: (rs_drain(red, it, sums), 0)[1], 0)
            red.finish()

    D = pltpu.SemaphoreType.DMA
    p1, p2 = phase_one, phase_two
    xt = lambda j: jnp.where(j < TILES, j, j - TILES)
    tok = one_time(512, 128)
    in_specs = [
        pl.BlockSpec((1, 512, 256), lambda j: (p1(j), 0, 0)),
        pl.BlockSpec((1, 512, 256), lambda j: (14 + p1(j), 0, 0)),
        pl.BlockSpec((2, 512, 128), lambda j: (p1(j), 0, 0)),
        pl.BlockSpec((1, 512, 256), lambda j: (xt(j), 0, 0)),
        pl.BlockSpec((8, 256), lambda j: (0, 19 + p1(j))),
        pl.BlockSpec((1, 512, 256), lambda j: (2 + p2(j), 0, 0)),
        pl.BlockSpec((1, 16, 256), lambda j: (2 + p2(j), 32, 0)),
        pl.BlockSpec((8, 256), lambda j: (0, p2(j))),
        one_time(12, 2, 128, 256), tok, tok, one_time(12, 8, 512), tok, tok, one_time(8, 128), one_time(2, 512, 128),
        BC, BCH, BCT, RAW, one_time(4, 2, 4, 48, 512), one_time(512, 1536),
    ]
    out_specs = (
        pl.BlockSpec((1, 512, 256), lambda j: (p1(j), 0, 0)),
        pl.BlockSpec((512, 256), lambda j: (0, p1(j))),
        one_time(14, 512, 256), one_time(13, 8, 256), one_time(8, 128), one_time(12, 8, 256), one_time(24, 2, 48, 128),
    )
    out_shape = (S((12, 512, 256), bf), S((512, 3072), bf), S((14, 512, 256), bf), S((13, 8, 256), f32), S((8, 128), f32), S((12, 8, 256), f32), S((24, 2, 48, 128), f32))
    scratch = (
        [V((2, 3, 128, 128), f32), V((512, 128), f32), V((512, 128), f32), V((512, 128), f32), V((2, 3, 128, 128), f32), V((2, 128, 256), f32)]
        + Chain.scratch()
        + [V((2, 264, 256), f32), V((2, 264, 256), f32), V((2, 272, 256), f32), V((2, 272, 256), f32), V((512, 128), f32), V((512, 128), f32), V((2, 8, 128), f32),
           V((13, 16, 256), bf), V((13, 16, 256), f32), V((13, 16, 256), bf), D((13,)), D((13,))]
        + [V((12, 512, 256), f32), V((512, 256), bf), V((512, 256), bf), V((3, 4, 2, 4, 48, 512), bf)]
        + Reduce.scratch(n, R, sk)
    )
    return pl.pallas_call(
        kernel, grid=(2 * TILES,), in_specs=in_specs, out_specs=out_specs, out_shape=out_shape, scratch_shapes=scratch,
        compiler_params=pltpu.CompilerParams(vmem_limit_bytes=63 << 20, collective_id=collective_id, has_side_effects=True), name="back",
    )(mixed, proj, dn, x, par, proj, proj, par, ent, ds, step, dst, b, c, hp, rq, proj, proj, par, proj, low_t.reshape(4, 2, 4, 48, 512), cot)


def rs_drain(red, it, sums):
    red.step(it, None, sums)


def end_call(low_t, dcp, dz, ol, win, wout, tok, cot, par, cg, rows, hg, collective_id, skew=2):
    n, R = 14, 48

    def kernel(lhs, dcp_ref, dz_ref, ol_ref, win_hbm, wout_hbm, tok, cot, par_ref, cg_ref, rows_ref, hg_ref, sums, blk, tg, small_o,
               wbuf, wsem, obuf, osem, dn, flat, mail, box, m_out, m_in, *refs):
        me = Place()
        def wcopy(t, p): return pltpu.make_async_copy(win_hbm.at[p], wbuf.at[lax.rem(t, 2), 0 if p is t else 1], wsem.at[lax.rem(t, 2), 0 if p is t else 1])
        def ocopy(i): return pltpu.make_async_copy(wout_hbm.at[i], obuf.at[lax.rem(i, 2)], osem.at[lax.rem(i, 2)])
        def fetch(t):
            wcopy(t, t).start()
            @pl.when(t < 12)
            def _(): wcopy(t, t + 14).start()
        fetch(jnp.int32(0))
        ocopy(jnp.int32(0)).start()
        ocopy(jnp.int32(1)).start()
        bar = pltpu.get_barrier_semaphore()
        def sg(k, _):
            pl.semaphore_signal(bar, inc=1, device_id=me.any_peer(k), device_id_type=MESH)
            return 0
        lax.fori_loop(1, 32, sg, 0)
        pl.semaphore_wait(bar, 31)
        red = Reduce(me, n, R, refs, skew)
        def post(k):
            to = lax.rem(me.line + k, 32)
            return send(mail.at[to], box.at[k - 1], m_out.at[k - 1], m_in.at[k - 1], me.any_peer(k))

        def tail():
            gain = par_ref[5:6, 3328:4864]
            def block(t, acc):
                r = pl.ds(pl.multiple_of(t * 64, 64), 64)
                xf = tok[r].astype(f32)
                h = lax.rsqrt(jnp.mean(xf * xf, axis=-1, keepdims=True) + 1e-5)
                d = dn[r]
                gd = d * gain
                tg[r] = cot[r].astype(f32) + (h * gd - xf * (h * h * h * jnp.mean(gd * xf, axis=-1, keepdims=True)))
                return acc + jnp.sum(d * xf * h, axis=0, keepdims=True)
            norm = lax.fori_loop(0, 8, block, jnp.zeros((1, 1536), f32))
            flat[...] = jnp.zeros_like(flat)
            for j in range(13):
                flat[0:5, 256 * j:256 * j + 256] = cg_ref[j, 0:5]
            flat[5:6, 0:1536] = norm
            for j in range(12):
                flat[6:7, 256 * j:256 * j + 256] = rows_ref[j, 0:1]
            for o in range(32):
                b = [(o * w // 128) * 128 for w in (104, 48, 96)]
                mail[o, 0:5] = flat[0:5, b[0]:b[0] + 256]
                mail[o, 5:6] = flat[5:6, b[1]:b[1] + 256]
                mail[o, 6:7] = flat[6:7, b[2]:b[2] + 256]
                mail[o, 7:8] = hg_ref[0:1]
            lax.fori_loop(1, 32, lambda k, _: (post(k).start(), 0)[1], 0)

        def dgrad(t, q, dp):
            s = lax.rem(t, 2)
            w = jnp.concatenate([wbuf[s, q, h].reshape(1536, 128) for h in range(2)], axis=1)
            return lax.dot_general(dp, w, (((1,), (1,)), ((), ())), preferred_element_type=f32)

        def loop(it, _):
            red.step(it, lambda i, c: jnp.dot(lhs[:, c].reshape(16 * R, 512), dcp_ref[i], preferred_element_type=f32).reshape(2, 2, 4 * R, 256), sums)
            @pl.when(it < n)
            def _():
                @pl.when(it + 1 < n)
                def _(): fetch(it + 1)
                wcopy(it, it).wait()
                r = dgrad(it, 0, dcp_ref[it])
                @pl.when(it == 0)
                def _(): dn[...] = r
                @pl.when(it > 0)
                def _(): dn[...] += r
            @pl.when(it < 12)
            def _():
                wcopy(it, it + 14).wait()
                dn[...] += dgrad(it, 1, dz_ref[it])
            @pl.when(it == n)
            def _(): tail()
            @pl.when((it >= n) & (it < n + 6))
            def _():
                i = it - n
                ocopy(i).wait()
                s = lax.rem(i, 2)
                w = jnp.concatenate([obuf[s, h].reshape(3072, 128) for h in range(2)], axis=1)
                at = pl.ds(pl.multiple_of(i * 256, 256), 256)
                blk[:, at] = (tok[:, at].astype(f32) + jnp.dot(ol_ref[...], w, preferred_element_type=f32)).astype(bf)
                @pl.when(i + 2 < 6)
                def _(): ocopy(i + 2).start()
            return 0
        lax.fori_loop(0, n + 4 * skew, loop, 0)
        small_o[...] = mail[me.line]
        def take(k, _):
            post(k).wait()
            small_o[...] += box[k - 1]
            return 0
        lax.fori_loop(1, 32, take, 0)
        red.finish()

    D, Sd = pltpu.SemaphoreType.DMA, jax.ShapeDtypeStruct
    vm, hb = pl.BlockSpec(memory_space=pltpu.VMEM), pl.BlockSpec(memory_space=pl.ANY)
    return pl.pallas_call(
        kernel, out_shape=(Sd((n, 2, R, 128), f32), Sd((512, 1536), bf), Sd((512, 1536), f32), Sd((8, 256), f32)),
        in_specs=[vm] * 4 + [hb] * 2 + [vm] * 6, out_specs=(vm, vm, vm, vm),
        scratch_shapes=[V((2, 2, 2, 2, 2, 2, 192, 128), bf), D((2, 2)), V((2, 2, 2, 2, 2, 384, 128), bf), D((2,)),
                        V((512, 1536), f32), V((8, 3584), f32), V((32, 8, 256), f32), V((31, 8, 256), f32), D((31,)), D((31,))]
        + Reduce.scratch(n, R, skew),
        compiler_params=pltpu.CompilerParams(collective_id=collective_id, has_side_effects=True, vmem_limit_bytes=63 << 20), name="end",
    )(low_t.reshape(4, 2, 192, 512), dcp, dz, ol, win, wout, tok, cot, par, cg, rows, hg)


def dt_part(raw, hp, step_o, ds_o, dst_o):
    pre = raw + hp[2:3]
    step = jnp.maximum(pre, 0.0) + jnp.log1p(jnp.exp(-jnp.abs(pre)))
    rate = step * -jnp.exp(hp[0:1])
    step_o[...] = step
    r = lax.broadcasted_iota(jnp.int32, (256, 256), 0)
    c = lax.broadcasted_iota(jnp.int32, (256, 256), 1)
    low = (c <= r).astype(bf)
    for g in range(2):
        ds_o[256 * g:256 * g + 256] = mul_exact(low, rate[256 * g:256 * g + 256])
    turned = ds_o[...].T
    for p in range(TILES):
        dst_o[p, 0:4] = turned[4 * p:4 * p + 4]


def bc_part(block, taps, b_o, c_o, pad, s_s, bt_s):
    fill_pad(pad, block, block[512:528])
    for g, co in enumerate(conv(pad, taps)):
        act = co * sig(co)
        b, c = act[:, :128], act[:, 128:]
        b_o[256 * g:256 * g + 256] = b
        c_o[256 * g:256 * g + 256] = c
        bt_s[g] = b.T
        s_s[g, 0] = mul(c[:128], b[:128], NT)
        s_s[g, 1] = mul(c[128:], b[128:], NT)
        s_s[g, 2] = mul(c[128:], b[:128], NT)


def sf1_tile(j, block, taps, step, ds, dst, x_s, yi_s, part, pad, s_s, bt_s):
    fill_pad(pad, block, block[512:528])
    rds = rolled(ds[...], j)
    dsc = spread(rds)
    stc = spread(rolled(step[...], j))
    ok = causal(False)
    for g, co in enumerate(conv(pad, taps)):
        b0 = 256 * g
        x = co * sig(co)
        x_s[j, b0:b0 + 256] = x
        xs = x * stc[b0:b0 + 256]
        xp = halves(xs)
        d = dsc[b0:b0 + 256]
        ys = []
        for q in range(2):
            b = b0 + 128 * q
            y = []
            for m in range(2):
                w = []
                for h in (2 * m, 2 * m + 1):
                    gap = rds[b:b + 128, h:h + 1] - dst[j, h:h + 1, b:b + 128]
                    w.append(s_s[g, q] * jnp.exp(jnp.where(ok, gap, -1e30)))
                y.append(mul(jnp.concatenate(w, 1), heads_apart(part_of(xp, slice(128 * q, 128 * q + 128), slice(128 * m, 128 * m + 128)))))
            ys.append(jnp.concatenate(y, 1))
        mid = d[127:128]
        ys[1] = ys[1] + jnp.exp(d[128:] - mid) * mul(s_s[g, 2], jnp.exp(mid - d[:128]) * xs[:128])
        yi_s[j, b0:b0 + 128] = ys[0]
        yi_s[j, b0 + 128:b0 + 256] = ys[1]
        part[j, g] = mul(bt_s[g], jnp.exp(d[255:256] - d) * xs)


def sf2_tile(j, z, gain, ds, c_r, hp, x_s, yi_s, got, dn, a1, a2):
    dsc = spread(rolled(ds[...], j))
    skip = spread(rolled(hp[...], j))[1:2]
    for g in range(2):
        r = slice(256 * g, 256 * g + 256)
        mixed = yi_s[j, r] + jnp.exp(dsc[r]) * mul(c_r[r], got[j, g]) + skip * x_s[j, r]
        yi_s[j, r] = mixed
        gated = mixed * (z[r] * sig(z[r]))
        a1[r] += gated * gated
        a2[r] += gain * jnp.concatenate([dn[2 * j, r], dn[2 * j + 1, r]], 1) * gated


def front_call(src_in, src_out, small, tokens, edge, cotangent, hp, collective_id, skew=2):
    NI, NO = src_in.shape[0], src_out.shape[0]
    T, DM = tokens.shape
    TE = T + 16
    FIRST = NI - TILES
    Z0 = FIRST + NO

    def kernel(src_in, src_out, small_ref, tok_ref, edge_ref, cot_ref, hp,
               proj_hbm, win, wout, x_hbm, mixed_hbm, low_hbm, dn_hbm, par_ref, ent_o, step_o, ds_o, dst_o, b_o, c_o, rq_o,
               sm, low_e, edge_in, pbuf, wbuf, obuf, x_s, yi_s, dn_ref, a1, a2, pad, s_s, bt_s, got, part, out, out_sem, in_sem, *sems):
        gs, os_, zs, (sm_out, sm_in, ed_out, ed_in, pb_sem, wl_sem, ol_sem, x_sem, mx_sem, dn_sem, low_sem) = sems[:9], sems[9:18], sems[18:27], sems[27:]
        me = Place()
        bar = pltpu.get_barrier_semaphore()
        def sg(k, _):
            pl.semaphore_signal(bar, inc=1, device_id=me.any_peer(k), device_id_type=MESH)
            return 0
        lax.fori_loop(1, 32, sg, 0)
        pl.semaphore_wait(bar, 31)
        ga = Gather(me, FIRST, src_in, win, gs, skew)
        gb = Gather(me, NO, src_out, wout, os_, skew)
        gz = Gather(me, NI - FIRST, src_in, win, zs, skew, FIRST)
        line = Chain(me, 1, got, part, out, out_sem, in_sem, keeper(ds_o))

        def small_copy(k):
            return send(small_ref, sm.at[me.line], sm_out.at[k - 1], sm_in.at[k - 1], me.any_peer(k))
        def edge_copy():
            return send(edge_ref, edge_in, ed_out, ed_in, {"seq": lax.rem(me.z + 1, 4)})
        lax.fori_loop(1, 32, lambda k, _: (small_copy(k).start(), 0)[1], 0)
        edge_copy().start()
        sm[me.line] = small_ref[...]
        ga.step(0)
        ga.step(1)
        line.start()
        a1[...] = jnp.zeros_like(a1)
        a2[...] = jnp.zeros_like(a2)
        par_ref[...] = jnp.zeros_like(par_ref)
        lax.fori_loop(1, 32, lambda k, _: (small_copy(k).wait(), 0)[1], 0)
        edge_copy().wait()
        for o in range(32):
            for base, width, stop in ((0, 104, 3328), (3328, 48, 4864), (4864, 96, 7936)):
                at = base + (o * width // 128) * 128
                wd = min(256, stop - at)
                par_ref[:, at:at + wd] += sm[o][:, :wd]
        gain = par_ref[5:6, 3328:4864]
        keep = (me.z > 0).astype(f32)

        def norm(v):
            v = v.astype(f32)
            return (v * lax.rsqrt(jnp.mean(v * v, axis=-1, keepdims=True) + 1e-5) * gain).astype(bf)
        def nloop(t, _):
            r = pl.ds(pl.multiple_of(t * 64, 64), 64)
            low_e[r] = norm(tok_ref[r])
            return 0
        lax.fori_loop(0, T // 64, nloop, 0)
        low_e[T:] = norm(edge_in[...].astype(f32) * keep)
        low_copy = pltpu.make_async_copy(low_e.at[0:T], low_hbm, low_sem)
        dn_copy = pltpu.make_async_copy(dn_ref, dn_hbm, dn_sem)
        low_copy.start()

        def two(i): return lax.rem(i, 2)
        def pcopy(i): return pltpu.make_async_copy(pbuf.at[two(i)], proj_hbm.at[i], pb_sem.at[two(i)])
        def wload(i): return pltpu.make_async_copy(win.at[i], wbuf.at[two(i)], wl_sem.at[two(i)])
        def oload(i): return pltpu.make_async_copy(wout.at[i], obuf.at[two(i)], ol_sem.at[two(i)])
        def xcopy(j): return pltpu.make_async_copy(x_s.at[j], x_hbm.at[j], x_sem.at[j])
        def mcopy(j): return pltpu.make_async_copy(yi_s.at[j], mixed_hbm.at[j], mx_sem.at[j])
        def cols(base, j): return pl.ds(pl.multiple_of(base + j * 256, 128), 256)

        LAG = 4 * skew
        def chunk(i):
            s = two(i)
            wload(i).wait()
            @pl.when(i >= 2)
            def _(): pcopy(i - 2).wait()
            w = jnp.concatenate([wbuf[s, h].reshape(DM, 128) for h in range(2)], axis=1)
            pbuf[s] = jnp.dot(low_e[...], w, preferred_element_type=f32)
            pcopy(i).start()
            return pbuf.at[s]

        def loop(it, _):
            @pl.when(it >= 2)
            def _(): ga.step(it)
            gb.step(it - FIRST)
            gz.step(it - Z0)
            a = it - LAG
            @pl.when((a >= 0) & (a < FIRST))
            def _():
                ga.arrived(a)
                wload(a).start()
            @pl.when((a >= FIRST) & (a < Z0))
            def _():
                gb.arrived(a - FIRST)
                oload(a - FIRST).start()
            @pl.when((a >= Z0) & (a < Z0 + TILES))
            def _():
                gz.arrived(a - Z0)
                wload(a - NO).start()
            i = a - 1
            @pl.when((i >= 0) & (i < FIRST))
            def _():
                block = chunk(i)

                @pl.when(i == 0)
                def _(): dt_part(block[0:512, 0:128], hp, step_o, ds_o, dst_o)
                @pl.when(i == 1)
                def _(): bc_part(block, par_ref[:, 3072:3328], b_o, c_o, pad, s_s, bt_s)
                @pl.when(i >= 2)
                def _():
                    j = i - 2
                    sf1_tile(j, block, par_ref[:, cols(0, j)], step_o, ds_o, dst_o, x_s, yi_s, part, pad, s_s, bt_s)
                    xcopy(j).start()
            line.every_other(i - 2)
            @pl.when((i >= FIRST) & (i < Z0))
            def _():
                i2 = i - FIRST
                s = two(i2)
                oload(i2).wait()
                a_ = cot_ref[:, cols(0, i2)]
                def rows(q, _):
                    y = q // 4
                    x = lax.rem(q // 2, 2)
                    c = lax.rem(q, 2)
                    w = jnp.concatenate([obuf[s, h, y, x, c] for h in range(2)], axis=1)
                    r = lax.dot_general(a_, w, NT, preferred_element_type=f32)
                    for t in range(3):
                        rt = r[:, 128 * t:128 * t + 128]
                        @pl.when(i2 == 0)
                        def _(): dn_ref[3 * q + t] = rt
                        @pl.when(i2 > 0)
                        def _(): dn_ref[3 * q + t] += rt
                    return 0
                lax.fori_loop(0, 8, rows, 0)
                @pl.when(i2 == NO - 1)
                def _(): dn_copy.start()
            @pl.when(i >= Z0)
            def _():
                j = i - Z0
                block = chunk(i - NO)
                sf2_tile(j, block, par_ref[6:7, cols(4864, j)], ds_o, c_o, hp, x_s, yi_s, got, dn_ref, a1, a2)
                mcopy(j).start()
            return 0
        lax.fori_loop(0, NI + NO + LAG + 1, loop, 0)

        q = jnp.sum(a2[...], axis=1, keepdims=True) * (1.0 / 3072)
        r = lax.rsqrt(jnp.sum(a1[...], axis=1, keepdims=True) * (1.0 / 3072) + 1e-5)
        rq_o[0] = jnp.broadcast_to(r, (512, 128))
        rq_o[1] = jnp.broadcast_to(r * r * r * q, (512, 128))
        ent_o[...] = got[...]
        pcopy(NI - 2).wait()
        pcopy(NI - 1).wait()
        lax.fori_loop(0, TILES, lambda j, _: (mcopy(j).wait(), 0)[1], 0)
        lax.fori_loop(0, TILES, lambda j, _: (xcopy(j).wait(), 0)[1], 0)
        dn_copy.wait()
        low_copy.wait()
        line.finish()
        ga.finish()
        gb.finish()
        gz.finish()

    D = pltpu.SemaphoreType.DMA
    vm, hb = pl.BlockSpec(memory_space=pltpu.VMEM), pl.BlockSpec(memory_space=pl.ANY)
    wi, wo = (NI, 2, 2, 2, 2, 192, 128), (NO, 2, 2, 2, 2, 384, 128)
    tile = S((TILES, T, 256), f32)
    col = S((T, 128), f32)
    return pl.pallas_call(
        kernel,
        out_shape=(S((NI, TE, 256), f32), S(wi, bf), S(wo, bf), tile, tile, S((T, DM), bf), S((24, T, 128), f32), S((8, 7936), f32),
                   S((TILES, 2, 128, 256), bf), col, col, S((TILES, 8, T), f32), col, col, S((2, T, 128), f32)),
        in_specs=[vm] * 7,
        out_specs=(hb,) * 7 + (vm,) * 8,
        scratch_shapes=[V((32, 8, 256), f32), V((TE, DM), bf), V((16, DM), bf), V((2, TE, 256), f32), V((2,) + wi[1:], bf), V((2,) + wo[1:], bf),
                        V((TILES, T, 256), f32), V((TILES, T, 256), f32), V((24, T, 128), f32), V((T, 256), f32), V((T, 256), f32), V((2, 264, 256), f32), V((2, 3, 128, 128), f32), V((2, 128, 256), f32)]
        + Chain.scratch() + Gather.sems(FIRST, skew) + Gather.sems(NO, skew) + Gather.sems(TILES, skew)
        + [D((31,)), D((31,)), D, D, D((2,)), D((2,)), D((2,)), D((TILES,)), D((TILES,)), D, D],
        compiler_params=pltpu.CompilerParams(collective_id=collective_id, has_side_effects=True, vmem_limit_bytes=63 << 20),
        name="front",
    )(src_in, src_out, small, tokens, edge, cotangent, hp)


def fast(adamw, tokens, cotangent, in_proj, in_mom, in_var, out_proj, out_mom, out_var, conv_params, conv_mom, conv_var,
         norm_gain, norm_mom, norm_var, gate_gain, gate_mom, gate_var, head_params, head_mom, head_var):
    line = lax.axis_index("dp") * 4 + lax.axis_index("seq")
    src_in, src_out, small = arrange(in_proj, out_proj, conv_params, norm_gain, gate_gain, line)
    edge = jnp.pad(tokens[:, 253:], ((0, 0), (0, 5), (0, 0))).reshape(16, 1536)
    tok, cot = tokens.reshape(512, 1536), cotangent.reshape(512, 1536)
    hp = jnp.pad(head_params, ((0, 5), (0, 80)))
    proj, win, wout, x, mixed, low, dn, par, ent, step, ds, dst, b, c, rq = front_call(src_in, src_out, small, tok, edge, cot, hp, 1)
    low_t = low.T
    dz, ol, dcp, cg, hg, rows, sums = back_call(mixed, proj, dn, x, par, ent, ds, step, dst, b, c, hp, rq, low_t, cot, 5)
    skip = jnp.sum(rows[:, 1].reshape(48, 64), axis=1)
    heads = jnp.pad(jnp.concatenate([hg[0, :48], skip, hg[2, :48]])[None], ((0, 7), (0, 112)))
    last, block, tokens_grad, small_sum = end_call(low_t, dcp, dz, ol, win, wout, tok, cot, par, cg, rows, heads, 3)
    out_grad = sums[12:].reshape(6, 2, 2, 48, 128).transpose(1, 3, 0, 2, 4).reshape(96, 1536)
    in_grad = jnp.concatenate([sums[:12].transpose(2, 0, 1, 3).reshape(48, 3072), jnp.concatenate([last[2:], last[1:2], last[:1]]).transpose(2, 0, 1, 3).reshape(48, 3584)[:, :3376]], axis=1)
    tokens_grad = tokens_grad.reshape(2, 256, 1536)
    mine = lambda row, n, w: lax.dynamic_slice(small_sum, (row, lax.rem(line * w, 128)), (n, w))
    conv_grad, norm_grad, gate_grad = mine(0, 5, 104), mine(5, 1, 48)[0], mine(6, 1, 96)[0]
    head_grad = small_sum[7, :144].reshape(3, 48)
    res = [(in_proj, in_mom, in_var, in_grad, 0.1), (out_proj, out_mom, out_var, out_grad, 0.1), (conv_params, conv_mom, conv_var, conv_grad, 0.1),
           (norm_gain, norm_mom, norm_var, norm_grad, 0.0), (gate_gain, gate_mom, gate_var, gate_grad, 0.0), (head_params, head_mom, head_var, head_grad, 0.0)]
    new = [v for a in res for v in adamw(*a)]
    return (block.reshape(2, 256, 1536), tokens_grad, in_grad, out_grad, conv_grad, norm_grad, gate_grad, head_grad, *new)


def solution(mesh):
    in_specs = (
        P("dp", "seq", None),
        P("dp", "seq", None),
        P(("dp", "seq"), None),
        P(("dp", "seq"), None),
        P(("dp", "seq"), None),
        P(("dp", "seq"), None),
        P(("dp", "seq"), None),
        P(("dp", "seq"), None),
        P(None, ("dp", "seq")),
        P(None, ("dp", "seq")),
        P(None, ("dp", "seq")),
        P(("dp", "seq")),
        P(("dp", "seq")),
        P(("dp", "seq")),
        P(("dp", "seq")),
        P(("dp", "seq")),
        P(("dp", "seq")),
        P(),
        P(),
        P(),
    )
    out_specs = (
        P("dp", "seq", None),
        P("dp", "seq", None),
        P(("dp", "seq"), None),
        P(("dp", "seq"), None),
        P(None, ("dp", "seq")),
        P(("dp", "seq")),
        P(("dp", "seq")),
        P(),
        P(("dp", "seq"), None),
        P(("dp", "seq"), None),
        P(("dp", "seq"), None),
        P(("dp", "seq"), None),
        P(("dp", "seq"), None),
        P(("dp", "seq"), None),
        P(None, ("dp", "seq")),
        P(None, ("dp", "seq")),
        P(None, ("dp", "seq")),
        P(("dp", "seq")),
        P(("dp", "seq")),
        P(("dp", "seq")),
        P(("dp", "seq")),
        P(("dp", "seq")),
        P(("dp", "seq")),
        P(),
        P(),
        P(),
    )
    own = tuple(mesh.shape[a] for a in ("dp", "seq")) == (8, 4)
    step = functools.partial(fast, adamw) if own else body
    return jax.shard_map(step, mesh=mesh, in_specs=in_specs, out_specs=out_specs, check_vma=False)
```

```python
import functools

import jax
import jax.numpy as jnp
from jax import lax
from jax.experimental import pallas as pl
from jax.experimental.pallas import tpu as pltpu
from jax.sharding import PartitionSpec as P

MESH = pl.DeviceIdType.MESH
bf = jnp.bfloat16
f32 = jnp.float32

DI = 3072
HEADS = 48
HEAD_DIM = 64
STATE = 128
KERNEL = 4
STEP = 3
CONV = 3328


highest = lax.Precision.HIGHEST
norm_eps = 1e-05
beta_one = 0.9
beta_two = 0.95
learn_rate = 0.01
decay_rate = 0.1
adam_eps = 1e-08


def from_behind(array, axis, by):
    size = lax.axis_size(axis)
    pairs = [(i, i + by) for i in range(size) if 0 <= i + by < size]
    return lax.ppermute(array, axis, pairs)


def entering(part, axis, combine, identity):
    place = lax.axis_index(axis)
    gathered = jax.tree.map(lambda a: lax.all_gather(a, axis), part)
    state = jax.tree.map(lambda a, e: jnp.zeros_like(a) + jnp.asarray(e, a.dtype), part, identity)

    def one(lap, state):
        return combine(
            state, jax.tree.map(lambda a: lax.dynamic_index_in_dim(a, lap, 0, False), gathered)
        )

    return lax.fori_loop(0, place, one, state)


def prefix(array, axis, combine, identity):
    size, here = (lax.axis_size(axis), lax.axis_index(axis))
    everything = jax.tree.map(
        lambda part, kind: lax.all_gather(part.astype(kind), axis),
        array,
        jax.tree.map(lambda a: jnp.bfloat16 if a.dtype == jnp.float32 else a.dtype, array),
    )
    start = jax.tree.map(
        lambda part, zero: jnp.broadcast_to(jnp.asarray(zero, part.dtype), part.shape),
        array,
        identity,
    )

    def lap(k, before):
        at = size - 1 - k
        reached = at > here
        new = combine(
            before, jax.tree.map(lambda part, own: part[at].astype(own.dtype), everything, array)
        )
        return jax.tree.map(lambda a, b: jnp.where(reached, a, b), new, before)

    return lax.fori_loop(0, size, lap, start)


def rms_scale(values, gain):
    return values * lax.rsqrt(jnp.mean(values * values, axis=-1, keepdims=True) + norm_eps) * gain


def adamw(weight, moment_one, moment_two, gradient, decay_on):
    one_new = beta_one * moment_one + (1.0 - beta_one) * gradient
    two_new = beta_two * moment_two + (1.0 - beta_two) * gradient * gradient
    mean_hat = one_new / (1.0 - beta_one**STEP)
    var_hat = two_new / (1.0 - beta_two**STEP)
    weight_new = weight - learn_rate * (
        mean_hat / (jnp.sqrt(var_hat) + adam_eps) + decay_on * weight
    )
    return (weight_new, one_new, two_new)


def fold_pair(earlier, later):
    decay_early, state_early = earlier
    decay_later, state_later = later
    return (decay_early * decay_later, decay_later[:, :, None, None] * state_early + state_later)


def intra_item(pieces):
    head_x, b_proj, c_proj, step_size, decay_sum = pieces
    length = decay_sum.shape[0]
    scores = jnp.dot(c_proj, b_proj.T, precision=highest)
    row_ids = lax.broadcasted_iota(jnp.int32, (length, length), 0)
    col_ids = lax.broadcasted_iota(jnp.int32, (length, length), 1)
    causal = (col_ids <= row_ids)[None, :, :]
    sums_by_head = decay_sum.T
    gap_sums = sums_by_head[:, :, None] - sums_by_head[:, None, :]
    decay_mat = jnp.exp(jnp.where(causal, gap_sums, -1e30))
    weights = scores[None, :, :] * decay_mat * step_size.T[:, None, :]
    return jnp.einsum("hts,shp->thp", weights, head_x, precision=highest)


def front(conv_in, previous, conv_weight, step_raw, head_weight):
    seq_count = conv_in.shape[0]
    length = conv_in.shape[1]
    padded = jnp.concatenate([previous, conv_in], axis=1)
    conv_out = conv_weight[KERNEL]
    for tap_index in range(KERNEL):
        conv_out = conv_out + conv_weight[tap_index] * padded[:, tap_index : tap_index + length, :]
    activated = jax.nn.silu(conv_out)
    head_x = activated[:, :, :DI].reshape(seq_count, length, HEADS, HEAD_DIM)
    b_proj = activated[:, :, DI : DI + STATE]
    c_proj = activated[:, :, DI + STATE :]
    step_size = jax.nn.softplus(step_raw + head_weight[2])
    decay_sum = jnp.cumsum(step_size * -jnp.exp(head_weight[0]), axis=1)
    last_sum = decay_sum[:, -1, :]
    tail_weight = jnp.exp(last_sum[:, None, :] - decay_sum) * step_size
    local_state = jnp.einsum("gsh,gshp,gsn->ghpn", tail_weight, head_x, b_proj, precision=highest)
    return (local_state, jnp.exp(last_sum), head_x, b_proj, c_proj, step_size, decay_sum)


def back(head_x, b_proj, c_proj, step_size, decay_sum, head_weight, gate_z, gate_weight, state_in):
    seq_count = gate_z.shape[0]
    length = gate_z.shape[1]
    inner_out = lax.map(jax.checkpoint(intra_item), (head_x, b_proj, c_proj, step_size, decay_sum))
    carried = jnp.exp(decay_sum)[..., None] * jnp.einsum(
        "gtn,ghpn->gthp", c_proj, state_in, precision=highest
    )
    mixed_y = inner_out + carried + head_weight[1][:, None] * head_x
    gated = mixed_y.reshape(seq_count, length, DI) * jax.nn.silu(gate_z)
    return rms_scale(gated, gate_weight)


def body(
    tokens,
    cotangent,
    in_proj,
    in_proj_mom,
    in_proj_var,
    out_proj,
    out_proj_mom,
    out_proj_var,
    conv_params,
    conv_mom,
    conv_var,
    norm_gain,
    norm_mom,
    norm_var,
    gate_gain,
    gate_mom,
    gate_var,
    head_params,
    head_mom,
    head_var,
):
    in_full, out_full = (
        lax.all_gather(in_proj.astype(jnp.bfloat16), ("dp", "seq"), axis=0, tiled=True),
        lax.all_gather(out_proj.astype(jnp.bfloat16), ("dp", "seq"), axis=0, tiled=True),
    )
    conv_full, norm_full, gate_full = (
        lax.all_gather(conv_params, ("dp", "seq"), axis=1, tiled=True),
        lax.all_gather(norm_gain, ("dp", "seq"), axis=0, tiled=True),
        lax.all_gather(gate_gain, ("dp", "seq"), axis=0, tiled=True),
    )
    length = tokens.shape[1]
    rim_start = length - (KERNEL - 1)
    inputs = tokens.astype(jnp.float32)
    normed_in, norm_pull = jax.vjp(rms_scale, inputs, norm_full)
    lowered = normed_in.astype(jnp.bfloat16)
    projected = jnp.einsum("gtd,dp->gtp", lowered, in_full, preferred_element_type=jnp.float32)
    gate_z = projected[:, :, :DI]
    conv_in = projected[:, :, DI : DI + CONV]
    step_raw = projected[:, :, DI + CONV :]
    previous = from_behind(conv_in[:, rim_start:, :], "seq", 1)
    front_out, front_pull = jax.vjp(front, conv_in, previous, conv_full, step_raw, head_params)
    local_state, decays, head_x, b_proj, c_proj, step_size, decay_sum = front_out
    unit_decay = jnp.ones_like(decays)
    zero_state = jnp.zeros_like(local_state)
    reached, state_in = entering((decays, local_state), "seq", fold_pair, (unit_decay, zero_state))
    out_normed, back_pull = jax.vjp(
        back, head_x, b_proj, c_proj, step_size, decay_sum, head_params, gate_z, gate_full, state_in
    )
    out_lowered = out_normed.astype(jnp.bfloat16)
    branch = jnp.einsum("gti,id->gtd", out_lowered, out_full, preferred_element_type=jnp.float32)
    block_out = (inputs + branch).astype(jnp.bfloat16)
    out_grad_local = jnp.einsum(
        "gti,gtd->id", out_lowered, cotangent, preferred_element_type=jnp.float32
    )
    d_normed = jnp.einsum("gtd,id->gti", cotangent, out_full, preferred_element_type=jnp.float32)
    (
        d_head_x,
        d_b_proj,
        d_c_proj,
        d_step,
        d_decay_sum,
        d_head_back,
        d_gate_z,
        d_gate_gain,
        d_state_in,
    ) = back_pull(d_normed)
    later_decay, d_state_out = prefix(
        (decays, d_state_in), "seq", fold_pair, (unit_decay, zero_state)
    )
    d_decays = jnp.sum(d_state_out * state_in, axis=(2, 3))
    d_conv_in, d_previous, d_conv, d_step_raw, d_head_front = front_pull(
        (d_state_out, d_decays, d_head_x, d_b_proj, d_c_proj, d_step, d_decay_sum)
    )
    returned = from_behind(d_previous.astype(jnp.bfloat16), "seq", -1).astype(d_previous.dtype)
    d_conv_in = jnp.concatenate(
        [d_conv_in[:, :rim_start, :], d_conv_in[:, rim_start:, :] + returned], axis=1
    )
    d_projected = jnp.concatenate([d_gate_z, d_conv_in, d_step_raw], axis=-1).astype(jnp.bfloat16)
    in_grad_local = jnp.einsum(
        "gtd,gtp->dp", lowered, d_projected, preferred_element_type=jnp.float32
    )
    d_normed_in = jnp.einsum(
        "gtp,dp->gtd", d_projected, in_full, preferred_element_type=jnp.float32
    )
    d_inputs, norm_grad_local = norm_pull(d_normed_in)
    tokens_grad = cotangent.astype(jnp.float32) + d_inputs
    head_grad = lax.psum(d_head_back + d_head_front, ("dp", "seq"))
    in_grad, out_grad, conv_grad, norm_grad, gate_grad = (
        lax.psum_scatter(in_grad_local, ("dp", "seq"), scatter_dimension=0, tiled=True),
        lax.psum_scatter(out_grad_local, ("dp", "seq"), scatter_dimension=0, tiled=True),
        lax.psum_scatter(d_conv, ("dp", "seq"), scatter_dimension=1, tiled=True),
        lax.psum_scatter(norm_grad_local, ("dp", "seq"), scatter_dimension=0, tiled=True),
        lax.psum_scatter(d_gate_gain, ("dp", "seq"), scatter_dimension=0, tiled=True),
    )
    in_new, in_mom_new, in_var_new = adamw(in_proj, in_proj_mom, in_proj_var, in_grad, decay_rate)
    out_new, out_mom_new, out_var_new = adamw(
        out_proj, out_proj_mom, out_proj_var, out_grad, decay_rate
    )
    conv_new, conv_mom_new, conv_var_new = adamw(
        conv_params, conv_mom, conv_var, conv_grad, decay_rate
    )
    norm_new, norm_mom_new, norm_var_new = adamw(norm_gain, norm_mom, norm_var, norm_grad, 0.0)
    gate_new, gate_mom_new, gate_var_new = adamw(gate_gain, gate_mom, gate_var, gate_grad, 0.0)
    head_new, head_mom_new, head_var_new = adamw(head_params, head_mom, head_var, head_grad, 0.0)
    return (
        block_out,
        tokens_grad,
        in_grad,
        out_grad,
        conv_grad,
        norm_grad,
        gate_grad,
        head_grad,
        in_new,
        in_mom_new,
        in_var_new,
        out_new,
        out_mom_new,
        out_var_new,
        conv_new,
        conv_mom_new,
        conv_var_new,
        norm_new,
        norm_mom_new,
        norm_var_new,
        gate_new,
        gate_mom_new,
        gate_var_new,
        head_new,
        head_mom_new,
        head_var_new,
    )


class Place:
    def __init__(self):
        self.dp = dp = lax.axis_index("dp")
        self.z = lax.axis_index("seq")
        self.c = c = lax.rem(dp, 2)
        self.x = x = lax.rem(dp // 2, 2)
        self.y = y = dp // 4
        self.line = dp * 4 + self.z
        self.core_peer = {"dp": dp + 1 - 2 * c}
        self.x_peer = {"dp": dp + 2 - 4 * x}
        self.y_peer = {"dp": dp + 4 - 8 * y}

    def z_peer(self, k):
        return {"seq": lax.rem(self.z + k, 4)}

    def any_peer(self, k):
        at = lax.rem(self.line + k, 32)
        return {"dp": at // 4, "seq": lax.rem(at, 4)}

    def near(self):
        return (self.core_peer, self.x_peer, self.y_peer, self.z_peer(1), self.z_peer(2), self.z_peer(3))


def greet(peers):
    bar = pltpu.get_barrier_semaphore()
    for peer in peers:
        pl.semaphore_signal(bar, inc=1, device_id=peer, device_id_type=MESH)
    pl.semaphore_wait(bar, len(peers))


def send(src, dst, out_sem, in_sem, peer):
    return pltpu.make_async_remote_copy(
        src_ref=src, dst_ref=dst, send_sem=out_sem, recv_sem=in_sem, device_id=peer, device_id_type=MESH
    )


class Gather:
    def __init__(self, me, n, src, w, sems, skew, base=0):
        self.base = base
        self.me, self.n, self.src, self.w, self.sk, self.slots = me, n, src, w, skew, skew + 1
        self.rows = src.shape[2]
        self.o1, self.o2, self.o3, self.o4, self.i1, self.i2, self.i3, self.i4, self.own = sems

    @staticmethod
    def sems(n, skew):
        D = pltpu.SemaphoreType.DMA
        return [D((skew + 1, 3)), D((skew + 1, 2)), D((skew + 1, 2)), D((skew + 1,)), D((n, 3)), D((n, 2)), D((n, 2)), D((n,)), D((skew + 1,))]

    def mine(self, i, s):
        m = self.me
        rows = pl.ds(pl.multiple_of(m.z * self.rows, 16), self.rows)
        return pltpu.make_async_copy(self.src.at[self.base + i], self.w.at[self.base + i, :, m.y, m.x, m.c, rows], self.own.at[s])

    def c1(self, i, s, k):
        m, w = self.me, self.w
        rows = pl.ds(pl.multiple_of(m.z * self.rows, 16), self.rows)
        return send(self.src.at[self.base + i], w.at[self.base + i, :, m.y, m.x, m.c, rows], self.o1.at[s, k - 1], self.i1.at[i, k - 1], m.z_peer(k))

    def c2(self, i, s, h):
        m, w = self.me, self.w
        part = w.at[self.base + i, h, m.y, m.x, m.c]
        return send(part, part, self.o2.at[s, h], self.i2.at[i, h], (m.y_peer, m.x_peer)[h])

    def c3(self, i, s, h):
        m, w = self.me, self.w
        part = w.at[self.base + i, 0, :, m.x, m.c] if h == 0 else w.at[self.base + i, 1, m.y, :, m.c]
        return send(part, part, self.o3.at[s, h], self.i3.at[i, h], (m.x_peer, m.y_peer)[h])

    def c4(self, i, s):
        m, w = self.me, self.w
        part = w.at[self.base + i, :, :, :, m.c]
        return send(part, part, self.o4.at[s], self.i4.at[i], m.core_peer)

    def step(self, it):
        n, sk, ns = self.n, self.sk, self.slots

        def stage(lag, body):
            @pl.when((it >= lag * sk) & (it < n + lag * sk))
            def _():
                i = it - lag * sk
                body(i, lax.rem(i, ns))

        def first(i, s):
            m = self.me
            @pl.when(i >= ns)
            def _():
                for k in (1, 2, 3): self.c1(i, s, k).wait_send()
            self.mine(i, s).start()
            for k in (2, 1, 3): self.c1(i, s, k).start()

        def second(i, s):
            @pl.when(i >= ns)
            def _():
                for h in range(2): self.c2(i, s, h).wait_send()
            self.mine(i, s).wait()
            for k in (1, 2, 3): self.c1(i, s, k).wait_recv()
            for h in range(2): self.c2(i, s, h).start()

        def third(i, s):
            @pl.when(i >= ns)
            def _():
                for h in range(2): self.c3(i, s, h).wait_send()
            for h in range(2):
                self.c2(i, s, h).wait_recv()
                self.c3(i, s, h).start()

        def fourth(i, s):
            @pl.when(i >= ns)
            def _(): self.c4(i, s).wait_send()
            for h in range(2): self.c3(i, s, h).wait_recv()
            self.c4(i, s).start()

        stage(0, first); stage(1, second); stage(2, third); stage(3, fourth)

    def arrived(self, i):
        self.c4(i, 0).wait_recv()

    def finish(self):
        for j in range(self.slots):
            i = self.n - self.slots + j
            s = i % self.slots
            for k in (1, 2, 3): self.c1(i, s, k).wait_send()
            for h in range(2):
                self.c2(i, s, h).wait_send()
                self.c3(i, s, h).wait_send()
            self.c4(i, s).wait_send()


TILES = 12
NN, NT, TN_ = (((1,), (0,)), ((), ())), (((1,), (1,)), ((), ())), (((0,), (0,)), ((), ()))


def one(a, b, dims):
    return lax.dot_general(a, b, dims, preferred_element_type=f32)


def halves(a):
    hi = a.astype(bf)
    return hi, (a - hi.astype(f32)).astype(bf)


def cross(a, b, dims=NN):
    (ah, al), (bh, bl) = (v if isinstance(v, tuple) else (v, None) for v in (a, b))
    out = one(ah, bh, dims)
    if bl is not None:
        out = out + one(ah, bl, dims)
    if al is not None:
        out = out + one(al, bh, dims)
    return out


def mul(a, b, dims=NN):
    return cross(*(v if isinstance(v, tuple) or v.dtype == bf else halves(v) for v in (a, b)), dims)


def mul_exact(a, b, dims=NN, left=True):
    v = b if left else a
    h = v.astype(bf)
    r = v - h.astype(f32)
    m = r.astype(bf)
    l = (r - m.astype(f32)).astype(bf)
    if left:
        a = a.astype(bf)
        return one(a, h, dims) + (one(a, m, dims) + one(a, l, dims))
    b = b.astype(bf)
    return one(h, b, dims) + (one(m, b, dims) + one(l, b, dims))


def to_heads(a, spot):
    return cross(halves(a), spot)


def rolled(a, j):
    return pltpu.roll(a, lax.rem(128 - 4 * j, 128), 1)


def spread(r):
    lane = lax.broadcasted_iota(jnp.int32, (r.shape[0], 128), 1)
    return jnp.concatenate([jnp.where(lane < 64, r[:, h:h + 1], r[:, h + 1:h + 2]) for h in (0, 2)], 1)


def by_head(v):
    lane = lax.broadcasted_iota(jnp.int32, v.shape, 1)
    zero = jnp.zeros_like(v)
    return jnp.concatenate([jnp.where(lane < 64, v, zero), jnp.where(lane >= 64, v, zero)], 0)


def heads_apart(pair):
    return tuple(by_head(v.astype(f32)).astype(bf) for v in pair)


def part_of(pair, *index):
    return tuple(v[index] for v in pair)


def spot_of(j):
    p = lax.broadcasted_iota(jnp.int32, (256, 128), 0)
    lane = lax.broadcasted_iota(jnp.int32, (256, 128), 1)
    return (lane == 4 * j + p // 64).astype(bf)


def fill_pad(pad, cin, halo):
    for g in range(2):
        pad[g, 5:8] = halo[8 * g:8 * g + 3]
        pad[g, 8:264] = cin[256 * g:256 * g + 256]


def conv(pad, taps):
    out = []
    for g in range(2):
        acc = taps[4:5]
        for k in range(4):
            acc = acc + taps[k:k + 1] * pad[g, 5 + k:261 + k]
        out.append(acc)
    return out


def sig(v):
    return 1.0 / (1.0 + jnp.exp(-v))


def causal(flip):
    r = lax.broadcasted_iota(jnp.int32, (128, 128), 0)
    c = lax.broadcasted_iota(jnp.int32, (128, 128), 1)
    return (r <= c) if flip else (c <= r)


class Chain:
    def __init__(self, me, by, got, part, out, out_sem, in_sem, keep):
        self.me, self.by, self.got, self.part, self.out, self.out_sem, self.in_sem, self.keep = me, by, got, part, out, out_sem, in_sem, keep
        self.place = me.z if by == 1 else 3 - me.z

    def copy(self, i):
        s = lax.rem(i, 3)
        return send(self.out.at[s], self.got.at[i], self.out_sem.at[s], self.in_sem.at[i], self.me.z_peer(1 if self.by == 1 else 3))

    def tile(self, i):
        @pl.when(self.place > 0)
        def _(): self.copy(i).wait_recv()

        @pl.when(self.place < 3)
        def _():
            @pl.when(i >= 3)
            def _(): self.copy(i - 3).wait_send()
            s = lax.rem(i, 3)
            for g in range(2):
                self.out[s, g] = (self.keep(i, g) * self.got[i, g].astype(f32) + self.part[i, g]).astype(bf)
            self.copy(i).start()

    def start(self):
        @pl.when(self.place == 0)
        def _(): self.got[...] = jnp.zeros_like(self.got)

    def every_other(self, i):
        u = i - self.place
        @pl.when((u >= 0) & (u < 2 * TILES) & (lax.rem(u, 2) == 0))
        def _(): self.tile(u // 2)

    def four_of_seven(self, i):
        u = i - self.place
        m = lax.rem(u, 7)
        t = 4 * (u // 7) + (m + 1) // 2
        @pl.when((u >= 0) & (t < TILES) & ((m == 0) | (lax.rem(m, 2) == 1)))
        def _(): self.tile(t)

    def finish(self):
        @pl.when(self.place < 3)
        def _():
            for i in range(TILES - 3, TILES): self.copy(i).wait_send()

    @staticmethod
    def scratch():
        D = pltpu.SemaphoreType.DMA
        return [V((TILES, 2, 128, 256), bf), V((TILES, 2, 128, 256), f32), V((3, 2, 128, 256), bf), D((3,)), D((TILES,))]


def keeper(ds):
    def keep(i, g):
        end = 256 * g + 248
        return jnp.exp(spread(rolled(ds[end:end + 8], i))[7:8])
    return keep


V = pltpu.VMEM


def sb1_start(b_r, c_r, dst_acc, dc_acc, dds_acc, xu_acc, skips, st_s, ct_s):
    for a in (dst_acc, dc_acc, dds_acc, xu_acc, skips):
        a[...] = jnp.zeros_like(a)
    for g in range(2):
        b, c = b_r[256 * g:256 * g + 256], c_r[256 * g:256 * g + 256]
        st_s[g, 0] = mul(b[:128], c[:128], NT)
        st_s[g, 1] = mul(b[128:], c[128:], NT)
        st_s[g, 2] = mul(b[:128], c[128:], NT)
        ct_s[g] = c.T


def sb1_tile(j, mixed, z, dn, x, ent, gain, ds, step, dst, hp, rq, dxa_s, dz_o, dz_s, ol_o, lhs_s, rows_o,
             dst_acc, dc_acc, dds_acc, xu_acc, skips, st_s, ct_s, part):
    rds = rolled(ds[...], j)
    dsc = spread(rds)
    stc = spread(rolled(step[...], j))
    skip = spread(rolled(hp[...], j))[1:2]
    ok = causal(True)
    spot = spot_of(j)
    dgain = jnp.zeros((1, 256), f32)
    turned = []
    dskip = jnp.zeros((1, 256), f32)
    for g in range(2):
        r = slice(256 * g, 256 * g + 256)
        zz, mx, xx = z[0, r], mixed[0, r], x[0, r]
        dnr = jnp.concatenate([dn[0, r], dn[1, r]], 1)
        s = sig(zz)
        sil = zz * s
        gated = mx * sil
        rr, kk = (jnp.concatenate([rq[k, r]] * 2, 1) for k in (0, 1))
        gr = gated * rr
        ol = gr * gain[6:7]
        ol_o[r] = ol.astype(bf)
        turned.append(ol.T.astype(bf))
        dgain += jnp.sum(dnr * gr, axis=0, keepdims=True)
        dg = rr * (gain[6:7] * dnr) - gated * kk
        dy = dg * sil
        dz = (dg * mx * (s * (1.0 + zz * (1.0 - s)))).astype(bf)
        dz_o[0, r] = dz
        dz_s[r] = dz
        dskip += jnp.sum(dy * xx, axis=0, keepdims=True)
        d = dsc[r]
        eu = halves(jnp.exp(d) * dy)
        part[j, g] = mul(ct_s[g], eu)
        dc_acc[r] += mul(eu, ent[j, g], NT)
        dds_acc[r] += to_heads(dy * (mx - skip * xx), spot)
        xs = xx * stc[r]
        dp, xp = halves(dy), halves(xs)
        us = []
        for q in range(2):
            b = 256 * g + 128 * q
            lo = slice(128 * q, 128 * q + 128)
            u, acc = [], 0.0
            for m in range(2):
                e = []
                for h in (2 * m, 2 * m + 1):
                    gap = dst[j, h:h + 1, b:b + 128] - rds[b:b + 128, h:h + 1]
                    e.append(jnp.exp(jnp.where(ok, gap, -1e30)))
                w = jnp.concatenate([st_s[g, q] * e[0], st_s[g, q] * e[1]], 1)
                cols = slice(128 * m, 128 * m + 128)
                dh = heads_apart(part_of(dp, lo, cols))
                u.append(mul(w, dh))
                gt = mul(part_of(xp, lo, cols), dh, NT)
                acc = acc + (gt[:, :128] * e[0] + gt[:, 128:] * e[1])
            dst_acc[g, q] += acc
            us.append(jnp.concatenate(u, 1))
        mid = d[127:128]
        v = jnp.exp(mid - d[:128])
        ud = halves(jnp.exp(d[128:] - mid) * dy[128:])
        us[0] = us[0] + v * mul(st_s[g, 2], ud)
        dst_acc[g, 2] += mul(v * xs[:128], ud, NT)
        u = jnp.concatenate(us, 0)
        xu_acc[r] += to_heads(xx * u, spot)
        dxa_s[j, r] = skip * dy + stc[r] * u
    rows_o[j, 0:1] = dgain
    rows_o[j, 1:8] = jnp.zeros((7, 256), f32)
    skips[...] += to_heads(jnp.broadcast_to(dskip, (8, 256)), spot)
    turned = jnp.concatenate(turned, 1)
    for k in range(16):
        at = 16 * j + k
        q = at // 3
        owner, sub = q // 2, lax.rem(q, 2)
        rows = pl.ds(pl.multiple_of(lax.rem(at, 3) * 16, 16), 16)
        lhs_s[1 + sub, owner // 8, lax.rem(owner // 4, 2), lax.rem(owner, 4), rows] = turned[16 * k:16 * k + 16]


def conv_back(pad, dpad, dco, taps):
    w = taps.shape[1]
    grads = []
    for k in range(4):
        grads.append(sum(jnp.sum(dco[g] * pad[g, 5 + k:261 + k], axis=0, keepdims=True) for g in range(2)))
    grads.append(sum(jnp.sum(dco[g], axis=0, keepdims=True) for g in range(2)))
    grads.append(jnp.zeros((3, w), f32))
    din, prev = [], []
    for g in range(2):
        dpad[g, 0:8] = jnp.zeros((8, w), f32)
        dpad[g, 8:264] = dco[g]
        dpad[g, 264:272] = jnp.zeros((8, w), f32)
        din.append(sum(taps[k:k + 1] * dpad[g, 11 - k:267 - k] for k in range(4)))
        prev.append(sum(taps[k:k + 1] * dpad[g, 3 - k:11 - k] for k in range(4)))
    return jnp.concatenate(grads, 0), din, prev


def sb2_make(me, dcp_o, cg_o, hg_o, pad, pad2, dpad, dpad2, db_s, xut_s, de_s, prv, lst, edge_in, e_out, e_in):
    def edge(i):
        return send(prv.at[i], edge_in.at[i], e_out.at[i], e_in.at[i], me.z_peer(3))

    def pass_edge(i, prev, din):
        for g in range(2):
            lst[i, 8 * g:8 * g + 8] = din[g][248:]
        prv[i] = jnp.concatenate(prev, 0).astype(bf)

        @pl.when(me.z > 0)
        def _(): edge(i).start()

    def start():
        for a in (db_s, xut_s, de_s):
            a[...] = jnp.zeros_like(a)

    def tile(j, dxa_s, x, cin, halo, taps, got, ent, ds, step, b_r):
        dsc = spread(rolled(ds[...], j))
        stc = spread(rolled(step[...], j))
        spot = spot_of(j)
        fill_pad(pad, cin[0], halo[0])
        dco = []
        for g, co in enumerate(conv(pad, taps)):
            r = slice(256 * g, 256 * g + 256)
            d, xx, st, e = dsc[r], x[0, r], got[j, g], ent[j, g]
            tail = jnp.exp(d[255:256] - d)
            ut = tail * mul(b_r[r], st)
            xut_s[r] += to_heads(xx * ut, spot)
            db_s[r] += mul(tail * stc[r] * xx, st, NT)
            row = jnp.sum(st.astype(f32) * e.astype(f32), axis=0, keepdims=True)
            de_s[g] += to_heads(jnp.broadcast_to(row, (8, 256)), spot)
            dx = dxa_s[j, r] + stc[r] * ut
            s = sig(co)
            dco.append(dx * (s * (1.0 + co * (1.0 - s))))
        grads, din, prev = conv_back(pad, dpad, dco, taps)
        cg_o[j] = grads
        for g in range(2):
            dcp_o[j + 2, 256 * g:256 * g + 256] = din[g].astype(bf)
        pass_edge(j, prev, din)

    def final(bcin, bchalo, bctaps, raw, ds, step, b_r, c_r, hp, dst_acc, dc_acc, dds_acc, xu_acc, skips):
        fill_pad(pad2, bcin[0], bchalo[0])
        dco2 = []
        for g, co in enumerate(conv(pad2, bctaps)):
            r0 = 256 * g
            b, c = b_r[r0:r0 + 256], c_r[r0:r0 + 256]
            db, dc = db_s[r0:r0 + 256], dc_acc[r0:r0 + 256]
            db = db + jnp.concatenate([mul(dst_acc[g, 0], c[:128]) + mul(dst_acc[g, 2], c[128:]), mul(dst_acc[g, 1], c[128:])], 0)
            dc = dc + jnp.concatenate([mul(dst_acc[g, 0].T, b[:128]), mul(dst_acc[g, 1].T, b[128:]) + mul(dst_acc[g, 2].T, b[:128])], 0)
            s = sig(co)
            dco2.append(jnp.concatenate([db, dc], 1) * (s * (1.0 + co * (1.0 - s))))
        grads, din, prev = conv_back(pad2, dpad2, dco2, bctaps)
        cg_o[12] = grads
        for g in range(2):
            dcp_o[1, 256 * g:256 * g + 256] = din[g].astype(bf)
        pass_edge(TILES, prev, din)
        st = step[...]
        xut = xut_s[...]
        speed = -jnp.exp(hp[0:1])
        dds = dds_acc[...] - st * (xu_acc[...] + xut)
        lane = lax.broadcasted_iota(jnp.int32, (512, 128), 1)
        tok = lax.broadcasted_iota(jnp.int32, (256, 128), 0)
        rr = lax.broadcasted_iota(jnp.int32, (256, 256), 0)
        cc = lax.broadcasted_iota(jnp.int32, (256, 256), 1)
        up = (cc >= rr).astype(bf)
        drate = []
        for g in range(2):
            r = slice(256 * g, 256 * g + 256)
            end = jnp.sum(st[r] * xut[r], axis=0, keepdims=True) + de_s[g][0:1] * jnp.exp(ds[256 * g + 255:256 * g + 256])
            drate.append(mul_exact(up, dds[r] + jnp.where(tok == 255, end, 0.0)))
        drate = jnp.concatenate(drate, 0)
        dstep = xu_acc[...] + xut + drate * speed
        draw = jnp.where(lane < 48, dstep * sig(raw[0] + hp[2:3]), 0.0)
        dcp_o[0, :, 0:128] = draw.astype(bf)
        dcp_o[0, :, 128:256] = jnp.zeros((512, 128), bf)
        hg_o[0:1] = jnp.sum(drate * st * speed, axis=0, keepdims=True)
        hg_o[1:2] = skips[0:1]
        hg_o[2:3] = jnp.sum(draw, axis=0, keepdims=True)
        hg_o[3:8] = jnp.zeros((5, 128), f32)

        @pl.when(me.z < 3)
        def _():
            def patch(i, _):
                edge(i).wait_recv()
                for g in range(2):
                    rows = lst[i, 8 * g:8 * g + 8] + edge_in[i, 8 * g:8 * g + 8].astype(f32)
                    dcp_o[jnp.where(i < TILES, i + 2, 1), 256 * g + 248:256 * g + 256] = rows.astype(bf)
                return 0
            lax.fori_loop(0, TILES + 1, patch, 0)

        @pl.when(me.z > 0)
        def _(): lax.fori_loop(0, TILES + 1, lambda i, _: (edge(i).wait_send(), 0)[1], 0)

    return start, tile, final


S = jax.ShapeDtypeStruct
V = pltpu.VMEM


def const(*shape):
    return pl.BlockSpec(shape, lambda j: (0,) * len(shape), pipeline_mode=pl.Buffered(1))


BC = pl.BlockSpec((1, 512, 256), lambda j: (1, 0, 0), pipeline_mode=pl.Buffered(1))
BCH = pl.BlockSpec((1, 16, 256), lambda j: (1, 32, 0), pipeline_mode=pl.Buffered(1))
RAW = pl.BlockSpec((1, 512, 128), lambda j: (0, 0, 0), pipeline_mode=pl.Buffered(1))
BCT = pl.BlockSpec((8, 256), lambda j: (0, 12), pipeline_mode=pl.Buffered(1))


class Reduce:
    def __init__(self, me, n, rows, refs, skew):
        self.me, self.n, self.rows, self.sk, self.slots, self.ring = me, n, rows, skew, skew + 1, skew + 2
        (self.own1, self.own2, self.own3, self.s0, self.s1, self.s2, self.s3, self.r0, self.r1, self.r2, self.r3,
         self.o0, self.o1, self.o2, self.o3, self.i0, self.i1, self.i2, self.i3, self.free) = refs

    @staticmethod
    def scratch(n, rows, skew):
        V, D, k = pltpu.VMEM, pltpu.SemaphoreType.DMA, skew + 1
        z = 4 * rows
        return [V((k, 2, 2, z, 128), f32), V((k, 2, z, 128), f32), V((k, 2, rows, 128), f32),
                V((k, 2, 2, 2, z, 128), f32), V((k, 2, 2, z, 128), bf), V((k, 2, z, 128), bf), V((k, 3, 2, rows, 128), bf),
                V((skew + 2, 2, 2, 2, z, 128), f32), V((n, 2, 2, z, 128), bf), V((n, 2, z, 128), bf), V((n, 3, 2, rows, 128), bf),
                D((k,)), D((k, 2)), D((k, 2)), D((k, 3)), D((n,)), D((n, 2)), D((n, 2)), D((n, 3)), pltpu.SemaphoreType.REGULAR]

    def c0(self, i, s):
        return send(self.s0.at[s], self.r0.at[lax.rem(i, self.ring)], self.o0.at[s], self.i0.at[i], self.me.core_peer)

    def c1(self, i, s, h):
        return send(self.s1.at[s, h], self.r1.at[i, h], self.o1.at[s, h], self.i1.at[i, h], (self.me.x_peer, self.me.y_peer)[h])

    def c2(self, i, s, h):
        return send(self.s2.at[s, h], self.r2.at[i, h], self.o2.at[s, h], self.i2.at[i, h], (self.me.y_peer, self.me.x_peer)[h])

    def c3(self, i, s, k):
        return send(self.s3.at[s, k - 1], self.r3.at[i, k - 1], self.o3.at[s, k - 1], self.i3.at[i, k - 1], self.me.z_peer(k))

    def step(self, it, product, put):
        n, sk, ns, R = self.n, self.sk, self.slots, self.rows
        me, x, y, z, c = self.me, self.me.x, self.me.y, self.me.z, self.me.c

        def stage(lag, body):
            @pl.when((it >= lag * sk) & (it < n + lag * sk))
            def _():
                i = it - lag * sk
                body(i, lax.rem(i, ns))

        def zero(i, s):
            @pl.when(i >= ns)
            def _(): self.c0(i, s).wait_send()
            part = product(i, 1 - c, ((0, 0), (0, 1), (1, 0), (1, 1))).reshape(2, 2, 4 * R, 256)
            for h in range(2):
                self.s0[s, h] = part[..., h * 128:(h + 1) * 128]
            @pl.when(i >= self.ring)
            def _(): pl.semaphore_wait(self.free, 1)
            self.c0(i, s).start()

        def first(i, s):
            r0, own1, s1 = self.r0, self.own1, self.s1
            q = lax.rem(i, self.ring)
            @pl.when(i >= ns)
            def _():
                for h in range(2): self.c1(i, s, h).wait_send()
            blocks = [(yy, xx) for xx in (1 - x, x) for yy in (1 - y, y)]
            part = product(i, c, blocks)
            self.c0(i, s).wait_recv()
            for k, (yy, xx) in enumerate(blocks):
                a = part[k, :, :128] + r0[q, 0, yy, xx]
                b = part[k, :, 128:] + r0[q, 1, yy, xx]
                if k < 2:
                    s1[s, 0, yy] = a.astype(bf)
                else:
                    own1[s, 0, yy] = a
                if k % 2 == 0:
                    s1[s, 1, xx] = b.astype(bf)
                else:
                    own1[s, 1, xx] = b
                if k == 1:
                    self.c1(i, s, 0).start()
                if k == 2:
                    self.c1(i, s, 1).start()
            pl.semaphore_signal(self.free, inc=1, device_id=me.core_peer, device_id_type=MESH)

        def second(i, s):
            own1, r1 = self.own1, self.r1
            @pl.when(i >= ns)
            def _():
                for h in range(2): self.c2(i, s, h).wait_send()
            for h, g in ((0, y), (1, x)):
                self.c1(i, s, h).wait_recv()
                self.s2[s, h] = (own1[s, h, 1 - g] + r1[i, h, 1 - g].astype(f32)).astype(bf)
                self.c2(i, s, h).start()
                self.own2[s, h] = own1[s, h, g] + r1[i, h, g].astype(f32)

        def third(i, s):
            own2, r2 = self.own2, self.r2
            @pl.when(i >= ns)
            def _():
                for k in (1, 2, 3): self.c3(i, s, k).wait_send()
            for h in range(2): self.c2(i, s, h).wait_recv()
            for k in (2, 1, 3):
                rows = pl.ds(pl.multiple_of(lax.rem(z + k, 4) * R, 16), R)
                for h in range(2):
                    self.s3[s, k - 1, h] = (own2[s, h, rows] + r2[i, h, rows].astype(f32)).astype(bf)
                self.c3(i, s, k).start()
            rows = pl.ds(pl.multiple_of(z * R, 16), R)
            for h in range(2):
                self.own3[s, h] = own2[s, h, rows] + r2[i, h, rows].astype(f32)

        def last(i, s):
            for k in (1, 2, 3): self.c3(i, s, k).wait_recv()
            acc = self.own3[s]
            for k in range(3): acc = acc + self.r3[i, k].astype(f32)
            put(i, acc)

        stage(0, zero); stage(1, first); stage(2, second); stage(3, third); stage(4, last)

    def finish(self):
        for j in range(self.slots):
            i = self.n - self.slots + j
            s = i % self.slots
            self.c0(i, s).wait_send()
            for h in range(2):
                self.c1(i, s, h).wait_send()
                self.c2(i, s, h).wait_send()
            for k in (1, 2, 3): self.c3(i, s, k).wait_send()
        pl.semaphore_wait(self.free, self.ring)


def one_time(*shape):
    return pl.BlockSpec(shape, lambda j: (0,) * len(shape), pipeline_mode=pl.Buffered(1))


def phase_one(j):
    return jnp.minimum(j, TILES - 1)


def phase_two(j):
    return jnp.maximum(j - TILES, 0)


def back_call(mixed, proj, dn, x, par, ent, ds, step, dst, b, c, hp, rq, low_t, cot, collective_id):
    n, R, sk = 24, 48, 1

    def kernel(mixed, z, dn, x, gain, cin, halo, taps, ent, ds, step, dst, b_r, c_r, hp, rq, bcin, bchalo, bctaps, raw, low_t, cot,
               dz_o, ol_o, dcp_o, cg_o, hg_o, rows_o, zsum, osum,
               dst_acc, dc_acc, dds_acc, xu_acc, skips, st_s, ct_s, got, part, out, out_sem, in_sem,
               pad, pad2, dpad, dpad2, db_s, xut_s, de_s, prv, lst, edge_in, e_out, e_in,
               dxa_s, dz_s, rhs, lhs_s, *refs):
        j = pl.program_id(0)
        me = Place()
        line = Chain(me, -1, got, part, out, out_sem, in_sem, keeper(ds))
        red = Reduce(me, n, R, refs, sk)
        two_start, two_tile, two_final = sb2_make(me, dcp_o, cg_o, hg_o, pad, pad2, dpad, dpad2, db_s, xut_s, de_s, prv, lst, edge_in, e_out, e_in)

        def product(i, core, blocks):
            li = i // 12 * (1 + lax.rem(i, 2))
            rows = [lhs_s[li, 2 * yy + xx, core].reshape(4 * R, 512) for yy, xx in blocks]
            return jnp.dot(jnp.concatenate(rows, 0), rhs[lax.rem(i, 2)], preferred_element_type=f32).reshape(4, 4 * R, 256)

        def put(i, acc):
            both = jnp.concatenate([acc[0], acc[1]], 1)
            @pl.when(i < 12)
            def _(): zsum[:, pl.ds(pl.multiple_of(i * 256, 256), 256)] = both
            @pl.when(i >= 12)
            def _():
                k = i - 12
                osum[pl.ds(pl.multiple_of(lax.rem(k, 2) * 48, 16), 48), pl.ds(pl.multiple_of(k // 2 * 256, 256), 256)] = both

        def rs(it):
            @pl.when(it < 12)
            def _(): rhs[lax.rem(it, 2)] = dz_s[...]
            @pl.when((it >= 12) & (it < n))
            def _(): rhs[lax.rem(it, 2)] = cot[:, pl.ds(pl.multiple_of((it - 12) // 2 * 256, 256), 256)]
            red.step(it, product, put)

        @pl.when(j == 0)
        def _():
            greet(me.near())
            line.start()
            sb1_start(b_r, c_r, dst_acc, dc_acc, dds_acc, xu_acc, skips, st_s, ct_s)
            lhs_s[0] = low_t[...]

        @pl.when(j < TILES)
        def _():
            sb1_tile(j, mixed, z, dn, x, ent, gain, ds, step, dst, hp, rq, dxa_s, dz_o, dz_s, ol_o, lhs_s, rows_o,
                     dst_acc, dc_acc, dds_acc, xu_acc, skips, st_s, ct_s, part)
        line.four_of_seven(j)

        @pl.when(j == TILES)
        def _(): two_start()

        @pl.when(j >= TILES)
        def _(): two_tile(j - TILES, dxa_s, x, cin, halo, taps, got, ent, ds, step, b_r)

        rs(j)

        @pl.when(j == 2 * TILES - 1)
        def _():
            two_final(bcin, bchalo, bctaps, raw, ds, step, b_r, c_r, hp, dst_acc, dc_acc, dds_acc, xu_acc, skips)
            line.finish()
            lax.fori_loop(n, n + 4 * sk, lambda it, _: (rs(it), 0)[1], 0)
            red.finish()

    D = pltpu.SemaphoreType.DMA
    p1, p2 = phase_one, phase_two
    xt = lambda j: jnp.where(j < TILES, j, j - TILES)
    tok = one_time(512, 128)
    in_specs = [
        pl.BlockSpec((1, 512, 256), lambda j: (p1(j), 0, 0)),
        pl.BlockSpec((1, 512, 256), lambda j: (14 + p1(j), 0, 0)),
        pl.BlockSpec((2, 512, 128), lambda j: (p1(j), 0, 0)),
        pl.BlockSpec((1, 512, 256), lambda j: (xt(j), 0, 0)),
        pl.BlockSpec((8, 256), lambda j: (0, 19 + p1(j))),
        pl.BlockSpec((1, 512, 256), lambda j: (2 + p2(j), 0, 0)),
        pl.BlockSpec((1, 16, 256), lambda j: (2 + p2(j), 32, 0)),
        pl.BlockSpec((8, 256), lambda j: (0, p2(j))),
        one_time(12, 2, 128, 256), tok, tok, one_time(12, 8, 512), tok, tok, one_time(8, 128), one_time(2, 512, 128),
        BC, BCH, BCT, RAW, one_time(4, 2, 4, 48, 512), one_time(512, 1536),
    ]
    out_specs = (
        pl.BlockSpec((1, 512, 256), lambda j: (p1(j), 0, 0)),
        pl.BlockSpec((512, 256), lambda j: (0, p1(j))),
        one_time(14, 512, 256), one_time(13, 8, 256), one_time(8, 128), one_time(12, 8, 256), one_time(48, 3072), one_time(96, 1536),
    )
    out_shape = (S((12, 512, 256), bf), S((512, 3072), bf), S((14, 512, 256), bf), S((13, 8, 256), f32), S((8, 128), f32), S((12, 8, 256), f32), S((48, 3072), f32), S((96, 1536), f32))
    scratch = (
        [V((2, 3, 128, 128), f32), V((512, 128), f32), V((512, 128), f32), V((512, 128), f32), V((8, 128), f32), V((2, 3, 128, 128), f32), V((2, 128, 256), f32)]
        + Chain.scratch()
        + [V((2, 264, 256), f32), V((2, 264, 256), f32), V((2, 272, 256), f32), V((2, 272, 256), f32), V((512, 128), f32), V((512, 128), f32), V((2, 8, 128), f32),
           V((13, 16, 256), bf), V((13, 16, 256), f32), V((13, 16, 256), bf), D((13,)), D((13,))]
        + [V((12, 512, 256), f32), V((512, 256), bf), V((2, 512, 256), bf), V((3, 4, 2, 4, 48, 512), bf)]
        + Reduce.scratch(n, R, sk)
    )
    return pl.pallas_call(
        kernel, grid=(2 * TILES,), in_specs=in_specs, out_specs=out_specs, out_shape=out_shape, scratch_shapes=scratch,
        compiler_params=pltpu.CompilerParams(vmem_limit_bytes=63 << 20, collective_id=collective_id, has_side_effects=True), name="back",
    )(mixed, proj, dn, x, par, proj, proj, par, ent, ds, step, dst, b, c, hp, rq, proj, proj, par, proj, low_t.reshape(4, 2, 4, 48, 512), cot)


def end_call(low_t, dcp, dz, ol, win, wout, tok, cot, par, cg, rows, hg, collective_id, skew=2):
    n, R = 14, 48

    def kernel(lhs, dcp_ref, dz_ref, ol_ref, win_hbm, wout_hbm, tok, cot, par_ref, cg_ref, rows_ref, hg_ref, sums, blk, tg, small_o,
               wbuf, wsem, obuf, osem, dn, flat, mail, box, m_out, m_in, *refs):
        me = Place()
        def wcopy(t, p): return pltpu.make_async_copy(win_hbm.at[p], wbuf.at[lax.rem(t, 2), 0 if p is t else 1], wsem.at[lax.rem(t, 2), 0 if p is t else 1])
        def ocopy(i): return pltpu.make_async_copy(wout_hbm.at[i], obuf.at[lax.rem(i, 2)], osem.at[lax.rem(i, 2)])
        def fetch(t):
            wcopy(t, t).start()
            @pl.when(t < 12)
            def _(): wcopy(t, t + 14).start()
        fetch(jnp.int32(0))
        ocopy(jnp.int32(0)).start()
        ocopy(jnp.int32(1)).start()
        bar = pltpu.get_barrier_semaphore()
        def sg(k, _):
            pl.semaphore_signal(bar, inc=1, device_id=me.any_peer(k), device_id_type=MESH)
            return 0
        lax.fori_loop(1, 32, sg, 0)
        pl.semaphore_wait(bar, 31)
        red = Reduce(me, n, R, refs, skew)
        def post(k):
            to = lax.rem(me.line + k, 32)
            return send(mail.at[to], box.at[k - 1], m_out.at[k - 1], m_in.at[k - 1], me.any_peer(k))

        def tail():
            gain = par_ref[5:6, 3328:4864]
            def block(t, acc):
                r = pl.ds(pl.multiple_of(t * 64, 64), 64)
                xf = tok[r].astype(f32)
                h = lax.rsqrt(jnp.mean(xf * xf, axis=-1, keepdims=True) + 1e-5)
                d = dn[r]
                gd = d * gain
                tg[r] = cot[r].astype(f32) + (h * gd - xf * (h * h * h * jnp.mean(gd * xf, axis=-1, keepdims=True)))
                return acc + jnp.sum(d * xf * h, axis=0, keepdims=True)
            norm = lax.fori_loop(0, 8, block, jnp.zeros((1, 1536), f32))
            flat[...] = jnp.zeros_like(flat)
            for j in range(13):
                flat[0:5, 256 * j:256 * j + 256] = cg_ref[j, 0:5]
            flat[5:6, 0:1536] = norm
            for j in range(12):
                flat[6:7, 256 * j:256 * j + 256] = rows_ref[j, 0:1]
            turned = pltpu.roll(hg_ref[...], 64, 1)
            heads = jnp.concatenate([hg_ref[0:1] + turned[2:3], hg_ref[1:2]], 1)
            for o in range(32):
                b = [(o * w // 128) * 128 for w in (104, 48, 96)]
                mail[o, 0:5] = flat[0:5, b[0]:b[0] + 256]
                mail[o, 5:6] = flat[5:6, b[1]:b[1] + 256]
                mail[o, 6:7] = flat[6:7, b[2]:b[2] + 256]
                mail[o, 7:8] = heads
            lax.fori_loop(1, 32, lambda k, _: (post(k).start(), 0)[1], 0)

        def product(i, core, blocks):
            rows = [lhs[2 * yy + xx, core] for yy, xx in blocks]
            return jnp.dot(jnp.concatenate(rows, 0), dcp_ref[i], preferred_element_type=f32).reshape(4, 4 * R, 256)

        def put(i, acc):
            at = jnp.where(i == 0, 13 * 256, jnp.where(i == 1, 12 * 256, (i - 2) * 256))
            sums[:, pl.ds(pl.multiple_of(at, 256), 256)] = jnp.concatenate([acc[0], acc[1]], 1)

        def dgrad(t, q, dp):
            s = lax.rem(t, 2)
            w = jnp.concatenate([wbuf[s, q, h].reshape(1536, 128) for h in range(2)], axis=1)
            return lax.dot_general(dp, w, (((1,), (1,)), ((), ())), preferred_element_type=f32)

        def loop(it, _):
            red.step(it, product, put)
            @pl.when(it < n)
            def _():
                @pl.when(it + 1 < n)
                def _(): fetch(it + 1)
                wcopy(it, it).wait()
                r = dgrad(it, 0, dcp_ref[it])
                @pl.when(it == 0)
                def _(): dn[...] = r
                @pl.when(it > 0)
                def _(): dn[...] += r
            @pl.when(it < 12)
            def _():
                wcopy(it, it + 14).wait()
                dn[...] += dgrad(it, 1, dz_ref[it])
            @pl.when(it == n)
            def _(): tail()
            @pl.when((it >= n) & (it < n + 6))
            def _():
                i = it - n
                ocopy(i).wait()
                s = lax.rem(i, 2)
                w = jnp.concatenate([obuf[s, h].reshape(3072, 128) for h in range(2)], axis=1)
                at = pl.ds(pl.multiple_of(i * 256, 256), 256)
                blk[:, at] = (tok[:, at].astype(f32) + jnp.dot(ol_ref[...], w, preferred_element_type=f32)).astype(bf)
                @pl.when(i + 2 < 6)
                def _(): ocopy(i + 2).start()
            return 0
        lax.fori_loop(0, n + 4 * skew, loop, 0)
        small_o[...] = mail[me.line]
        def take(k, _):
            post(k).wait()
            small_o[...] += box[k - 1]
            return 0
        lax.fori_loop(1, 32, take, 0)
        red.finish()

    D, Sd = pltpu.SemaphoreType.DMA, jax.ShapeDtypeStruct
    vm, hb = pl.BlockSpec(memory_space=pltpu.VMEM), pl.BlockSpec(memory_space=pl.ANY)
    return pl.pallas_call(
        kernel, out_shape=(Sd((R, n * 256), f32), Sd((512, 1536), bf), Sd((512, 1536), f32), Sd((8, 256), f32)),
        in_specs=[vm] * 4 + [hb] * 2 + [vm] * 6, out_specs=(vm, vm, vm, vm),
        scratch_shapes=[V((2, 2, 2, 2, 2, 2, 192, 128), bf), D((2, 2)), V((2, 2, 2, 2, 2, 384, 128), bf), D((2,)),
                        V((512, 1536), f32), V((8, 3584), f32), V((32, 8, 256), f32), V((31, 8, 256), f32), D((31,)), D((31,))]
        + Reduce.scratch(n, R, skew),
        compiler_params=pltpu.CompilerParams(collective_id=collective_id, has_side_effects=True, vmem_limit_bytes=63 << 20), name="end",
    )(low_t.reshape(4, 2, 192, 512), dcp, dz, ol, win, wout, tok, cot, par, cg, rows, hg)


def dt_part(raw, hp, step_o, ds_o, dst_o):
    pre = raw + hp[2:3]
    step = jnp.maximum(pre, 0.0) + jnp.log1p(jnp.exp(-jnp.abs(pre)))
    rate = step * -jnp.exp(hp[0:1])
    step_o[...] = step
    r = lax.broadcasted_iota(jnp.int32, (256, 256), 0)
    c = lax.broadcasted_iota(jnp.int32, (256, 256), 1)
    low = (c <= r).astype(bf)
    for g in range(2):
        ds_o[256 * g:256 * g + 256] = mul_exact(low, rate[256 * g:256 * g + 256])
    turned = ds_o[...].T
    for p in range(TILES):
        dst_o[p, 0:4] = turned[4 * p:4 * p + 4]


def bc_part(block, taps, b_o, c_o, pad, s_s, bt_s):
    fill_pad(pad, block, block[512:528])
    for g, co in enumerate(conv(pad, taps)):
        act = co * sig(co)
        b, c = act[:, :128], act[:, 128:]
        b_o[256 * g:256 * g + 256] = b
        c_o[256 * g:256 * g + 256] = c
        bt_s[g] = b.T
        s_s[g, 0] = mul(c[:128], b[:128], NT)
        s_s[g, 1] = mul(c[128:], b[128:], NT)
        s_s[g, 2] = mul(c[128:], b[:128], NT)


def sf1_tile(j, block, taps, step, ds, dst, x_s, yi_s, part, pad, s_s, bt_s):
    fill_pad(pad, block, block[512:528])
    rds = rolled(ds[...], j)
    dsc = spread(rds)
    stc = spread(rolled(step[...], j))
    ok = causal(False)
    for g, co in enumerate(conv(pad, taps)):
        b0 = 256 * g
        x = co * sig(co)
        x_s[j, b0:b0 + 256] = x
        xs = x * stc[b0:b0 + 256]
        xp = halves(xs)
        d = dsc[b0:b0 + 256]
        ys = []
        for q in range(2):
            b = b0 + 128 * q
            y = []
            for m in range(2):
                w = []
                for h in (2 * m, 2 * m + 1):
                    gap = rds[b:b + 128, h:h + 1] - dst[j, h:h + 1, b:b + 128]
                    w.append(s_s[g, q] * jnp.exp(jnp.where(ok, gap, -1e30)))
                y.append(mul(jnp.concatenate(w, 1), heads_apart(part_of(xp, slice(128 * q, 128 * q + 128), slice(128 * m, 128 * m + 128)))))
            ys.append(jnp.concatenate(y, 1))
        mid = d[127:128]
        ys[1] = ys[1] + jnp.exp(d[128:] - mid) * mul(s_s[g, 2], jnp.exp(mid - d[:128]) * xs[:128])
        yi_s[j, b0:b0 + 128] = ys[0]
        yi_s[j, b0 + 128:b0 + 256] = ys[1]
        part[j, g] = mul(bt_s[g], jnp.exp(d[255:256] - d) * xs)


def sf2_tile(j, z, gain, ds, c_r, hp, x_s, yi_s, got, dn, a1, a2):
    dsc = spread(rolled(ds[...], j))
    skip = spread(rolled(hp[...], j))[1:2]
    for g in range(2):
        r = slice(256 * g, 256 * g + 256)
        mixed = yi_s[j, r] + jnp.exp(dsc[r]) * mul(c_r[r], got[j, g]) + skip * x_s[j, r]
        yi_s[j, r] = mixed
        gated = mixed * (z[r] * sig(z[r]))
        a1[r] += gated * gated
        a2[r] += gain * jnp.concatenate([dn[2 * j, r], dn[2 * j + 1, r]], 1) * gated


def front_call(in_proj, out_proj, conv_params, norm_gain, gate_gain, head_params, tokens, cotangent, collective_id, skew=2):
    NI, NO = 26, 6
    AT = [6400, 6144] + [3072 + 256 * p for p in range(12)] + [256 * p for p in range(12)]
    T, DM = tokens.shape
    TE = T + 16
    FIRST = NI - TILES
    Z0 = FIRST + NO

    def kernel(in_ref, out_ref, conv_ref, norm_ref, gate_ref, head_ref, tok_ref, cot_ref,
               proj_hbm, win, wout, x_hbm, mixed_hbm, low_hbm, dn_hbm, hp, par_ref, ent_o, step_o, ds_o, dst_o, b_o, c_o, rq_o,
               src_in, src_out, small_ref, edge_ref, low_t, sm, low_e, edge_in, pbuf, wbuf, obuf, x_s, yi_s, dn_ref, a1, a2, pad, s_s, bt_s, got, part, out, out_sem, in_sem, *sems):
        gs, os_, zs, (sm_out, sm_in, ed_out, ed_in, pb_sem, wl_sem, ol_sem, x_sem, mx_sem, dn_sem, low_sem) = sems[:9], sems[9:18], sems[18:27], sems[27:]
        me = Place()
        bar = pltpu.get_barrier_semaphore()
        def sg(k, _):
            pl.semaphore_signal(bar, inc=1, device_id=me.any_peer(k), device_id_type=MESH)
            return 0
        lax.fori_loop(1, 32, sg, 0)
        pl.semaphore_wait(bar, 31)
        ga = Gather(me, FIRST, src_in, win, gs, skew)
        gb = Gather(me, NO, src_out, wout, os_, skew)
        gz = Gather(me, NI - FIRST, src_in, win, zs, skew, FIRST)
        line = Chain(me, 1, got, part, out, out_sem, in_sem, keeper(ds_o))

        def take(p):
            if p == 0:
                src_in[0] = jnp.zeros((2, 48, 128), bf)
                src_in[0, 0, :, 0:48] = in_ref[:, 6400:6448].astype(bf)
            else:
                for h in range(2):
                    src_in[p, h] = in_ref[:, AT[p] + 128 * h:AT[p] + 128 * h + 128].astype(bf)
        small_ref[...] = jnp.zeros_like(small_ref)
        small_ref[0:5, 0:104] = conv_ref[...]
        small_ref[5:6, 0:48] = norm_ref[...]
        small_ref[6:7, 0:96] = gate_ref[...]
        row = lax.broadcasted_iota(jnp.int32, (8, 256), 0)
        first, second, third = (pltpu.roll(small_ref[...], lax.rem(me.line * w, 128), 1) for w in (104, 48, 96))
        small_ref[...] = jnp.where(row < 5, first, jnp.where(row == 5, second, third))
        row = lax.broadcasted_iota(jnp.int32, (16, DM), 0)
        ends = [tok_ref[256 * g + 240:256 * g + 256].astype(f32) for g in range(2)]
        edge_ref[...] = jnp.where(row < 8, pltpu.roll(ends[0], 3, 0), pltpu.roll(ends[1], 11, 0)).astype(bf)
        hp[...] = jnp.zeros_like(hp)
        hp[0:3, 0:48] = head_ref[...]
        take(0)
        take(1)

        def small_copy(k):
            return send(small_ref, sm.at[me.line], sm_out.at[k - 1], sm_in.at[k - 1], me.any_peer(k))
        def edge_copy():
            return send(edge_ref, edge_in, ed_out, ed_in, {"seq": lax.rem(me.z + 1, 4)})
        lax.fori_loop(1, 32, lambda k, _: (small_copy(k).start(), 0)[1], 0)
        edge_copy().start()
        sm[me.line] = small_ref[...]
        ga.step(0)
        ga.step(1)
        for p in range(2, NI): take(p)
        for p in range(NO):
            for h in range(2):
                src_out[p, h] = out_ref[:, 256 * p + 128 * h:256 * p + 128 * h + 128].astype(bf)
        line.start()
        a1[...] = jnp.zeros_like(a1)
        a2[...] = jnp.zeros_like(a2)
        par_ref[...] = jnp.zeros_like(par_ref)
        lax.fori_loop(1, 32, lambda k, _: (small_copy(k).wait(), 0)[1], 0)
        edge_copy().wait()
        for o in range(32):
            for base, width, stop in ((0, 104, 3328), (3328, 48, 4864), (4864, 96, 7936)):
                at = base + (o * width // 128) * 128
                wd = min(256, stop - at)
                par_ref[:, at:at + wd] += sm[o][:, :wd]
        gain = par_ref[5:6, 3328:4864]
        keep = (me.z > 0).astype(f32)

        def norm(v):
            v = v.astype(f32)
            return (v * lax.rsqrt(jnp.mean(v * v, axis=-1, keepdims=True) + 1e-5) * gain).astype(bf)
        def nloop(t, _):
            r = pl.ds(pl.multiple_of(t * 64, 64), 64)
            low_e[r] = norm(tok_ref[r])
            return 0
        lax.fori_loop(0, T // 64, nloop, 0)
        low_e[T:] = norm(edge_in[...].astype(f32) * keep)
        low_copy = pltpu.make_async_copy(low_t, low_hbm, low_sem)
        dn_copy = pltpu.make_async_copy(dn_ref, dn_hbm, dn_sem)

        def two(i): return lax.rem(i, 2)
        def pcopy(i): return pltpu.make_async_copy(pbuf.at[two(i)], proj_hbm.at[i], pb_sem.at[two(i)])
        def wload(i): return pltpu.make_async_copy(win.at[i], wbuf.at[two(i)], wl_sem.at[two(i)])
        def oload(i): return pltpu.make_async_copy(wout.at[i], obuf.at[two(i)], ol_sem.at[two(i)])
        def xcopy(j): return pltpu.make_async_copy(x_s.at[j], x_hbm.at[j], x_sem.at[j])
        def mcopy(j): return pltpu.make_async_copy(yi_s.at[j], mixed_hbm.at[j], mx_sem.at[j])
        def cols(base, j): return pl.ds(pl.multiple_of(base + j * 256, 128), 256)

        LAG = 4 * skew
        def chunk(i):
            s = two(i)
            wload(i).wait()
            @pl.when(i >= 2)
            def _(): pcopy(i - 2).wait()
            w = jnp.concatenate([wbuf[s, h].reshape(DM, 128) for h in range(2)], axis=1)
            pbuf[s] = jnp.dot(low_e[...], w, preferred_element_type=f32)
            pcopy(i).start()
            return pbuf.at[s]

        def loop(it, _):
            @pl.when(it >= 2)
            def _(): ga.step(it)
            gb.step(it - FIRST)
            gz.step(it - Z0)
            @pl.when((it >= 2) & (it < 6))
            def _():
                rows = pl.ds(pl.multiple_of((it - 2) * 128, 128), 128)
                low_t[:, rows] = low_e[rows].astype(f32).T.astype(bf)
            @pl.when(it == 6)
            def _(): low_copy.start()
            a = it - LAG
            @pl.when((a >= 0) & (a < FIRST))
            def _():
                ga.arrived(a)
                wload(a).start()
            @pl.when((a >= FIRST) & (a < Z0))
            def _():
                gb.arrived(a - FIRST)
                oload(a - FIRST).start()
            @pl.when((a >= Z0) & (a < Z0 + TILES))
            def _():
                gz.arrived(a - Z0)
                wload(a - NO).start()
            i = a - 1
            @pl.when((i >= 0) & (i < FIRST))
            def _():
                block = chunk(i)

                @pl.when(i == 0)
                def _(): dt_part(block[0:512, 0:128], hp, step_o, ds_o, dst_o)
                @pl.when(i == 1)
                def _(): bc_part(block, par_ref[:, 3072:3328], b_o, c_o, pad, s_s, bt_s)
                @pl.when(i >= 2)
                def _():
                    j = i - 2
                    sf1_tile(j, block, par_ref[:, cols(0, j)], step_o, ds_o, dst_o, x_s, yi_s, part, pad, s_s, bt_s)
                    xcopy(j).start()
            line.every_other(i - 2)
            @pl.when((i >= FIRST) & (i < Z0))
            def _():
                i2 = i - FIRST
                s = two(i2)
                oload(i2).wait()
                a_ = cot_ref[:, cols(0, i2)]
                def rows(q, _):
                    y = q // 4
                    x = lax.rem(q // 2, 2)
                    c = lax.rem(q, 2)
                    w = jnp.concatenate([obuf[s, h, y, x, c] for h in range(2)], axis=1)
                    r = lax.dot_general(a_, w, NT, preferred_element_type=f32)
                    for t in range(3):
                        rt = r[:, 128 * t:128 * t + 128]
                        @pl.when(i2 == 0)
                        def _(): dn_ref[3 * q + t] = rt
                        @pl.when(i2 > 0)
                        def _(): dn_ref[3 * q + t] += rt
                    return 0
                lax.fori_loop(0, 8, rows, 0)
                @pl.when(i2 == NO - 1)
                def _(): dn_copy.start()
            @pl.when(i >= Z0)
            def _():
                j = i - Z0
                block = chunk(i - NO)
                sf2_tile(j, block, par_ref[6:7, cols(4864, j)], ds_o, c_o, hp, x_s, yi_s, got, dn_ref, a1, a2)
                mcopy(j).start()
            return 0
        lax.fori_loop(0, NI + NO + LAG + 1, loop, 0)

        q = jnp.sum(a2[...], axis=1, keepdims=True) * (1.0 / 3072)
        r = lax.rsqrt(jnp.sum(a1[...], axis=1, keepdims=True) * (1.0 / 3072) + 1e-5)
        rq_o[0] = jnp.broadcast_to(r, (512, 128))
        rq_o[1] = jnp.broadcast_to(r * r * r * q, (512, 128))
        ent_o[...] = got[...]
        pcopy(NI - 2).wait()
        pcopy(NI - 1).wait()
        lax.fori_loop(0, TILES, lambda j, _: (mcopy(j).wait(), 0)[1], 0)
        lax.fori_loop(0, TILES, lambda j, _: (xcopy(j).wait(), 0)[1], 0)
        dn_copy.wait()
        low_copy.wait()
        line.finish()
        ga.finish()
        gb.finish()
        gz.finish()

    D = pltpu.SemaphoreType.DMA
    vm, hb = pl.BlockSpec(memory_space=pltpu.VMEM), pl.BlockSpec(memory_space=pl.ANY)
    wi, wo = (NI, 2, 2, 2, 2, 192, 128), (NO, 2, 2, 2, 2, 384, 128)
    tile = S((TILES, T, 256), f32)
    col = S((T, 128), f32)
    return pl.pallas_call(
        kernel,
        out_shape=(S((NI, TE, 256), f32), S(wi, bf), S(wo, bf), tile, tile, S((DM, T), bf), S((24, T, 128), f32), S((8, 128), f32), S((8, 7936), f32),
                   S((TILES, 2, 128, 256), bf), col, col, S((TILES, 8, T), f32), col, col, S((2, T, 128), f32)),
        in_specs=[vm] * 8,
        out_specs=(hb,) * 7 + (vm,) * 9,
        scratch_shapes=[V((NI, 2, 48, 128), bf), V((NO, 2, 96, 128), bf), V((8, 256), f32), V((16, DM), bf), V((DM, T), bf), V((32, 8, 256), f32), V((TE, DM), bf), V((16, DM), bf), V((2, TE, 256), f32), V((2,) + wi[1:], bf), V((2,) + wo[1:], bf),
                        V((TILES, T, 256), f32), V((TILES, T, 256), f32), V((24, T, 128), f32), V((T, 256), f32), V((T, 256), f32), V((2, 264, 256), f32), V((2, 3, 128, 128), f32), V((2, 128, 256), f32)]
        + Chain.scratch() + Gather.sems(FIRST, skew) + Gather.sems(NO, skew) + Gather.sems(TILES, skew)
        + [D((31,)), D((31,)), D, D, D((2,)), D((2,)), D((2,)), D((TILES,)), D((TILES,)), D, D],
        compiler_params=pltpu.CompilerParams(collective_id=collective_id, has_side_effects=True, vmem_limit_bytes=63 << 20),
        name="front",
    )(in_proj, out_proj, conv_params, norm_gain, gate_gain, head_params, tokens, cotangent)


def fast(adamw, tokens, cotangent, in_proj, in_mom, in_var, out_proj, out_mom, out_var, conv_params, conv_mom, conv_var,
         norm_gain, norm_mom, norm_var, gate_gain, gate_mom, gate_var, head_params, head_mom, head_var):
    line = lax.axis_index("dp") * 4 + lax.axis_index("seq")
    tok, cot = tokens.reshape(512, 1536), cotangent.reshape(512, 1536)
    proj, win, wout, x, mixed, low_t, dn, hp, par, ent, step, ds, dst, b, c, rq = front_call(
        in_proj, out_proj, conv_params, norm_gain[None], gate_gain[None], head_params, tok, cot, 1
    )
    dz, ol, dcp, cg, hg, rows, z_sum, out_grad = back_call(mixed, proj, dn, x, par, ent, ds, step, dst, b, c, hp, rq, low_t, cot, 5)
    last, block, tokens_grad, small_sum = end_call(low_t, dcp, dz, ol, win, wout, tok, cot, par, cg, rows, hg, 3)
    in_grad = jnp.concatenate([z_sum, last[:, :3376]], axis=1)
    tokens_grad = tokens_grad.reshape(2, 256, 1536)
    mine = lambda row, n, w: lax.dynamic_slice(small_sum, (row, lax.rem(line * w, 128)), (n, w))
    conv_grad, norm_grad, gate_grad = mine(0, 5, 104), mine(5, 1, 48)[0], mine(6, 1, 96)[0]
    head_grad = jnp.stack([small_sum[7, 0:48], small_sum[7, 128:176], small_sum[7, 64:112]])
    res = [(in_proj, in_mom, in_var, in_grad, 0.1), (out_proj, out_mom, out_var, out_grad, 0.1), (conv_params, conv_mom, conv_var, conv_grad, 0.1),
           (norm_gain, norm_mom, norm_var, norm_grad, 0.0), (gate_gain, gate_mom, gate_var, gate_grad, 0.0), (head_params, head_mom, head_var, head_grad, 0.0)]
    new = [v for a in res for v in adamw(*a)]
    return (block.reshape(2, 256, 1536), tokens_grad, in_grad, out_grad, conv_grad, norm_grad, gate_grad, head_grad, *new)


def solution(mesh):
    in_specs = (
        P("dp", "seq", None),
        P("dp", "seq", None),
        P(("dp", "seq"), None),
        P(("dp", "seq"), None),
        P(("dp", "seq"), None),
        P(("dp", "seq"), None),
        P(("dp", "seq"), None),
        P(("dp", "seq"), None),
        P(None, ("dp", "seq")),
        P(None, ("dp", "seq")),
        P(None, ("dp", "seq")),
        P(("dp", "seq")),
        P(("dp", "seq")),
        P(("dp", "seq")),
        P(("dp", "seq")),
        P(("dp", "seq")),
        P(("dp", "seq")),
        P(),
        P(),
        P(),
    )
    out_specs = (
        P("dp", "seq", None),
        P("dp", "seq", None),
        P(("dp", "seq"), None),
        P(("dp", "seq"), None),
        P(None, ("dp", "seq")),
        P(("dp", "seq")),
        P(("dp", "seq")),
        P(),
        P(("dp", "seq"), None),
        P(("dp", "seq"), None),
        P(("dp", "seq"), None),
        P(("dp", "seq"), None),
        P(("dp", "seq"), None),
        P(("dp", "seq"), None),
        P(None, ("dp", "seq")),
        P(None, ("dp", "seq")),
        P(None, ("dp", "seq")),
        P(("dp", "seq")),
        P(("dp", "seq")),
        P(("dp", "seq")),
        P(("dp", "seq")),
        P(("dp", "seq")),
        P(("dp", "seq")),
        P(),
        P(),
        P(),
    )
    own = tuple(mesh.shape[a] for a in ("dp", "seq")) == (8, 4)
    step = functools.partial(fast, adamw) if own else body
    return jax.shard_map(step, mesh=mesh, in_specs=in_specs, out_specs=out_specs, check_vma=False)
```

```python
import functools

import jax
import jax.numpy as jnp
from jax import lax
from jax.experimental import pallas as pl
from jax.experimental.pallas import tpu as pltpu
from jax.sharding import PartitionSpec as P

MESH = pl.DeviceIdType.MESH
bf = jnp.bfloat16
f32 = jnp.float32

DI = 3072
HEADS = 48
HEAD_DIM = 64
STATE = 128
KERNEL = 4
STEP = 3
CONV = 3328


highest = lax.Precision.HIGHEST
norm_eps = 1e-05
beta_one = 0.9
beta_two = 0.95
learn_rate = 0.01
decay_rate = 0.1
adam_eps = 1e-08


def from_behind(array, axis, by):
    size = lax.axis_size(axis)
    pairs = [(i, i + by) for i in range(size) if 0 <= i + by < size]
    return lax.ppermute(array, axis, pairs)


def entering(part, axis, combine, identity):
    place = lax.axis_index(axis)
    gathered = jax.tree.map(lambda a: lax.all_gather(a, axis), part)
    state = jax.tree.map(lambda a, e: jnp.zeros_like(a) + jnp.asarray(e, a.dtype), part, identity)

    def one(lap, state):
        return combine(
            state, jax.tree.map(lambda a: lax.dynamic_index_in_dim(a, lap, 0, False), gathered)
        )

    return lax.fori_loop(0, place, one, state)


def prefix(array, axis, combine, identity):
    size, here = (lax.axis_size(axis), lax.axis_index(axis))
    everything = jax.tree.map(
        lambda part, kind: lax.all_gather(part.astype(kind), axis),
        array,
        jax.tree.map(lambda a: jnp.bfloat16 if a.dtype == jnp.float32 else a.dtype, array),
    )
    start = jax.tree.map(
        lambda part, zero: jnp.broadcast_to(jnp.asarray(zero, part.dtype), part.shape),
        array,
        identity,
    )

    def lap(k, before):
        at = size - 1 - k
        reached = at > here
        new = combine(
            before, jax.tree.map(lambda part, own: part[at].astype(own.dtype), everything, array)
        )
        return jax.tree.map(lambda a, b: jnp.where(reached, a, b), new, before)

    return lax.fori_loop(0, size, lap, start)


def rms_scale(values, gain):
    return values * lax.rsqrt(jnp.mean(values * values, axis=-1, keepdims=True) + norm_eps) * gain


def adamw(weight, moment_one, moment_two, gradient, decay_on):
    one_new = beta_one * moment_one + (1.0 - beta_one) * gradient
    two_new = beta_two * moment_two + (1.0 - beta_two) * gradient * gradient
    mean_hat = one_new / (1.0 - beta_one**STEP)
    var_hat = two_new / (1.0 - beta_two**STEP)
    weight_new = weight - learn_rate * (
        mean_hat / (jnp.sqrt(var_hat) + adam_eps) + decay_on * weight
    )
    return (weight_new, one_new, two_new)


def fold_pair(earlier, later):
    decay_early, state_early = earlier
    decay_later, state_later = later
    return (decay_early * decay_later, decay_later[:, :, None, None] * state_early + state_later)


def intra_item(pieces):
    head_x, b_proj, c_proj, step_size, decay_sum = pieces
    length = decay_sum.shape[0]
    scores = jnp.dot(c_proj, b_proj.T, precision=highest)
    row_ids = lax.broadcasted_iota(jnp.int32, (length, length), 0)
    col_ids = lax.broadcasted_iota(jnp.int32, (length, length), 1)
    causal = (col_ids <= row_ids)[None, :, :]
    sums_by_head = decay_sum.T
    gap_sums = sums_by_head[:, :, None] - sums_by_head[:, None, :]
    decay_mat = jnp.exp(jnp.where(causal, gap_sums, -1e30))
    weights = scores[None, :, :] * decay_mat * step_size.T[:, None, :]
    return jnp.einsum("hts,shp->thp", weights, head_x, precision=highest)


def front(conv_in, previous, conv_weight, step_raw, head_weight):
    seq_count = conv_in.shape[0]
    length = conv_in.shape[1]
    padded = jnp.concatenate([previous, conv_in], axis=1)
    conv_out = conv_weight[KERNEL]
    for tap_index in range(KERNEL):
        conv_out = conv_out + conv_weight[tap_index] * padded[:, tap_index : tap_index + length, :]
    activated = jax.nn.silu(conv_out)
    head_x = activated[:, :, :DI].reshape(seq_count, length, HEADS, HEAD_DIM)
    b_proj = activated[:, :, DI : DI + STATE]
    c_proj = activated[:, :, DI + STATE :]
    step_size = jax.nn.softplus(step_raw + head_weight[2])
    decay_sum = jnp.cumsum(step_size * -jnp.exp(head_weight[0]), axis=1)
    last_sum = decay_sum[:, -1, :]
    tail_weight = jnp.exp(last_sum[:, None, :] - decay_sum) * step_size
    local_state = jnp.einsum("gsh,gshp,gsn->ghpn", tail_weight, head_x, b_proj, precision=highest)
    return (local_state, jnp.exp(last_sum), head_x, b_proj, c_proj, step_size, decay_sum)


def back(head_x, b_proj, c_proj, step_size, decay_sum, head_weight, gate_z, gate_weight, state_in):
    seq_count = gate_z.shape[0]
    length = gate_z.shape[1]
    inner_out = lax.map(jax.checkpoint(intra_item), (head_x, b_proj, c_proj, step_size, decay_sum))
    carried = jnp.exp(decay_sum)[..., None] * jnp.einsum(
        "gtn,ghpn->gthp", c_proj, state_in, precision=highest
    )
    mixed_y = inner_out + carried + head_weight[1][:, None] * head_x
    gated = mixed_y.reshape(seq_count, length, DI) * jax.nn.silu(gate_z)
    return rms_scale(gated, gate_weight)


def body(
    tokens,
    cotangent,
    in_proj,
    in_proj_mom,
    in_proj_var,
    out_proj,
    out_proj_mom,
    out_proj_var,
    conv_params,
    conv_mom,
    conv_var,
    norm_gain,
    norm_mom,
    norm_var,
    gate_gain,
    gate_mom,
    gate_var,
    head_params,
    head_mom,
    head_var,
):
    in_full, out_full = (
        lax.all_gather(in_proj.astype(jnp.bfloat16), ("dp", "seq"), axis=0, tiled=True),
        lax.all_gather(out_proj.astype(jnp.bfloat16), ("dp", "seq"), axis=0, tiled=True),
    )
    conv_full, norm_full, gate_full = (
        lax.all_gather(conv_params, ("dp", "seq"), axis=1, tiled=True),
        lax.all_gather(norm_gain, ("dp", "seq"), axis=0, tiled=True),
        lax.all_gather(gate_gain, ("dp", "seq"), axis=0, tiled=True),
    )
    length = tokens.shape[1]
    rim_start = length - (KERNEL - 1)
    inputs = tokens.astype(jnp.float32)
    normed_in, norm_pull = jax.vjp(rms_scale, inputs, norm_full)
    lowered = normed_in.astype(jnp.bfloat16)
    projected = jnp.einsum("gtd,dp->gtp", lowered, in_full, preferred_element_type=jnp.float32)
    gate_z = projected[:, :, :DI]
    conv_in = projected[:, :, DI : DI + CONV]
    step_raw = projected[:, :, DI + CONV :]
    previous = from_behind(conv_in[:, rim_start:, :], "seq", 1)
    front_out, front_pull = jax.vjp(front, conv_in, previous, conv_full, step_raw, head_params)
    local_state, decays, head_x, b_proj, c_proj, step_size, decay_sum = front_out
    unit_decay = jnp.ones_like(decays)
    zero_state = jnp.zeros_like(local_state)
    reached, state_in = entering((decays, local_state), "seq", fold_pair, (unit_decay, zero_state))
    out_normed, back_pull = jax.vjp(
        back, head_x, b_proj, c_proj, step_size, decay_sum, head_params, gate_z, gate_full, state_in
    )
    out_lowered = out_normed.astype(jnp.bfloat16)
    branch = jnp.einsum("gti,id->gtd", out_lowered, out_full, preferred_element_type=jnp.float32)
    block_out = (inputs + branch).astype(jnp.bfloat16)
    out_grad_local = jnp.einsum(
        "gti,gtd->id", out_lowered, cotangent, preferred_element_type=jnp.float32
    )
    d_normed = jnp.einsum("gtd,id->gti", cotangent, out_full, preferred_element_type=jnp.float32)
    (
        d_head_x,
        d_b_proj,
        d_c_proj,
        d_step,
        d_decay_sum,
        d_head_back,
        d_gate_z,
        d_gate_gain,
        d_state_in,
    ) = back_pull(d_normed)
    later_decay, d_state_out = prefix(
        (decays, d_state_in), "seq", fold_pair, (unit_decay, zero_state)
    )
    d_decays = jnp.sum(d_state_out * state_in, axis=(2, 3))
    d_conv_in, d_previous, d_conv, d_step_raw, d_head_front = front_pull(
        (d_state_out, d_decays, d_head_x, d_b_proj, d_c_proj, d_step, d_decay_sum)
    )
    returned = from_behind(d_previous.astype(jnp.bfloat16), "seq", -1).astype(d_previous.dtype)
    d_conv_in = jnp.concatenate(
        [d_conv_in[:, :rim_start, :], d_conv_in[:, rim_start:, :] + returned], axis=1
    )
    d_projected = jnp.concatenate([d_gate_z, d_conv_in, d_step_raw], axis=-1).astype(jnp.bfloat16)
    in_grad_local = jnp.einsum(
        "gtd,gtp->dp", lowered, d_projected, preferred_element_type=jnp.float32
    )
    d_normed_in = jnp.einsum(
        "gtp,dp->gtd", d_projected, in_full, preferred_element_type=jnp.float32
    )
    d_inputs, norm_grad_local = norm_pull(d_normed_in)
    tokens_grad = cotangent.astype(jnp.float32) + d_inputs
    head_grad = lax.psum(d_head_back + d_head_front, ("dp", "seq"))
    in_grad, out_grad, conv_grad, norm_grad, gate_grad = (
        lax.psum_scatter(in_grad_local, ("dp", "seq"), scatter_dimension=0, tiled=True),
        lax.psum_scatter(out_grad_local, ("dp", "seq"), scatter_dimension=0, tiled=True),
        lax.psum_scatter(d_conv, ("dp", "seq"), scatter_dimension=1, tiled=True),
        lax.psum_scatter(norm_grad_local, ("dp", "seq"), scatter_dimension=0, tiled=True),
        lax.psum_scatter(d_gate_gain, ("dp", "seq"), scatter_dimension=0, tiled=True),
    )
    in_new, in_mom_new, in_var_new = adamw(in_proj, in_proj_mom, in_proj_var, in_grad, decay_rate)
    out_new, out_mom_new, out_var_new = adamw(
        out_proj, out_proj_mom, out_proj_var, out_grad, decay_rate
    )
    conv_new, conv_mom_new, conv_var_new = adamw(
        conv_params, conv_mom, conv_var, conv_grad, decay_rate
    )
    norm_new, norm_mom_new, norm_var_new = adamw(norm_gain, norm_mom, norm_var, norm_grad, 0.0)
    gate_new, gate_mom_new, gate_var_new = adamw(gate_gain, gate_mom, gate_var, gate_grad, 0.0)
    head_new, head_mom_new, head_var_new = adamw(head_params, head_mom, head_var, head_grad, 0.0)
    return (
        block_out,
        tokens_grad,
        in_grad,
        out_grad,
        conv_grad,
        norm_grad,
        gate_grad,
        head_grad,
        in_new,
        in_mom_new,
        in_var_new,
        out_new,
        out_mom_new,
        out_var_new,
        conv_new,
        conv_mom_new,
        conv_var_new,
        norm_new,
        norm_mom_new,
        norm_var_new,
        gate_new,
        gate_mom_new,
        gate_var_new,
        head_new,
        head_mom_new,
        head_var_new,
    )


class Place:
    def __init__(self):
        self.dp = dp = lax.axis_index("dp")
        self.z = lax.axis_index("seq")
        self.c = c = lax.rem(dp, 2)
        self.x = x = lax.rem(dp // 2, 2)
        self.y = y = dp // 4
        self.line = dp * 4 + self.z
        self.core_peer = {"dp": dp + 1 - 2 * c}
        self.x_peer = {"dp": dp + 2 - 4 * x}
        self.y_peer = {"dp": dp + 4 - 8 * y}

    def z_peer(self, k):
        return {"seq": lax.rem(self.z + k, 4)}

    def any_peer(self, k):
        at = lax.rem(self.line + k, 32)
        return {"dp": at // 4, "seq": lax.rem(at, 4)}

    def near(self):
        return (self.core_peer, self.x_peer, self.y_peer, self.z_peer(1), self.z_peer(2), self.z_peer(3))


def greet(peers):
    bar = pltpu.get_barrier_semaphore()
    for peer in peers:
        pl.semaphore_signal(bar, inc=1, device_id=peer, device_id_type=MESH)
    pl.semaphore_wait(bar, len(peers))


def send(src, dst, out_sem, in_sem, peer):
    return pltpu.make_async_remote_copy(
        src_ref=src, dst_ref=dst, send_sem=out_sem, recv_sem=in_sem, device_id=peer, device_id_type=MESH
    )


class Gather:
    def __init__(self, me, n, src, w, sems, skew, base=0):
        self.base = base
        self.me, self.n, self.src, self.w, self.sk, self.slots = me, n, src, w, skew, skew + 1
        self.rows = src.shape[2]
        self.o1, self.o2, self.o3, self.o4, self.i1, self.i2, self.i3, self.i4, self.own = sems

    @staticmethod
    def sems(n, skew):
        D = pltpu.SemaphoreType.DMA
        return [D((skew + 1, 3)), D((skew + 1, 2)), D((skew + 1, 2)), D((skew + 1,)), D((n, 3)), D((n, 2)), D((n, 2)), D((n,)), D((skew + 1,))]

    def mine(self, i, s):
        m = self.me
        rows = pl.ds(pl.multiple_of(m.z * self.rows, 16), self.rows)
        return pltpu.make_async_copy(self.src.at[self.base + i], self.w.at[self.base + i, :, m.y, m.x, m.c, rows], self.own.at[s])

    def c1(self, i, s, k):
        m, w = self.me, self.w
        rows = pl.ds(pl.multiple_of(m.z * self.rows, 16), self.rows)
        return send(self.src.at[self.base + i], w.at[self.base + i, :, m.y, m.x, m.c, rows], self.o1.at[s, k - 1], self.i1.at[i, k - 1], m.z_peer(k))

    def c2(self, i, s, h):
        m, w = self.me, self.w
        part = w.at[self.base + i, h, m.y, m.x, m.c]
        return send(part, part, self.o2.at[s, h], self.i2.at[i, h], (m.y_peer, m.x_peer)[h])

    def c3(self, i, s, h):
        m, w = self.me, self.w
        part = w.at[self.base + i, 0, :, m.x, m.c] if h == 0 else w.at[self.base + i, 1, m.y, :, m.c]
        return send(part, part, self.o3.at[s, h], self.i3.at[i, h], (m.x_peer, m.y_peer)[h])

    def c4(self, i, s):
        m, w = self.me, self.w
        part = w.at[self.base + i, :, :, :, m.c]
        return send(part, part, self.o4.at[s], self.i4.at[i], m.core_peer)

    def step(self, it):
        n, sk, ns = self.n, self.sk, self.slots

        def stage(lag, body):
            @pl.when((it >= lag * sk) & (it < n + lag * sk))
            def _():
                i = it - lag * sk
                body(i, lax.rem(i, ns))

        def first(i, s):
            m = self.me
            @pl.when(i >= ns)
            def _():
                for k in (1, 2, 3): self.c1(i, s, k).wait_send()
            self.mine(i, s).start()
            for k in (2, 1, 3): self.c1(i, s, k).start()

        def second(i, s):
            @pl.when(i >= ns)
            def _():
                for h in range(2): self.c2(i, s, h).wait_send()
            self.mine(i, s).wait()
            for k in (1, 2, 3): self.c1(i, s, k).wait_recv()
            for h in range(2): self.c2(i, s, h).start()

        def third(i, s):
            @pl.when(i >= ns)
            def _():
                for h in range(2): self.c3(i, s, h).wait_send()
            for h in range(2):
                self.c2(i, s, h).wait_recv()
                self.c3(i, s, h).start()

        def fourth(i, s):
            @pl.when(i >= ns)
            def _(): self.c4(i, s).wait_send()
            for h in range(2): self.c3(i, s, h).wait_recv()
            self.c4(i, s).start()

        stage(0, first); stage(1, second); stage(2, third); stage(3, fourth)

    def arrived(self, i):
        self.c4(i, 0).wait_recv()

    def finish(self):
        for j in range(self.slots):
            i = self.n - self.slots + j
            s = i % self.slots
            for k in (1, 2, 3): self.c1(i, s, k).wait_send()
            for h in range(2):
                self.c2(i, s, h).wait_send()
                self.c3(i, s, h).wait_send()
            self.c4(i, s).wait_send()


TILES = 12
NN, NT, TN_ = (((1,), (0,)), ((), ())), (((1,), (1,)), ((), ())), (((0,), (0,)), ((), ()))


def one(a, b, dims):
    return lax.dot_general(a, b, dims, preferred_element_type=f32)


def halves(a):
    hi = a.astype(bf)
    return hi, (a - hi.astype(f32)).astype(bf)


def cross(a, b, dims=NN):
    (ah, al), (bh, bl) = (v if isinstance(v, tuple) else (v, None) for v in (a, b))
    out = one(ah, bh, dims)
    if bl is not None:
        out = out + one(ah, bl, dims)
    if al is not None:
        out = out + one(al, bh, dims)
    return out


def mul(a, b, dims=NN):
    return cross(*(v if isinstance(v, tuple) or v.dtype == bf else halves(v) for v in (a, b)), dims)


def mul_exact(a, b, dims=NN, left=True):
    v = b if left else a
    h = v.astype(bf)
    r = v - h.astype(f32)
    m = r.astype(bf)
    l = (r - m.astype(f32)).astype(bf)
    if left:
        a = a.astype(bf)
        return one(a, h, dims) + (one(a, m, dims) + one(a, l, dims))
    b = b.astype(bf)
    return one(h, b, dims) + (one(m, b, dims) + one(l, b, dims))


def to_heads(a, spot):
    return cross(halves(a), spot)


def rolled(a, j):
    return pltpu.roll(a, lax.rem(128 - 4 * j, 128), 1)


def spread(r):
    lane = lax.broadcasted_iota(jnp.int32, (r.shape[0], 128), 1)
    return jnp.concatenate([jnp.where(lane < 64, r[:, h:h + 1], r[:, h + 1:h + 2]) for h in (0, 2)], 1)


def by_head(v):
    lane = lax.broadcasted_iota(jnp.int32, v.shape, 1)
    zero = jnp.zeros_like(v)
    return jnp.concatenate([jnp.where(lane < 64, v, zero), jnp.where(lane >= 64, v, zero)], 0)


def heads_apart(pair):
    return tuple(by_head(v.astype(f32)).astype(bf) for v in pair)


def part_of(pair, *index):
    return tuple(v[index] for v in pair)


def spot_of(j):
    p = lax.broadcasted_iota(jnp.int32, (256, 128), 0)
    lane = lax.broadcasted_iota(jnp.int32, (256, 128), 1)
    return (lane == 4 * j + p // 64).astype(bf)


def fill_pad(pad, cin, halo):
    for g in range(2):
        pad[g, 5:8] = halo[8 * g:8 * g + 3]
        pad[g, 8:264] = cin[256 * g:256 * g + 256]


def conv(pad, taps):
    out = []
    for g in range(2):
        acc = taps[4:5]
        for k in range(4):
            acc = acc + taps[k:k + 1] * pad[g, 5 + k:261 + k]
        out.append(acc)
    return out


def sig(v):
    return 1.0 / (1.0 + jnp.exp(-v))


def causal(flip):
    r = lax.broadcasted_iota(jnp.int32, (128, 128), 0)
    c = lax.broadcasted_iota(jnp.int32, (128, 128), 1)
    return (r <= c) if flip else (c <= r)


class Chain:
    def __init__(self, me, by, got, part, out, out_sem, in_sem, keep):
        self.me, self.by, self.got, self.part, self.out, self.out_sem, self.in_sem, self.keep = me, by, got, part, out, out_sem, in_sem, keep
        self.place = me.z if by == 1 else 3 - me.z

    def copy(self, i):
        s = lax.rem(i, 3)
        return send(self.out.at[s], self.got.at[i], self.out_sem.at[s], self.in_sem.at[i], self.me.z_peer(1 if self.by == 1 else 3))

    def tile(self, i):
        @pl.when(self.place > 0)
        def _(): self.copy(i).wait_recv()

        @pl.when(self.place < 3)
        def _():
            @pl.when(i >= 3)
            def _(): self.copy(i - 3).wait_send()
            s = lax.rem(i, 3)
            for g in range(2):
                self.out[s, g] = (self.keep(i, g) * self.got[i, g].astype(f32) + self.part[i, g]).astype(bf)
            self.copy(i).start()

    def start(self):
        @pl.when(self.place == 0)
        def _(): self.got[...] = jnp.zeros_like(self.got)

    def every_other(self, i):
        u = i - self.place
        @pl.when((u >= 0) & (u < 2 * TILES) & (lax.rem(u, 2) == 0))
        def _(): self.tile(u // 2)

    def four_of_seven(self, i):
        u = i - self.place
        m = lax.rem(u, 7)
        t = 4 * (u // 7) + (m + 1) // 2
        @pl.when((u >= 0) & (t < TILES) & ((m == 0) | (lax.rem(m, 2) == 1)))
        def _(): self.tile(t)

    def finish(self):
        @pl.when(self.place < 3)
        def _():
            for i in range(TILES - 3, TILES): self.copy(i).wait_send()

    @staticmethod
    def scratch():
        D = pltpu.SemaphoreType.DMA
        return [V((TILES, 2, 128, 256), bf), V((TILES, 2, 128, 256), f32), V((3, 2, 128, 256), bf), D((3,)), D((TILES,))]


def keeper(ds):
    def keep(i, g):
        end = 256 * g + 248
        return jnp.exp(spread(rolled(ds[end:end + 8], i))[7:8])
    return keep


V = pltpu.VMEM


def sb1_start(b_r, c_r, dst_acc, dc_acc, dds_acc, xu_acc, skips, st_s, ct_s):
    for a in (dst_acc, dc_acc, dds_acc, xu_acc, skips):
        a[...] = jnp.zeros_like(a)
    for g in range(2):
        b, c = b_r[256 * g:256 * g + 256], c_r[256 * g:256 * g + 256]
        st_s[g, 0] = mul(b[:128], c[:128], NT)
        st_s[g, 1] = mul(b[128:], c[128:], NT)
        st_s[g, 2] = mul(b[:128], c[128:], NT)
        ct_s[g] = c.T


def sb1_tile(j, mixed, z, dn, x, ent, gain, ds, step, dst, hp, rq, dxa_s, dz_o, dz_s, ol_o, lhs_s, rows_o,
             dst_acc, dc_acc, dds_acc, xu_acc, skips, st_s, ct_s, part):
    rds = rolled(ds[...], j)
    dsc = spread(rds)
    stc = spread(rolled(step[...], j))
    skip = spread(rolled(hp[...], j))[1:2]
    ok = causal(True)
    spot = spot_of(j)
    dgain = jnp.zeros((1, 256), f32)
    turned = []
    dskip = jnp.zeros((1, 256), f32)
    for g in range(2):
        r = slice(256 * g, 256 * g + 256)
        zz, mx, xx = z[0, r], mixed[0, r], x[0, r]
        dnr = jnp.concatenate([dn[0, r], dn[1, r]], 1)
        s = sig(zz)
        sil = zz * s
        gated = mx * sil
        rr, kk = (jnp.concatenate([rq[k, r]] * 2, 1) for k in (0, 1))
        gr = gated * rr
        ol = gr * gain[6:7]
        ol_o[r] = ol.astype(bf)
        turned.append(ol.T.astype(bf))
        dgain += jnp.sum(dnr * gr, axis=0, keepdims=True)
        dg = rr * (gain[6:7] * dnr) - gated * kk
        dy = dg * sil
        dz = (dg * mx * (s * (1.0 + zz * (1.0 - s)))).astype(bf)
        dz_o[0, r] = dz
        dz_s[r] = dz
        dskip += jnp.sum(dy * xx, axis=0, keepdims=True)
        d = dsc[r]
        eu = halves(jnp.exp(d) * dy)
        part[j, g] = mul(ct_s[g], eu)
        dc_acc[r] += mul(eu, ent[j, g], NT)
        dds_acc[r] += to_heads(dy * (mx - skip * xx), spot)
        xs = xx * stc[r]
        dp, xp = halves(dy), halves(xs)
        us = []
        for q in range(2):
            b = 256 * g + 128 * q
            lo = slice(128 * q, 128 * q + 128)
            u, acc = [], 0.0
            for m in range(2):
                e = []
                for h in (2 * m, 2 * m + 1):
                    gap = dst[j, h:h + 1, b:b + 128] - rds[b:b + 128, h:h + 1]
                    e.append(jnp.exp(jnp.where(ok, gap, -1e30)))
                w = jnp.concatenate([st_s[g, q] * e[0], st_s[g, q] * e[1]], 1)
                cols = slice(128 * m, 128 * m + 128)
                dh = heads_apart(part_of(dp, lo, cols))
                u.append(mul(w, dh))
                gt = mul(part_of(xp, lo, cols), dh, NT)
                acc = acc + (gt[:, :128] * e[0] + gt[:, 128:] * e[1])
            dst_acc[g, q] += acc
            us.append(jnp.concatenate(u, 1))
        mid = d[127:128]
        v = jnp.exp(mid - d[:128])
        ud = halves(jnp.exp(d[128:] - mid) * dy[128:])
        us[0] = us[0] + v * mul(st_s[g, 2], ud)
        dst_acc[g, 2] += mul(v * xs[:128], ud, NT)
        u = jnp.concatenate(us, 0)
        xu_acc[r] += to_heads(xx * u, spot)
        dxa_s[j, r] = skip * dy + stc[r] * u
    rows_o[j, 0:1] = dgain
    rows_o[j, 1:8] = jnp.zeros((7, 256), f32)
    skips[...] += to_heads(jnp.broadcast_to(dskip, (8, 256)), spot)
    turned = jnp.concatenate(turned, 1)
    for k in range(16):
        at = 16 * j + k
        q = at // 3
        owner, sub = q // 2, lax.rem(q, 2)
        rows = pl.ds(pl.multiple_of(lax.rem(at, 3) * 16, 16), 16)
        lhs_s[1 + sub, owner // 8, lax.rem(owner // 4, 2), lax.rem(owner, 4), rows] = turned[16 * k:16 * k + 16]


def conv_back(pad, dpad, dco, taps):
    w = taps.shape[1]
    grads = []
    for k in range(4):
        grads.append(sum(jnp.sum(dco[g] * pad[g, 5 + k:261 + k], axis=0, keepdims=True) for g in range(2)))
    grads.append(sum(jnp.sum(dco[g], axis=0, keepdims=True) for g in range(2)))
    grads.append(jnp.zeros((3, w), f32))
    din, prev = [], []
    for g in range(2):
        dpad[g, 0:8] = jnp.zeros((8, w), f32)
        dpad[g, 8:264] = dco[g]
        dpad[g, 264:272] = jnp.zeros((8, w), f32)
        din.append(sum(taps[k:k + 1] * dpad[g, 11 - k:267 - k] for k in range(4)))
        prev.append(sum(taps[k:k + 1] * dpad[g, 3 - k:11 - k] for k in range(4)))
    return jnp.concatenate(grads, 0), din, prev


def sb2_make(me, dcp_o, cg_o, hg_o, pad, pad2, dpad, dpad2, db_s, xut_s, de_s, prv, lst, edge_in, e_out, e_in):
    def edge(i):
        return send(prv.at[i], edge_in.at[i], e_out.at[i], e_in.at[i], me.z_peer(3))

    def pass_edge(i, prev, din):
        for g in range(2):
            lst[i, 8 * g:8 * g + 8] = din[g][248:]
        prv[i] = jnp.concatenate(prev, 0).astype(bf)

        @pl.when(me.z > 0)
        def _(): edge(i).start()

    def start():
        for a in (db_s, xut_s, de_s):
            a[...] = jnp.zeros_like(a)

    def tile(j, dxa_s, x, cin, halo, taps, got, ent, ds, step, b_r):
        dsc = spread(rolled(ds[...], j))
        stc = spread(rolled(step[...], j))
        spot = spot_of(j)
        fill_pad(pad, cin[0], halo[0])
        dco = []
        for g, co in enumerate(conv(pad, taps)):
            r = slice(256 * g, 256 * g + 256)
            d, xx, st, e = dsc[r], x[0, r], got[j, g], ent[j, g]
            tail = jnp.exp(d[255:256] - d)
            ut = tail * mul(b_r[r], st)
            xut_s[r] += to_heads(xx * ut, spot)
            db_s[r] += mul(tail * stc[r] * xx, st, NT)
            row = jnp.sum(st.astype(f32) * e.astype(f32), axis=0, keepdims=True)
            de_s[g] += to_heads(jnp.broadcast_to(row, (8, 256)), spot)
            dx = dxa_s[j, r] + stc[r] * ut
            s = sig(co)
            dco.append(dx * (s * (1.0 + co * (1.0 - s))))
        grads, din, prev = conv_back(pad, dpad, dco, taps)
        cg_o[j] = grads
        for g in range(2):
            dcp_o[j + 2, 256 * g:256 * g + 256] = din[g].astype(bf)
        pass_edge(j, prev, din)

    def final(bcin, bchalo, bctaps, raw, ds, step, b_r, c_r, hp, dst_acc, dc_acc, dds_acc, xu_acc, skips, pause):
        fill_pad(pad2, bcin[0], bchalo[0])
        dco2 = []
        for g, co in enumerate(conv(pad2, bctaps)):
            r0 = 256 * g
            b, c = b_r[r0:r0 + 256], c_r[r0:r0 + 256]
            db, dc = db_s[r0:r0 + 256], dc_acc[r0:r0 + 256]
            db = db + jnp.concatenate([mul(dst_acc[g, 0], c[:128]) + mul(dst_acc[g, 2], c[128:]), mul(dst_acc[g, 1], c[128:])], 0)
            dc = dc + jnp.concatenate([mul(dst_acc[g, 0].T, b[:128]), mul(dst_acc[g, 1].T, b[128:]) + mul(dst_acc[g, 2].T, b[:128])], 0)
            s = sig(co)
            dco2.append(jnp.concatenate([db, dc], 1) * (s * (1.0 + co * (1.0 - s))))
        pause(0)
        grads, din, prev = conv_back(pad2, dpad2, dco2, bctaps)
        cg_o[12] = grads
        for g in range(2):
            dcp_o[1, 256 * g:256 * g + 256] = din[g].astype(bf)
        pass_edge(TILES, prev, din)
        pause(1)
        st = step[...]
        xut = xut_s[...]
        speed = -jnp.exp(hp[0:1])
        dds = dds_acc[...] - st * (xu_acc[...] + xut)
        lane = lax.broadcasted_iota(jnp.int32, (512, 128), 1)
        tok = lax.broadcasted_iota(jnp.int32, (256, 128), 0)
        rr = lax.broadcasted_iota(jnp.int32, (256, 256), 0)
        cc = lax.broadcasted_iota(jnp.int32, (256, 256), 1)
        up = (cc >= rr).astype(bf)
        drate = []
        for g in range(2):
            r = slice(256 * g, 256 * g + 256)
            end = jnp.sum(st[r] * xut[r], axis=0, keepdims=True) + de_s[g][0:1] * jnp.exp(ds[256 * g + 255:256 * g + 256])
            drate.append(mul_exact(up, dds[r] + jnp.where(tok == 255, end, 0.0)))
        drate = jnp.concatenate(drate, 0)
        dstep = xu_acc[...] + xut + drate * speed
        draw = jnp.where(lane < 48, dstep * sig(raw[0] + hp[2:3]), 0.0)
        dcp_o[0, :, 0:128] = draw.astype(bf)
        dcp_o[0, :, 128:256] = jnp.zeros((512, 128), bf)
        hg_o[0:1] = jnp.sum(drate * st * speed, axis=0, keepdims=True)
        hg_o[1:2] = skips[0:1]
        hg_o[2:3] = jnp.sum(draw, axis=0, keepdims=True)
        hg_o[3:8] = jnp.zeros((5, 128), f32)

        @pl.when(me.z < 3)
        def _():
            def patch(i, _):
                edge(i).wait_recv()
                for g in range(2):
                    rows = lst[i, 8 * g:8 * g + 8] + edge_in[i, 8 * g:8 * g + 8].astype(f32)
                    dcp_o[jnp.where(i < TILES, i + 2, 1), 256 * g + 248:256 * g + 256] = rows.astype(bf)
                return 0
            lax.fori_loop(0, TILES + 1, patch, 0)

        @pl.when(me.z > 0)
        def _(): lax.fori_loop(0, TILES + 1, lambda i, _: (edge(i).wait_send(), 0)[1], 0)

    return start, tile, final


S = jax.ShapeDtypeStruct
V = pltpu.VMEM


def const(*shape):
    return pl.BlockSpec(shape, lambda j: (0,) * len(shape), pipeline_mode=pl.Buffered(1))


BC = pl.BlockSpec((1, 512, 256), lambda j: (1, 0, 0), pipeline_mode=pl.Buffered(1))
BCH = pl.BlockSpec((1, 16, 256), lambda j: (1, 32, 0), pipeline_mode=pl.Buffered(1))
RAW = pl.BlockSpec((1, 512, 128), lambda j: (0, 0, 0), pipeline_mode=pl.Buffered(1))
BCT = pl.BlockSpec((8, 256), lambda j: (0, 12), pipeline_mode=pl.Buffered(1))


class Reduce:
    def __init__(self, me, n, rows, refs, skew):
        self.me, self.n, self.rows, self.sk, self.slots, self.ring = me, n, rows, skew, skew + 1, skew + 2
        (self.own1, self.own2, self.own3, self.s0, self.s1, self.s2, self.s3, self.r0, self.r1, self.r2, self.r3,
         self.o0, self.o1, self.o2, self.o3, self.i0, self.i1, self.i2, self.i3, self.free) = refs

    @staticmethod
    def scratch(n, rows, skew):
        V, D, k = pltpu.VMEM, pltpu.SemaphoreType.DMA, skew + 1
        z = 4 * rows
        return [V((k, 2, 2, z, 128), f32), V((k, 2, z, 128), f32), V((k, 2, rows, 128), f32),
                V((k, 2, 2, 2, z, 128), f32), V((k, 2, 2, z, 128), bf), V((k, 2, z, 128), bf), V((k, 3, 2, rows, 128), bf),
                V((skew + 2, 2, 2, 2, z, 128), f32), V((n, 2, 2, z, 128), bf), V((n, 2, z, 128), bf), V((n, 3, 2, rows, 128), bf),
                D((k,)), D((k, 2)), D((k, 2)), D((k, 3)), D((n,)), D((n, 2)), D((n, 2)), D((n, 3)), pltpu.SemaphoreType.REGULAR]

    def c0(self, i, s):
        return send(self.s0.at[s], self.r0.at[lax.rem(i, self.ring)], self.o0.at[s], self.i0.at[i], self.me.core_peer)

    def c1(self, i, s, h):
        return send(self.s1.at[s, h], self.r1.at[i, h], self.o1.at[s, h], self.i1.at[i, h], (self.me.x_peer, self.me.y_peer)[h])

    def c2(self, i, s, h):
        return send(self.s2.at[s, h], self.r2.at[i, h], self.o2.at[s, h], self.i2.at[i, h], (self.me.y_peer, self.me.x_peer)[h])

    def c3(self, i, s, k):
        return send(self.s3.at[s, k - 1], self.r3.at[i, k - 1], self.o3.at[s, k - 1], self.i3.at[i, k - 1], self.me.z_peer(k))

    def step(self, it, product, put):
        n, sk, ns, R = self.n, self.sk, self.slots, self.rows
        me, x, y, z, c = self.me, self.me.x, self.me.y, self.me.z, self.me.c

        def stage(lag, body):
            @pl.when((it >= lag * sk) & (it < n + lag * sk))
            def _():
                i = it - lag * sk
                body(i, lax.rem(i, ns))

        def zero(i, s):
            @pl.when(i >= ns)
            def _(): self.c0(i, s).wait_send()
            part = product(i, 1 - c, ((0, 0), (0, 1), (1, 0), (1, 1))).reshape(2, 2, 4 * R, 256)
            for h in range(2):
                self.s0[s, h] = part[..., h * 128:(h + 1) * 128]
            @pl.when(i >= self.ring)
            def _(): pl.semaphore_wait(self.free, 1)
            self.c0(i, s).start()

        def first(i, s):
            r0, own1, s1 = self.r0, self.own1, self.s1
            q = lax.rem(i, self.ring)
            @pl.when(i >= ns)
            def _():
                for h in range(2): self.c1(i, s, h).wait_send()
            blocks = [(yy, xx) for xx in (1 - x, x) for yy in (1 - y, y)]
            part = product(i, c, blocks)
            self.c0(i, s).wait_recv()
            for k, (yy, xx) in enumerate(blocks):
                a = part[k, :, :128] + r0[q, 0, yy, xx]
                b = part[k, :, 128:] + r0[q, 1, yy, xx]
                if k < 2:
                    s1[s, 0, yy] = a.astype(bf)
                else:
                    own1[s, 0, yy] = a
                if k % 2 == 0:
                    s1[s, 1, xx] = b.astype(bf)
                else:
                    own1[s, 1, xx] = b
                if k == 1:
                    self.c1(i, s, 0).start()
                if k == 2:
                    self.c1(i, s, 1).start()
            pl.semaphore_signal(self.free, inc=1, device_id=me.core_peer, device_id_type=MESH)

        def second(i, s):
            own1, r1 = self.own1, self.r1
            @pl.when(i >= ns)
            def _():
                for h in range(2): self.c2(i, s, h).wait_send()
            for h, g in ((0, y), (1, x)):
                self.c1(i, s, h).wait_recv()
                self.s2[s, h] = (own1[s, h, 1 - g] + r1[i, h, 1 - g].astype(f32)).astype(bf)
                self.c2(i, s, h).start()
                self.own2[s, h] = own1[s, h, g] + r1[i, h, g].astype(f32)

        def third(i, s):
            own2, r2 = self.own2, self.r2
            @pl.when(i >= ns)
            def _():
                for k in (1, 2, 3): self.c3(i, s, k).wait_send()
            for h in range(2): self.c2(i, s, h).wait_recv()
            for k in (2, 1, 3):
                rows = pl.ds(pl.multiple_of(lax.rem(z + k, 4) * R, 16), R)
                for h in range(2):
                    self.s3[s, k - 1, h] = (own2[s, h, rows] + r2[i, h, rows].astype(f32)).astype(bf)
                self.c3(i, s, k).start()
            rows = pl.ds(pl.multiple_of(z * R, 16), R)
            for h in range(2):
                self.own3[s, h] = own2[s, h, rows] + r2[i, h, rows].astype(f32)

        def last(i, s):
            for k in (1, 2, 3): self.c3(i, s, k).wait_recv()
            acc = self.own3[s]
            for k in range(3): acc = acc + self.r3[i, k].astype(f32)
            put(i, acc)

        stage(0, zero); stage(1, first); stage(2, second); stage(3, third); stage(4, last)

    def finish(self):
        for j in range(self.slots):
            i = self.n - self.slots + j
            s = i % self.slots
            self.c0(i, s).wait_send()
            for h in range(2):
                self.c1(i, s, h).wait_send()
                self.c2(i, s, h).wait_send()
            for k in (1, 2, 3): self.c3(i, s, k).wait_send()
        pl.semaphore_wait(self.free, self.ring)


def one_time(*shape):
    return pl.BlockSpec(shape, lambda j: (0,) * len(shape), pipeline_mode=pl.Buffered(1))


def phase_one(j):
    return jnp.minimum(j, TILES - 1)


def phase_two(j):
    return jnp.maximum(j - TILES, 0)


def back_call(mixed, proj, dn, x, par, ent, ds, step, dst, b, c, hp, rq, low_t, cot, collective_id):
    n, R, sk = 24, 48, 1

    def kernel(mixed, z, dn, x, gain, cin, halo, taps, ent, ds, step, dst, b_r, c_r, hp, rq, bcin, bchalo, bctaps, raw, low_h, cot_h,
               dz_o, ol_o, dcp_o, cg_o, hg_o, rows_o, zsum, osum,
               dst_acc, dc_acc, dds_acc, xu_acc, skips, st_s, ct_s, got, part, out, out_sem, in_sem,
               pad, pad2, dpad, dpad2, db_s, xut_s, de_s, prv, lst, edge_in, e_out, e_in,
               dxa_s, dz_s, rhs, lhs_s, cot, low_sem, cot_sem, *refs):
        j = pl.program_id(0)
        me = Place()
        line = Chain(me, -1, got, part, out, out_sem, in_sem, keeper(ds))
        red = Reduce(me, n, R, refs, sk)
        two_start, two_tile, two_final = sb2_make(me, dcp_o, cg_o, hg_o, pad, pad2, dpad, dpad2, db_s, xut_s, de_s, prv, lst, edge_in, e_out, e_in)

        low_copy = pltpu.make_async_copy(low_h, lhs_s.at[0], low_sem)
        cot_copy = pltpu.make_async_copy(cot_h, cot, cot_sem)

        def product(i, core, blocks):
            li = i // 12 * (1 + lax.rem(i, 2))
            rows = [lhs_s[li, 2 * yy + xx, core].reshape(4 * R, 512) for yy, xx in blocks]
            return jnp.dot(jnp.concatenate(rows, 0), rhs[lax.rem(i, 2)], preferred_element_type=f32).reshape(4, 4 * R, 256)

        def put(i, acc):
            both = jnp.concatenate([acc[0], acc[1]], 1)
            @pl.when(i < 12)
            def _(): zsum[:, pl.ds(pl.multiple_of(i * 256, 256), 256)] = both
            @pl.when(i >= 12)
            def _():
                k = i - 12
                osum[pl.ds(pl.multiple_of(lax.rem(k, 2) * 48, 16), 48), pl.ds(pl.multiple_of(k // 2 * 256, 256), 256)] = both

        def rs(it):
            @pl.when(it < 12)
            def _(): rhs[lax.rem(it, 2)] = dz_s[...]
            @pl.when(it == 12)
            def _(): cot_copy.wait()
            @pl.when((it >= 12) & (it < n))
            def _(): rhs[lax.rem(it, 2)] = cot[:, pl.ds(pl.multiple_of((it - 12) // 2 * 256, 256), 256)]
            red.step(it, product, put)

        @pl.when(j == 0)
        def _():
            low_copy.start()
            cot_copy.start()
            greet(me.near())
            line.start()
            sb1_start(b_r, c_r, dst_acc, dc_acc, dds_acc, xu_acc, skips, st_s, ct_s)
            low_copy.wait()

        @pl.when(j < TILES)
        def _():
            sb1_tile(j, mixed, z, dn, x, ent, gain, ds, step, dst, hp, rq, dxa_s, dz_o, dz_s, ol_o, lhs_s, rows_o,
                     dst_acc, dc_acc, dds_acc, xu_acc, skips, st_s, ct_s, part)
        line.four_of_seven(j)

        @pl.when(j == TILES)
        def _(): two_start()

        @pl.when(j >= TILES)
        def _(): two_tile(j - TILES, dxa_s, x, cin, halo, taps, got, ent, ds, step, b_r)

        rs(j)

        @pl.when(j == 2 * TILES - 1)
        def _():
            two_final(bcin, bchalo, bctaps, raw, ds, step, b_r, c_r, hp, dst_acc, dc_acc, dds_acc, xu_acc, skips, lambda k: rs(jnp.int32(n + k)))
            line.finish()
            lax.fori_loop(n + 2, n + 4 * sk, lambda it, _: (rs(it), 0)[1], 0)
            red.finish()

    D = pltpu.SemaphoreType.DMA
    p1, p2 = phase_one, phase_two
    xt = lambda j: jnp.where(j < TILES, j, j - TILES)
    tok = one_time(512, 128)
    in_specs = [
        pl.BlockSpec((1, 512, 256), lambda j: (p1(j), 0, 0)),
        pl.BlockSpec((1, 512, 256), lambda j: (14 + p1(j), 0, 0)),
        pl.BlockSpec((2, 512, 128), lambda j: (p1(j), 0, 0)),
        pl.BlockSpec((1, 512, 256), lambda j: (xt(j), 0, 0)),
        pl.BlockSpec((8, 256), lambda j: (0, 19 + p1(j))),
        pl.BlockSpec((1, 512, 256), lambda j: (2 + p2(j), 0, 0)),
        pl.BlockSpec((1, 16, 256), lambda j: (2 + p2(j), 32, 0)),
        pl.BlockSpec((8, 256), lambda j: (0, p2(j))),
        one_time(12, 2, 128, 256), tok, tok, one_time(12, 8, 512), tok, tok, one_time(8, 128), one_time(2, 512, 128),
        BC, BCH, BCT, RAW, pl.BlockSpec(memory_space=pl.ANY), pl.BlockSpec(memory_space=pl.ANY),
    ]
    out_specs = (
        pl.BlockSpec((1, 512, 256), lambda j: (p1(j), 0, 0)),
        pl.BlockSpec((512, 256), lambda j: (0, p1(j))),
        one_time(14, 512, 256), one_time(13, 8, 256), one_time(8, 128), one_time(12, 8, 256), one_time(48, 3072), one_time(96, 1536),
    )
    out_shape = (S((12, 512, 256), bf), S((512, 3072), bf), S((14, 512, 256), bf), S((13, 8, 256), f32), S((8, 128), f32), S((12, 8, 256), f32), S((48, 3072), f32), S((96, 1536), f32))
    scratch = (
        [V((2, 3, 128, 128), f32), V((512, 128), f32), V((512, 128), f32), V((512, 128), f32), V((8, 128), f32), V((2, 3, 128, 128), f32), V((2, 128, 256), f32)]
        + Chain.scratch()
        + [V((2, 264, 256), f32), V((2, 264, 256), f32), V((2, 272, 256), f32), V((2, 272, 256), f32), V((512, 128), f32), V((512, 128), f32), V((2, 8, 128), f32),
           V((13, 16, 256), bf), V((13, 16, 256), f32), V((13, 16, 256), bf), D((13,)), D((13,))]
        + [V((12, 512, 256), f32), V((512, 256), bf), V((2, 512, 256), bf), V((3, 4, 2, 4, 48, 512), bf), V((512, 1536), bf), D, D]
        + Reduce.scratch(n, R, sk)
    )
    return pl.pallas_call(
        kernel, grid=(2 * TILES,), in_specs=in_specs, out_specs=out_specs, out_shape=out_shape, scratch_shapes=scratch,
        compiler_params=pltpu.CompilerParams(vmem_limit_bytes=63 << 20, collective_id=collective_id, has_side_effects=True), name="back",
    )(mixed, proj, dn, x, par, proj, proj, par, ent, ds, step, dst, b, c, hp, rq, proj, proj, par, proj, low_t.reshape(4, 2, 4, 48, 512), cot)


def end_call(low_t, dcp, dz, ol, win, wout, tok, cot, par, cg, rows, hg, collective_id, skew=2):
    n, R = 14, 48

    def kernel(lhs_h, dcp_h, dz_h, ol_h, win_hbm, wout_hbm, tok_h, cot_h, par_ref, cg_ref, rows_ref, hg_ref, sums, blk_h, tg_h, small_o,
               lhs, dcp_ref, dz_ref, ol_ref, tok, cot, blk, tg, in_sem, dcp_sem, dz_sem, out_sem, wbuf, wsem, obuf, osem, dn, flat, mail, box, m_out, m_in, *refs):
        me = Place()
        def wcopy(t, p): return pltpu.make_async_copy(win_hbm.at[p], wbuf.at[lax.rem(t, 2), 0 if p is t else 1], wsem.at[lax.rem(t, 2), 0 if p is t else 1])
        def ocopy(i): return pltpu.make_async_copy(wout_hbm.at[i], obuf.at[lax.rem(i, 2)], osem.at[lax.rem(i, 2)])
        def fetch(t):
            wcopy(t, t).start()
            @pl.when(t < 12)
            def _(): wcopy(t, t + 14).start()
        def dcp_copy(p): return pltpu.make_async_copy(dcp_h.at[p], dcp_ref.at[p], dcp_sem.at[p])
        def dz_copy(p): return pltpu.make_async_copy(dz_h.at[p], dz_ref.at[p], dz_sem.at[p])
        whole = [pltpu.make_async_copy(a, b, in_sem.at[k]) for k, (a, b) in enumerate(((lhs_h, lhs), (tok_h, tok), (cot_h, cot), (ol_h, ol_ref)))]
        tg_copy = pltpu.make_async_copy(tg, tg_h, out_sem.at[0])
        blk_copy = pltpu.make_async_copy(blk, blk_h, out_sem.at[1])
        whole[0].start()
        fetch(jnp.int32(0))
        def pull(p, _):
            dcp_copy(p).start()
            @pl.when(p < 12)
            def _(): dz_copy(p).start()
            return 0
        lax.fori_loop(0, n, pull, 0)
        for copy in whole[1:]: copy.start()
        ocopy(jnp.int32(0)).start()
        ocopy(jnp.int32(1)).start()
        bar = pltpu.get_barrier_semaphore()
        def sg(k, _):
            pl.semaphore_signal(bar, inc=1, device_id=me.any_peer(k), device_id_type=MESH)
            return 0
        lax.fori_loop(1, 32, sg, 0)
        pl.semaphore_wait(bar, 31)
        red = Reduce(me, n, R, refs, skew)
        def post(k):
            to = lax.rem(me.line + k, 32)
            return send(mail.at[to], box.at[k - 1], m_out.at[k - 1], m_in.at[k - 1], me.any_peer(k))

        def tail():
            gain = par_ref[5:6, 3328:4864]
            def block(t, acc):
                r = pl.ds(pl.multiple_of(t * 64, 64), 64)
                xf = tok[r].astype(f32)
                h = lax.rsqrt(jnp.mean(xf * xf, axis=-1, keepdims=True) + 1e-5)
                d = dn[r]
                gd = d * gain
                tg[r] = cot[r].astype(f32) + (h * gd - xf * (h * h * h * jnp.mean(gd * xf, axis=-1, keepdims=True)))
                return acc + jnp.sum(d * xf * h, axis=0, keepdims=True)
            norm = lax.fori_loop(0, 8, block, jnp.zeros((1, 1536), f32))
            flat[...] = jnp.zeros_like(flat)
            for j in range(13):
                flat[0:5, 256 * j:256 * j + 256] = cg_ref[j, 0:5]
            flat[5:6, 0:1536] = norm
            for j in range(12):
                flat[6:7, 256 * j:256 * j + 256] = rows_ref[j, 0:1]
            turned = pltpu.roll(hg_ref[...], 64, 1)
            heads = jnp.concatenate([hg_ref[0:1] + turned[2:3], hg_ref[1:2]], 1)
            for o in range(32):
                b = [(o * w // 128) * 128 for w in (104, 48, 96)]
                mail[o, 0:5] = flat[0:5, b[0]:b[0] + 256]
                mail[o, 5:6] = flat[5:6, b[1]:b[1] + 256]
                mail[o, 6:7] = flat[6:7, b[2]:b[2] + 256]
                mail[o, 7:8] = heads
            lax.fori_loop(1, 32, lambda k, _: (post(k).start(), 0)[1], 0)

        def product(i, core, blocks):
            rows = [lhs[2 * yy + xx, core] for yy, xx in blocks]
            return jnp.dot(jnp.concatenate(rows, 0), dcp_ref[i], preferred_element_type=f32).reshape(4, 4 * R, 256)

        def put(i, acc):
            at = jnp.where(i == 0, 13 * 256, jnp.where(i == 1, 12 * 256, (i - 2) * 256))
            sums[:, pl.ds(pl.multiple_of(at, 256), 256)] = jnp.concatenate([acc[0], acc[1]], 1)

        def weights(t, q):
            return jnp.concatenate([wbuf[lax.rem(t, 2), q, h].reshape(1536, 128) for h in range(2)], axis=1)

        def loop(it, _):
            @pl.when(it < n)
            def _(): dcp_copy(it).wait()
            @pl.when(it < 12)
            def _(): dz_copy(it).wait()
            red.step(it, product, put)
            @pl.when(it < n)
            def _():
                @pl.when(it + 1 < n)
                def _(): fetch(it + 1)
                wcopy(it, it).wait()
            @pl.when(it < 12)
            def _():
                wcopy(it, it + 14).wait()
                both = jnp.concatenate([dcp_ref[it], dz_ref[it]], 1)
                dn[...] += lax.dot_general(both, jnp.concatenate([weights(it, 0), weights(it, 1)], 1), NT, preferred_element_type=f32)
            @pl.when((it >= 12) & (it < n))
            def _():
                dn[...] += lax.dot_general(dcp_ref[it], weights(it, 0), NT, preferred_element_type=f32)
            @pl.when(it == n)
            def _():
                for copy in whole[1:]: copy.wait()
                tail()
                tg_copy.start()
            @pl.when((it >= n) & (it < n + 6))
            def _():
                i = it - n
                ocopy(i).wait()
                s = lax.rem(i, 2)
                w = jnp.concatenate([obuf[s, h].reshape(3072, 128) for h in range(2)], axis=1)
                at = pl.ds(pl.multiple_of(i * 256, 256), 256)
                blk[:, at] = (tok[:, at].astype(f32) + jnp.dot(ol_ref[...], w, preferred_element_type=f32)).astype(bf)
                @pl.when(i + 2 < 6)
                def _(): ocopy(i + 2).start()
            @pl.when(it == n + 5)
            def _(): blk_copy.start()
            return 0
        dn[...] = jnp.zeros_like(dn)
        whole[0].wait()
        lax.fori_loop(0, n + 4 * skew, loop, 0)
        small_o[...] = mail[me.line]
        def take(k, _):
            post(k).wait()
            small_o[...] += box[k - 1]
            return 0
        lax.fori_loop(1, 32, take, 0)
        tg_copy.wait()
        blk_copy.wait()
        red.finish()

    D, Sd = pltpu.SemaphoreType.DMA, jax.ShapeDtypeStruct
    vm, hb = pl.BlockSpec(memory_space=pltpu.VMEM), pl.BlockSpec(memory_space=pl.ANY)
    return pl.pallas_call(
        kernel, out_shape=(Sd((R, n * 256), f32), Sd((512, 1536), bf), Sd((512, 1536), f32), Sd((8, 256), f32)),
        in_specs=[hb] * 8 + [vm] * 4, out_specs=(vm, hb, hb, vm),
        scratch_shapes=[V((4, 2, 192, 512), bf), V((14, 512, 256), bf), V((12, 512, 256), bf), V((512, 3072), bf), V((512, 1536), bf), V((512, 1536), bf), V((512, 1536), bf), V((512, 1536), f32),
                        D((4,)), D((14,)), D((12,)), D((2,)), V((2, 2, 2, 2, 2, 2, 192, 128), bf), D((2, 2)), V((2, 2, 2, 2, 2, 384, 128), bf), D((2,)),
                        V((512, 1536), f32), V((8, 3584), f32), V((32, 8, 256), f32), V((31, 8, 256), f32), D((31,)), D((31,))]
        + Reduce.scratch(n, R, skew),
        compiler_params=pltpu.CompilerParams(collective_id=collective_id, has_side_effects=True, vmem_limit_bytes=63 << 20), name="end",
    )(low_t.reshape(4, 2, 192, 512), dcp, dz, ol, win, wout, tok, cot, par, cg, rows, hg)


def dt_part(raw, hp, step_o, ds_o, dst_o):
    pre = raw + hp[2:3]
    step = jnp.maximum(pre, 0.0) + jnp.log1p(jnp.exp(-jnp.abs(pre)))
    rate = step * -jnp.exp(hp[0:1])
    step_o[...] = step
    r = lax.broadcasted_iota(jnp.int32, (256, 256), 0)
    c = lax.broadcasted_iota(jnp.int32, (256, 256), 1)
    low = (c <= r).astype(bf)
    for g in range(2):
        ds_o[256 * g:256 * g + 256] = mul_exact(low, rate[256 * g:256 * g + 256])
    turned = ds_o[...].T
    for p in range(TILES):
        dst_o[p, 0:4] = turned[4 * p:4 * p + 4]


def bc_part(block, taps, b_o, c_o, pad, s_s, bt_s):
    fill_pad(pad, block, block[512:528])
    for g, co in enumerate(conv(pad, taps)):
        act = co * sig(co)
        b, c = act[:, :128], act[:, 128:]
        b_o[256 * g:256 * g + 256] = b
        c_o[256 * g:256 * g + 256] = c
        bt_s[g] = b.T
        s_s[g, 0] = mul(c[:128], b[:128], NT)
        s_s[g, 1] = mul(c[128:], b[128:], NT)
        s_s[g, 2] = mul(c[128:], b[:128], NT)


def sf1_tile(j, block, taps, step, ds, dst, x_s, yi_s, part, pad, s_s, bt_s):
    fill_pad(pad, block, block[512:528])
    rds = rolled(ds[...], j)
    dsc = spread(rds)
    stc = spread(rolled(step[...], j))
    ok = causal(False)
    for g, co in enumerate(conv(pad, taps)):
        b0 = 256 * g
        x = co * sig(co)
        x_s[j, b0:b0 + 256] = x
        xs = x * stc[b0:b0 + 256]
        xp = halves(xs)
        d = dsc[b0:b0 + 256]
        ys = []
        for q in range(2):
            b = b0 + 128 * q
            y = []
            for m in range(2):
                w = []
                for h in (2 * m, 2 * m + 1):
                    gap = rds[b:b + 128, h:h + 1] - dst[j, h:h + 1, b:b + 128]
                    w.append(s_s[g, q] * jnp.exp(jnp.where(ok, gap, -1e30)))
                y.append(mul(jnp.concatenate(w, 1), heads_apart(part_of(xp, slice(128 * q, 128 * q + 128), slice(128 * m, 128 * m + 128)))))
            ys.append(jnp.concatenate(y, 1))
        mid = d[127:128]
        ys[1] = ys[1] + jnp.exp(d[128:] - mid) * mul(s_s[g, 2], jnp.exp(mid - d[:128]) * xs[:128])
        yi_s[j, b0:b0 + 128] = ys[0]
        yi_s[j, b0 + 128:b0 + 256] = ys[1]
        part[j, g] = mul(bt_s[g], jnp.exp(d[255:256] - d) * xs)


def sf2_tile(j, z, gain, ds, c_r, hp, x_s, yi_s, got, dn, a1, a2):
    dsc = spread(rolled(ds[...], j))
    skip = spread(rolled(hp[...], j))[1:2]
    for g in range(2):
        r = slice(256 * g, 256 * g + 256)
        mixed = yi_s[j, r] + jnp.exp(dsc[r]) * mul(c_r[r], got[j, g]) + skip * x_s[j, r]
        yi_s[j, r] = mixed
        gated = mixed * (z[r] * sig(z[r]))
        a1[r] += gated * gated
        a2[r] += gain * jnp.concatenate([dn[2 * j, r], dn[2 * j + 1, r]], 1) * gated


def front_call(in_proj, out_proj, conv_params, norm_gain, gate_gain, head_params, tokens, cotangent, collective_id, skew=2):
    NI, NO = 26, 6
    AT = [6400, 6144] + [3072 + 256 * p for p in range(12)] + [256 * p for p in range(12)]
    T, DM = tokens.shape
    TE = T + 16
    FIRST = NI - TILES
    Z0 = FIRST + NO

    def kernel(in_ref, out_ref, conv_ref, norm_ref, gate_ref, head_ref, tok_ref, cot_ref,
               proj_hbm, win, wout, x_hbm, mixed_hbm, low_hbm, dn_hbm, hp, par_ref, ent_o, step_o, ds_o, dst_o, b_o, c_o, rq_o,
               src_in, src_out, small_ref, edge_ref, low_t, sm, low_e, edge_in, pbuf, wbuf, obuf, x_s, yi_s, dn_ref, a1, a2, pad, s_s, bt_s, got, part, out, out_sem, in_sem, *sems):
        gs, os_, zs, (sm_out, sm_in, ed_out, ed_in, pb_sem, wl_sem, ol_sem, x_sem, mx_sem, dn_sem, low_sem) = sems[:9], sems[9:18], sems[18:27], sems[27:]
        me = Place()
        bar = pltpu.get_barrier_semaphore()
        def sg(k, _):
            pl.semaphore_signal(bar, inc=1, device_id=me.any_peer(k), device_id_type=MESH)
            return 0
        lax.fori_loop(1, 32, sg, 0)
        pl.semaphore_wait(bar, 31)
        ga = Gather(me, FIRST, src_in, win, gs, skew)
        gb = Gather(me, NO, src_out, wout, os_, skew)
        gz = Gather(me, NI - FIRST, src_in, win, zs, skew, FIRST)
        line = Chain(me, 1, got, part, out, out_sem, in_sem, keeper(ds_o))

        def take(p):
            if p == 0:
                src_in[0] = jnp.zeros((2, 48, 128), bf)
                src_in[0, 0, :, 0:48] = in_ref[:, 6400:6448].astype(bf)
            else:
                for h in range(2):
                    src_in[p, h] = in_ref[:, AT[p] + 128 * h:AT[p] + 128 * h + 128].astype(bf)
        small_ref[...] = jnp.zeros_like(small_ref)
        small_ref[0:5, 0:104] = conv_ref[...]
        small_ref[5:6, 0:48] = norm_ref[...]
        small_ref[6:7, 0:96] = gate_ref[...]
        row = lax.broadcasted_iota(jnp.int32, (8, 256), 0)
        first, second, third = (pltpu.roll(small_ref[...], lax.rem(me.line * w, 128), 1) for w in (104, 48, 96))
        small_ref[...] = jnp.where(row < 5, first, jnp.where(row == 5, second, third))
        row = lax.broadcasted_iota(jnp.int32, (16, DM), 0)
        ends = [tok_ref[256 * g + 240:256 * g + 256].astype(f32) for g in range(2)]
        edge_ref[...] = jnp.where(row < 8, pltpu.roll(ends[0], 3, 0), pltpu.roll(ends[1], 11, 0)).astype(bf)
        hp[...] = jnp.zeros_like(hp)
        hp[0:3, 0:48] = head_ref[...]
        take(0)
        take(1)

        def small_copy(k):
            return send(small_ref, sm.at[me.line], sm_out.at[k - 1], sm_in.at[k - 1], me.any_peer(k))
        def edge_copy():
            return send(edge_ref, edge_in, ed_out, ed_in, {"seq": lax.rem(me.z + 1, 4)})
        lax.fori_loop(1, 32, lambda k, _: (small_copy(k).start(), 0)[1], 0)
        edge_copy().start()
        sm[me.line] = small_ref[...]
        ga.step(0)
        ga.step(1)
        for p in range(2, NI): take(p)
        for p in range(NO):
            for h in range(2):
                src_out[p, h] = out_ref[:, 256 * p + 128 * h:256 * p + 128 * h + 128].astype(bf)
        line.start()
        a1[...] = jnp.zeros_like(a1)
        a2[...] = jnp.zeros_like(a2)
        par_ref[...] = jnp.zeros_like(par_ref)
        lax.fori_loop(1, 32, lambda k, _: (small_copy(k).wait(), 0)[1], 0)
        edge_copy().wait()
        for o in range(32):
            for base, width, stop in ((0, 104, 3328), (3328, 48, 4864), (4864, 96, 7936)):
                at = base + (o * width // 128) * 128
                wd = min(256, stop - at)
                par_ref[:, at:at + wd] += sm[o][:, :wd]
        gain = par_ref[5:6, 3328:4864]
        keep = (me.z > 0).astype(f32)

        def norm(v):
            v = v.astype(f32)
            return (v * lax.rsqrt(jnp.mean(v * v, axis=-1, keepdims=True) + 1e-5) * gain).astype(bf)
        def nloop(t, _):
            r = pl.ds(pl.multiple_of(t * 64, 64), 64)
            low_e[r] = norm(tok_ref[r])
            return 0
        lax.fori_loop(0, T // 64, nloop, 0)
        low_e[T:] = norm(edge_in[...].astype(f32) * keep)
        low_copy = pltpu.make_async_copy(low_t, low_hbm, low_sem)
        dn_copy = pltpu.make_async_copy(dn_ref, dn_hbm, dn_sem)

        def two(i): return lax.rem(i, 2)
        def pcopy(i): return pltpu.make_async_copy(pbuf.at[two(i)], proj_hbm.at[i], pb_sem.at[two(i)])
        def wload(i): return pltpu.make_async_copy(win.at[i], wbuf.at[two(i)], wl_sem.at[two(i)])
        def oload(i): return pltpu.make_async_copy(wout.at[i], obuf.at[two(i)], ol_sem.at[two(i)])
        def xcopy(j): return pltpu.make_async_copy(x_s.at[j], x_hbm.at[j], x_sem.at[j])
        def mcopy(j): return pltpu.make_async_copy(yi_s.at[j], mixed_hbm.at[j], mx_sem.at[j])
        def cols(base, j): return pl.ds(pl.multiple_of(base + j * 256, 128), 256)

        LAG = 4 * skew
        def chunk(i):
            s = two(i)
            wload(i).wait()
            @pl.when(i >= 2)
            def _(): pcopy(i - 2).wait()
            w = jnp.concatenate([wbuf[s, h].reshape(DM, 128) for h in range(2)], axis=1)
            pbuf[s] = jnp.dot(low_e[...], w, preferred_element_type=f32)
            pcopy(i).start()
            return pbuf.at[s]

        def loop(it, _):
            @pl.when(it >= 2)
            def _(): ga.step(it)
            gb.step(it - FIRST)
            gz.step(it - Z0)
            @pl.when((it >= 2) & (it < 6))
            def _():
                rows = pl.ds(pl.multiple_of((it - 2) * 128, 128), 128)
                low_t[:, rows] = low_e[rows].astype(f32).T.astype(bf)
            @pl.when(it == 6)
            def _(): low_copy.start()
            a = it - LAG
            @pl.when((a >= 0) & (a < FIRST))
            def _():
                ga.arrived(a)
                wload(a).start()
            @pl.when((a >= FIRST) & (a < Z0))
            def _():
                gb.arrived(a - FIRST)
                oload(a - FIRST).start()
            @pl.when((a >= Z0) & (a < Z0 + TILES))
            def _():
                gz.arrived(a - Z0)
                wload(a - NO).start()
            i = a - 1
            @pl.when((i >= 0) & (i < FIRST))
            def _():
                block = chunk(i)

                @pl.when(i == 0)
                def _(): dt_part(block[0:512, 0:128], hp, step_o, ds_o, dst_o)
                @pl.when(i == 1)
                def _(): bc_part(block, par_ref[:, 3072:3328], b_o, c_o, pad, s_s, bt_s)
                @pl.when(i >= 2)
                def _():
                    j = i - 2
                    sf1_tile(j, block, par_ref[:, cols(0, j)], step_o, ds_o, dst_o, x_s, yi_s, part, pad, s_s, bt_s)
                    xcopy(j).start()
            line.every_other(i - 2)
            @pl.when((i >= FIRST) & (i < Z0))
            def _():
                i2 = i - FIRST
                s = two(i2)
                oload(i2).wait()
                a_ = cot_ref[:, cols(0, i2)]
                def rows(q, _):
                    y = q // 4
                    x = lax.rem(q // 2, 2)
                    c = lax.rem(q, 2)
                    w = jnp.concatenate([obuf[s, h, y, x, c] for h in range(2)], axis=1)
                    r = lax.dot_general(a_, w, NT, preferred_element_type=f32)
                    for t in range(3):
                        rt = r[:, 128 * t:128 * t + 128]
                        @pl.when(i2 == 0)
                        def _(): dn_ref[3 * q + t] = rt
                        @pl.when(i2 > 0)
                        def _(): dn_ref[3 * q + t] += rt
                    return 0
                lax.fori_loop(0, 8, rows, 0)
                @pl.when(i2 == NO - 1)
                def _(): dn_copy.start()
            @pl.when(i >= Z0)
            def _():
                j = i - Z0
                block = chunk(i - NO)
                sf2_tile(j, block, par_ref[6:7, cols(4864, j)], ds_o, c_o, hp, x_s, yi_s, got, dn_ref, a1, a2)
                mcopy(j).start()
            return 0
        lax.fori_loop(0, NI + NO + LAG + 1, loop, 0)

        q = jnp.sum(a2[...], axis=1, keepdims=True) * (1.0 / 3072)
        r = lax.rsqrt(jnp.sum(a1[...], axis=1, keepdims=True) * (1.0 / 3072) + 1e-5)
        rq_o[0] = jnp.broadcast_to(r, (512, 128))
        rq_o[1] = jnp.broadcast_to(r * r * r * q, (512, 128))
        ent_o[...] = got[...]
        pcopy(NI - 2).wait()
        pcopy(NI - 1).wait()
        lax.fori_loop(0, TILES, lambda j, _: (mcopy(j).wait(), 0)[1], 0)
        lax.fori_loop(0, TILES, lambda j, _: (xcopy(j).wait(), 0)[1], 0)
        dn_copy.wait()
        low_copy.wait()
        line.finish()
        ga.finish()
        gb.finish()
        gz.finish()

    D = pltpu.SemaphoreType.DMA
    vm, hb = pl.BlockSpec(memory_space=pltpu.VMEM), pl.BlockSpec(memory_space=pl.ANY)
    wi, wo = (NI, 2, 2, 2, 2, 192, 128), (NO, 2, 2, 2, 2, 384, 128)
    tile = S((TILES, T, 256), f32)
    col = S((T, 128), f32)
    return pl.pallas_call(
        kernel,
        out_shape=(S((NI, TE, 256), f32), S(wi, bf), S(wo, bf), tile, tile, S((DM, T), bf), S((24, T, 128), f32), S((8, 128), f32), S((8, 7936), f32),
                   S((TILES, 2, 128, 256), bf), col, col, S((TILES, 8, T), f32), col, col, S((2, T, 128), f32)),
        in_specs=[vm] * 8,
        out_specs=(hb,) * 7 + (vm,) * 9,
        scratch_shapes=[V((NI, 2, 48, 128), bf), V((NO, 2, 96, 128), bf), V((8, 256), f32), V((16, DM), bf), V((DM, T), bf), V((32, 8, 256), f32), V((TE, DM), bf), V((16, DM), bf), V((2, TE, 256), f32), V((2,) + wi[1:], bf), V((2,) + wo[1:], bf),
                        V((TILES, T, 256), f32), V((TILES, T, 256), f32), V((24, T, 128), f32), V((T, 256), f32), V((T, 256), f32), V((2, 264, 256), f32), V((2, 3, 128, 128), f32), V((2, 128, 256), f32)]
        + Chain.scratch() + Gather.sems(FIRST, skew) + Gather.sems(NO, skew) + Gather.sems(TILES, skew)
        + [D((31,)), D((31,)), D, D, D((2,)), D((2,)), D((2,)), D((TILES,)), D((TILES,)), D, D],
        compiler_params=pltpu.CompilerParams(collective_id=collective_id, has_side_effects=True, vmem_limit_bytes=63 << 20),
        name="front",
    )(in_proj, out_proj, conv_params, norm_gain, gate_gain, head_params, tokens, cotangent)


def fast(adamw, tokens, cotangent, in_proj, in_mom, in_var, out_proj, out_mom, out_var, conv_params, conv_mom, conv_var,
         norm_gain, norm_mom, norm_var, gate_gain, gate_mom, gate_var, head_params, head_mom, head_var):
    line = lax.axis_index("dp") * 4 + lax.axis_index("seq")
    tok, cot = tokens.reshape(512, 1536), cotangent.reshape(512, 1536)
    proj, win, wout, x, mixed, low_t, dn, hp, par, ent, step, ds, dst, b, c, rq = front_call(
        in_proj, out_proj, conv_params, norm_gain[None], gate_gain[None], head_params, tok, cot, 1
    )
    dz, ol, dcp, cg, hg, rows, z_sum, out_grad = back_call(mixed, proj, dn, x, par, ent, ds, step, dst, b, c, hp, rq, low_t, cot, 5)
    last, block, tokens_grad, small_sum = end_call(low_t, dcp, dz, ol, win, wout, tok, cot, par, cg, rows, hg, 3)
    in_grad = jnp.concatenate([z_sum, last[:, :3376]], axis=1)
    tokens_grad = tokens_grad.reshape(2, 256, 1536)
    mine = lambda row, n, w: lax.dynamic_slice(small_sum, (row, lax.rem(line * w, 128)), (n, w))
    conv_grad, norm_grad, gate_grad = mine(0, 5, 104), mine(5, 1, 48)[0], mine(6, 1, 96)[0]
    head_grad = jnp.stack([small_sum[7, 0:48], small_sum[7, 128:176], small_sum[7, 64:112]])
    res = [(in_proj, in_mom, in_var, in_grad, 0.1), (out_proj, out_mom, out_var, out_grad, 0.1), (conv_params, conv_mom, conv_var, conv_grad, 0.1),
           (norm_gain, norm_mom, norm_var, norm_grad, 0.0), (gate_gain, gate_mom, gate_var, gate_grad, 0.0), (head_params, head_mom, head_var, head_grad, 0.0)]
    new = [v for a in res for v in adamw(*a)]
    return (block.reshape(2, 256, 1536), tokens_grad, in_grad, out_grad, conv_grad, norm_grad, gate_grad, head_grad, *new)


def solution(mesh):
    in_specs = (
        P("dp", "seq", None),
        P("dp", "seq", None),
        P(("dp", "seq"), None),
        P(("dp", "seq"), None),
        P(("dp", "seq"), None),
        P(("dp", "seq"), None),
        P(("dp", "seq"), None),
        P(("dp", "seq"), None),
        P(None, ("dp", "seq")),
        P(None, ("dp", "seq")),
        P(None, ("dp", "seq")),
        P(("dp", "seq")),
        P(("dp", "seq")),
        P(("dp", "seq")),
        P(("dp", "seq")),
        P(("dp", "seq")),
        P(("dp", "seq")),
        P(),
        P(),
        P(),
    )
    out_specs = (
        P("dp", "seq", None),
        P("dp", "seq", None),
        P(("dp", "seq"), None),
        P(("dp", "seq"), None),
        P(None, ("dp", "seq")),
        P(("dp", "seq")),
        P(("dp", "seq")),
        P(),
        P(("dp", "seq"), None),
        P(("dp", "seq"), None),
        P(("dp", "seq"), None),
        P(("dp", "seq"), None),
        P(("dp", "seq"), None),
        P(("dp", "seq"), None),
        P(None, ("dp", "seq")),
        P(None, ("dp", "seq")),
        P(None, ("dp", "seq")),
        P(("dp", "seq")),
        P(("dp", "seq")),
        P(("dp", "seq")),
        P(("dp", "seq")),
        P(("dp", "seq")),
        P(("dp", "seq")),
        P(),
        P(),
        P(),
    )
    own = tuple(mesh.shape[a] for a in ("dp", "seq")) == (8, 4)
    step = functools.partial(fast, adamw) if own else body
    return jax.shard_map(step, mesh=mesh, in_specs=in_specs, out_specs=out_specs, check_vma=False)
```
